32 devices in a mesh: slab: 8 (over z, core), cross: 4 (over y, x).
Axes of the slice: x: 2, y: 2, z: 4, core: 2. Of those that a mesh axis runs over, the one named last changes fastest.
Arguments:
- forcing: float32 [2, 32, 256, 512], P(None, 'slab', 'cross'), may hold values from -6 to 6
- viscosity: float32 [32, 256, 512], P('slab', 'cross'), may hold values from 0.1 to 10
- owner_slot: int32 [512], replicated, may hold values from 0 to 511, each once
Outputs:
- velocity: float32 [2, 32, 256, 512], P(None, 'slab', 'cross')
- pressure: float32 [32, 512], P('slab', 'cross')
The draws below stay inside these ranges and needn't reach their ends.
All inputs are finite; a program needn't handle non-finite values.
Results may differ from the reference program's by a relative error of at most 0.00013.
Values sent between devices are 32-bit elements; how exact they have to be, the bound alone decides.
A program may use at most 64 MiB of HBM per device.

```python
import math
import jax
import jax.numpy as jnp

NZ = 512
OUTER = 2
DEGREE = 3
NX = 32
NY = 256


def draw_forcing(key, part):
    first = jax.random.fold_in(key, 0)
    ramp = 1.0 + 2.0 * jnp.arange(NX, dtype=jnp.float32) / max(NX - 1, 1)
    base = jnp.clip(jax.random.normal(first, (2, NX, NY, NZ), jnp.float32), -2.0, 2.0)
    return base * ramp[None, :, None, None]


def block_scale(key, extent, cuts, low, largest):
    level, own = 1.0, jax.random.fold_in(key, 6)
    for position, parts in cuts:
        heights = jnp.exp(jax.random.uniform(jax.random.fold_in(own, position), (parts,), jnp.float32, low / len(cuts), largest / len(cuts)))
        level = level * jnp.repeat(heights, extent[position] // parts).reshape([-1 if axis == position else 1 for axis in range(len(extent))])
    return level


def setup_inputs(seed: int = 0) -> dict:
    keys = jax.random.split(jax.random.key(seed), 4)
    return {
        "forcing": draw_forcing(jax.random.fold_in(keys[3], 71), 0),
        "viscosity": jnp.clip(jnp.exp(math.log(10.0) - 4.6051702 * jax.random.uniform(keys[1], (NX, NY, NZ), jnp.float32) ** block_scale(keys[1], (NX, NY, NZ), ((0, 8), (1, 4)), -0.2, 0.2)), 0.1, 10.0),
        "owner_slot": jax.random.permutation(keys[2], NZ).astype(jnp.int32),
    }


cheb_theta = 1.025
cheb_delta = 0.975


def face_parts(viscosity):
    rim = jnp.pad(viscosity, 1)
    centre = rim[1:-1, 1:-1, 1:-1]
    neighbours = [rim[2:, 1:-1, 1:-1], rim[:-2, 1:-1, 1:-1], rim[1:-1, 2:, 1:-1], rim[1:-1, :-2, 1:-1], rim[1:-1, 1:-1, 2:], rim[1:-1, 1:-1, :-2]]
    faces = [0.5 * (centre + nb) for nb in neighbours]
    diag = faces[0] + faces[1] + faces[2] + faces[3] + faces[4] + faces[5]
    return faces, diag


def apply_op(field, faces):
    padded = jnp.pad(field, ((0, 0), (1, 1), (1, 1), (1, 1)))
    neighbours = [padded[:, 2:, 1:-1, 1:-1], padded[:, :-2, 1:-1, 1:-1], padded[:, 1:-1, 2:, 1:-1], padded[:, 1:-1, :-2, 1:-1], padded[:, 1:-1, 1:-1, 2:], padded[:, 1:-1, 1:-1, :-2]]
    result = jnp.zeros_like(field)
    for face, nb in zip(faces, neighbours):
        result = result + face[None] * (field - nb)
    return result


def velocity_solve(rhs, faces, diag):
    sigma = cheb_theta / cheb_delta
    solved = rhs / (cheb_theta * diag[None])
    change = solved
    rho_prev = 1.0 / sigma
    for step in range(DEGREE - 1):
        resid = rhs - apply_op(solved, faces)
        rho = 1.0 / (2.0 * sigma - rho_prev)
        change = rho * rho_prev * change + (2.0 * rho / cheb_delta) * resid / diag[None]
        solved = solved + change
        rho_prev = rho
    return solved


def diverge(field, owner_slot):
    col_x = jnp.sum(field[0], axis=1)
    col_z = jnp.sum(field[1], axis=1)
    below = jnp.pad(col_x[:-1], ((1, 0), (0, 0)))
    behind = jnp.pad(col_z[:, :-1], ((0, 0), (1, 0)))
    local = col_x - below + col_z - behind
    return jnp.zeros_like(local).at[:, owner_slot].set(local)


def gradient(press, owner_slot, ny):
    column = press[:, owner_slot]
    grad_x = column - jnp.pad(column[1:], ((0, 1), (0, 0)))
    grad_z = column - jnp.pad(column[:, 1:], ((0, 0), (0, 1)))
    both = jnp.stack([grad_x, grad_z])[:, :, None, :]
    return jnp.broadcast_to(both, (2, column.shape[0], ny, column.shape[1]))


def reference(forcing, viscosity, owner_slot):
    faces, diag = face_parts(viscosity)
    ny = viscosity.shape[1]
    target = diverge(velocity_solve(forcing, faces, diag), owner_slot)
    pressure = jnp.zeros_like(target)
    resid = target
    dirn = target
    rr = jnp.sum(resid * resid)
    for step in range(OUTER):
        image = diverge(velocity_solve(gradient(dirn, owner_slot, ny), faces, diag), owner_slot)
        alpha = rr / jnp.sum(dirn * image)
        pressure = pressure + alpha * dirn
        if step + 1 < OUTER:
            resid = resid - alpha * image
            fresh = jnp.sum(resid * resid)
            dirn = resid + (fresh / rr) * dirn
            rr = fresh
    velocity = velocity_solve(forcing - gradient(pressure, owner_slot, ny), faces, diag)
    return velocity, pressure
```

```python
import functools

import jax
import jax.numpy as jnp
from jax import lax
from jax.experimental import pallas as pl
from jax.experimental.pallas import tpu as pltpu
from jax.sharding import PartitionSpec as P

MESH = pl.DeviceIdType.MESH

DEGREE = 3
LANES = 128
TILE = 8

cheb_theta = 1.025
cheb_delta = 0.975


def cheb_weights():
    sigma = cheb_theta / cheb_delta
    solved = [1.0 / cheb_theta] + [0.0] * (DEGREE - 1)
    change = list(solved)
    rho_prev = 1.0 / sigma
    for step in range(DEGREE - 1):
        resid = [(1.0 if k == 0 else solved[k - 1]) - solved[k] for k in range(DEGREE)]
        rho = 1.0 / (2.0 * sigma - rho_prev)
        change = [rho * rho_prev * c + 2.0 * rho / cheb_delta * r for c, r in zip(change, resid)]
        solved = [s + c for s, c in zip(solved, change)]
        rho_prev = rho
    return solved


NEAR = [(0, 0), (1, 0), (-1, 0), (0, 1), (0, -1)]
ALL = [(dx, dz) for dx in range(-2, 3) for dz in range(-2, 3) if abs(dx) + abs(dz) <= 2]


def chunks(cn, nz):
    n = min(cn, nz // LANES)
    return n, cn // n


def zshift(a, d):
    n = a.shape[-1]
    k = lax.broadcasted_iota(jnp.int32, a.shape, a.ndim - 1)
    keep = (k < n - d) if d > 0 else (k >= -d)
    return jnp.where(keep, pltpu.roll(a, (-d) % n, a.ndim - 1), 0.0)


def ring(a, d, axis):
    return a if d == 0 else pltpu.roll(a, (-d) % a.shape[axis], axis)


def rows(ref, lead, t, last):
    def tile(i):
        return ref[lead + (pl.ds(pl.multiple_of(i * TILE, TILE), TILE), slice(None))]

    cur = tile(t)
    row = lax.broadcasted_iota(jnp.int32, cur.shape, 0)
    up = pltpu.roll(jnp.where(row == 0, tile(jnp.minimum(t + 1, last)), cur), TILE - 1, 0)
    down = pltpu.roll(jnp.where(row == TILE - 1, tile(jnp.maximum(t - 1, 0)), cur), 1, 0)
    return cur, up, down


def stokes_body(
    sn, cn, visc, forc, owner, vel, press,
    V, F, ypk, fpk, YV, CV, YF, CF, DI, U, M, Y0, Z, BASE, FD,
    KF, CS, FRAME, KP, KR, EB, EBR, A1, A2, WIN, QS, KS, GSR, FULL,
    lsem, hs, hr, bs, br, ks, kr, as1, ar1, as2, ar2, osem, hop,
):
    slab, cross = lax.axis_index("slab"), lax.axis_index("cross")
    nx, ny, nz = visc.shape
    nt = ny // TILE + 2
    ng, per = chunks(cn, nz)
    mine = cross // per
    f32 = jnp.float32
    w0, w1, w2 = [2.0 * w for w in cheb_weights()]

    def dev(s, c):
        return {"slab": s, "cross": c}

    def there(ds):
        return (slab + ds >= 0) & (slab + ds < sn)

    def others(dc):
        return lax.rem(cross + dc, cn)

    left, right = slab > 0, slab < sn - 1
    up, down = cross > 0, cross < cn - 1
    side, wall = (left, right), (up, down)
    own = pl.ds(TILE, ny)

    load_v = pltpu.make_async_copy(visc, V.at[pl.ds(3, nx), own], lsem.at[0])
    load_f = pltpu.make_async_copy(forc, F.at[:, pl.ds(2, nx), own], lsem.at[1])
    load_v.start()
    load_f.start()
    barrier = pltpu.get_barrier_semaphore()
    for ds in (0, 1, -1):
        for dc in range(cn):
            if ds == 0 and dc == 0:
                continue
            if ds == 0:
                pl.semaphore_signal(barrier, inc=1, device_id=dev(slab, others(dc)), device_id_type=MESH)
            else:

                @pl.when(there(ds))
                def _():
                    pl.semaphore_signal(barrier, inc=1, device_id=dev(slab + ds, others(dc)), device_id_type=MESH)

    zero_v = jnp.zeros((nx + 6, TILE, nz), f32)
    V[:, 0:TILE, :] = zero_v
    V[:, TILE + ny : 2 * TILE + ny, :] = zero_v
    zero_f = jnp.zeros((2, nx + 4, TILE, nz), f32)
    F[:, :, 0:TILE, :] = zero_f
    F[:, :, TILE + ny : 2 * TILE + ny, :] = zero_f
    for s in range(2):

        @pl.when(jnp.logical_not(side[s]))
        def _():
            v0, f0 = (0, 0) if s == 0 else (nx + 3, nx + 2)
            V[v0 : v0 + 3, TILE : TILE + ny, :] = jnp.zeros((3, ny, nz), f32)
            F[:, f0 : f0 + 2, TILE : TILE + ny, :] = jnp.zeros((2, 2, ny, nz), f32)

    load_v.wait()
    ypk[0] = V[3 : 3 + nx, TILE : TILE + 4, :]
    ypk[1] = V[3 : 3 + nx, TILE + ny - 4 : TILE + ny, :]
    load_f.wait()
    fpk[0] = F[:, 2 : 2 + nx, TILE : TILE + 2, :]
    fpk[1] = F[:, 2 : 2 + nx, TILE + ny - 2 : TILE + ny, :]
    count = (cn - 1) + cn * (jnp.where(left, 1, 0) + jnp.where(right, 1, 0))
    pl.semaphore_wait(barrier, count)

    steps = max(0, (sn - 2).bit_length())

    def greet(k):
        for d in (-(2**k), 2**k):

            @pl.when(there(d))
            def _():
                pl.semaphore_signal(hop.at[k], inc=1, device_id=dev(slab + d, cross), device_id_type=MESH)

    def greeted(k):
        pl.semaphore_wait(hop.at[k], jnp.where(there(-(2**k)), 1, 0) + jnp.where(there(2**k), 1, 0))

    def send(src, dst, out, into, s, c):
        return pltpu.make_async_remote_copy(
            src_ref=src, dst_ref=dst, send_sem=hs.at[out], recv_sem=hr.at[into], device_id=dev(s, c),
            device_id_type=MESH,
        )

    def vx(s, k):
        src = visc.at[k if s == 0 else nx - 1 - k]
        dst = V.at[nx + 3 + k if s == 0 else 2 - k, own]
        return send(src, dst, s * 3 + k, (1 - s) * 3 + k, slab + (2 * s - 1), cross)

    def vy(w):
        return send(ypk.at[w], YV.at[1 - w], 6 + w, 7 - w, slab, cross + (2 * w - 1))

    def vc(w, s):
        src = ypk.at[w, pl.ds(0 if s == 0 else nx - 2, 2)]
        return send(src, CV.at[1 - w, 1 - s], 8 + 2 * w + s, 8 + 2 * (1 - w) + 1 - s, slab + (2 * s - 1), cross + (2 * w - 1))

    def fx(s, c):
        src = forc.at[c, pl.ds(0 if s == 0 else nx - 2, 2)]
        dst = F.at[c, pl.ds(nx + 2 if s == 0 else 0, 2), own]
        return send(src, dst, 12 + 2 * s + c, 12 + 2 * (1 - s) + c, slab + (2 * s - 1), cross)

    def fy(w):
        return send(fpk.at[w], YF.at[1 - w], 16 + w, 17 - w, slab, cross + (2 * w - 1))

    def fc(w, s):
        src = fpk.at[w, :, pl.ds(0 if s == 0 else nx - 1, 1)]
        return send(src, CF.at[1 - w, 1 - s], 18 + 2 * w + s, 18 + 2 * (1 - w) + 1 - s, slab + (2 * s - 1), cross + (2 * w - 1))

    def landed(ref, into):
        pltpu.make_async_copy(ref, ref, hr.at[into]).wait()

    def when_all(conds, run):
        cond = conds[0]
        for c in conds[1:]:
            cond = cond & c
        pl.when(cond)(run)

    viscous, forces = [], []
    for s in range(2):
        viscous.append(([side[s]], functools.partial(vx, s, 0)))
    for w in range(2):
        viscous.append(([wall[w]], functools.partial(vy, w)))
    for w in range(2):
        for s in range(2):
            viscous.append(([wall[w], side[s]], functools.partial(vc, w, s)))
    for k in (1, 2):
        for s in range(2):
            viscous.append(([side[s]], functools.partial(vx, s, k)))
    for w in range(2):
        forces.append(([wall[w]], functools.partial(fy, w)))
    for w in range(2):
        for s in range(2):
            forces.append(([wall[w], side[s]], functools.partial(fc, w, s)))
    for s in range(2):
        for c in range(2):
            forces.append(([side[s]], functools.partial(fx, s, c)))

    for conds, make in viscous + forces:
        when_all(conds, lambda: make().start())
    if steps > 0:
        greet(0)

    for s in range(2):
        for k in range(3):
            when_all([side[s]], lambda: landed(V.at[nx + 3 + k if s == 1 else 2 - k, own], s * 3 + k))
    for w in range(2):

        def put():
            landed(YV.at[w], 6 + w)
            r0 = 4 if w == 0 else TILE + ny
            V[3 : 3 + nx, r0 : r0 + 4, :] = YV[w]

        when_all([wall[w]], put)
        for s in range(2):

            def put():
                landed(CV.at[w, s], 8 + 2 * w + s)
                r0 = 4 if w == 0 else TILE + ny
                p0 = 1 if s == 0 else nx + 3
                V[p0 : p0 + 2, r0 : r0 + 4, :] = CV[w, s]

            when_all([wall[w], side[s]], put)

    def inside(plane, t):
        ok = ((plane >= 0) | left) & ((plane < nx) | right) & ((t > 0) | up) & ((t < nt - 1) | down)
        return jnp.where(ok, 1.0, 0.0)

    def diagonal(i, _):
        p, t = i // nt, i % nt
        c, yp, ym = rows(V, (p + 1,), t, nt - 1)
        at = pl.ds(pl.multiple_of(t * TILE, TILE), TILE)
        diag = V[p + 2, at, :] + V[p, at, :] + yp + ym + zshift(c, 1) + zshift(c, -1) + 6.0 * c
        DI[p, at, :] = inside(p - 2, t) * (1.0 / jnp.maximum(diag, 1e-30))
        return 0

    lax.fori_loop(0, (nx + 4) * nt, diagonal, 0)

    def near(i, _):
        p, t = i // nt, i % nt
        at = pl.ds(pl.multiple_of(t * TILE, TILE), TILE)
        v, vyp, vym = rows(V, (p + 2,), t, nt - 1)
        d, dyp, dym = rows(DI, (p + 1,), t, nt - 1)
        wd = w2 * d
        U[0, p, at, :] = wd * ((v + vyp) * dyp + (v + vym) * dym) + w1 * d
        U[1, p, at, :] = wd * ((v + V[p + 3, at, :]) * DI[p + 2, at, :])
        U[2, p, at, :] = wd * ((v + V[p + 1, at, :]) * DI[p, at, :])
        U[3, p, at, :] = wd * ((v + zshift(v, 1)) * zshift(d, 1))
        U[4, p, at, :] = wd * ((v + zshift(v, -1)) * zshift(d, -1))
        return 0

    lax.fori_loop(0, (nx + 2) * nt, near, 0)

    inner = nt - 2

    def coefficients(i, _):
        p, t = i // inner, i % inner + 1
        at = pl.ds(pl.multiple_of(t * TILE, TILE), TILE)
        to = pl.ds(pl.multiple_of(t * TILE - TILE, TILE), TILE)
        v, vyp, vym = rows(V, (p + 3,), t, nt - 1)
        d = DI[p + 2, at, :]
        yp, ym = d * (v + vyp), d * (v + vym)
        xp, xm = d * (v + V[p + 4, at, :]), d * (v + V[p + 2, at, :])
        zp, zm = d * (v + zshift(v, 1)), d * (v + zshift(v, -1))
        acc = {(0, 0): w0 * d}

        def add(o, a):
            acc[o] = acc[o] + a if o in acc else a

        for n, (dx, dz) in enumerate(NEAR):
            c, cu, cd = rows(U, (n, p + 1), t, nt - 1)
            add((dx, dz), yp * cu + ym * cd)
            add((dx + 1, dz), xp * U[n, p + 2, at, :])
            add((dx - 1, dz), xm * U[n, p, at, :])
            add((dx, dz + 1), zp * zshift(c, 1))
            add((dx, dz - 1), zm * zshift(c, -1))
        for n, o in enumerate(ALL):
            M[n, p, to, :] = acc[o]
        return 0

    lax.fori_loop(0, nx * inner, coefficients, 0)

    prow = lax.broadcasted_iota(jnp.int32, (nx, nz), 0)

    def sums(p, _):
        for n in range(len(ALL)):

            def part(t, acc):
                at = pl.ds(pl.multiple_of(t * TILE, TILE), TILE)
                af = pl.ds(pl.multiple_of(t * TILE + TILE, TILE), TILE)
                m = M[n, p, at, :]
                return acc[0] + m, acc[1] + m * F[0, p + 2, af, :], acc[2] + m * F[1, p + 2, af, :]

            blank = jnp.zeros((TILE, nz), f32)
            k, c0, c1 = lax.fori_loop(0, inner, part, (blank, blank, blank), unroll=True)
            here = prow == p
            for ref, a in ((KF.at[n], k), (CS.at[n, 0], c0), (CS.at[n, 1], c1)):
                ref[...] = jnp.where(here, jnp.sum(a, axis=0, keepdims=True), ref[...])
        return 0

    KF[...] = jnp.zeros_like(KF)
    CS[...] = jnp.zeros_like(CS)
    lax.fori_loop(0, nx, sums, 0)

    FRAME[...] = jnp.zeros_like(FRAME)
    for c in range(2):
        for dx in range(-2, 3):
            total = None
            for n, o in enumerate(ALL):
                if o[0] == dx:
                    a = CS[n, c]
                    a = a if o[1] == 0 else zshift(a, -o[1])
                    total = a if total is None else total + a
            FRAME[c, nx + dx : 2 * nx + dx, :] += total
    cx, cz = FRAME[0], FRAME[1]
    e = cx - pltpu.roll(cx, 1, 0) + cz - zshift(cz, -1)
    WIN[:, 0:LANES] = jnp.zeros((4 * nx, LANES), f32)
    WIN[:, LANES + nz :] = jnp.zeros((4 * nx, LANES), f32)
    WIN[:, LANES : LANES + nz] = e

    def wide(get, g):
        main, before, after = get(g + 1), get(g), get(g + 2)
        lane = lax.broadcasted_iota(jnp.int32, main.shape, 1)
        return main, jnp.where(lane < LANES // 2, after, before)

    for g in range(ng):
        main, halo = wide(lambda i: WIN[:, i * LANES : (i + 1) * LANES], g)
        for b in range(3):
            EB[g, b, :, 0:LANES] = main[b * nx : (b + 1) * nx]
            EB[g, b, :, LANES : 2 * LANES] = halo[b * nx : (b + 1) * nx]
        for n in range(len(ALL)):
            KP[g, n] = KF[n, :, g * LANES : (g + 1) * LANES]

    if steps > 0:
        greeted(0)
        if steps > 1:
            greet(1)

    def span(ds):
        return pl.ds(max(0, ds), 3 - abs(ds))

    def e_copy(ds, dc):
        return pltpu.make_async_remote_copy(
            src_ref=EB.at[others(dc) // per, span(ds)], dst_ref=EBR.at[2 - ds, cross, span(ds)],
            send_sem=bs.at[ds + 2], recv_sem=br.at[2 - ds], device_id=dev(slab + ds, others(dc)), device_id_type=MESH,
        )

    for ds in (0, 1, -1, 2, -2):

        def start():
            for dc in range(1 if ds == 0 else 0, cn):
                e_copy(ds, dc).start()

        when_all([there(ds)], start)
    for dc in range(1, cn):
        pltpu.make_async_remote_copy(
            src_ref=KP.at[others(dc) // per], dst_ref=KR.at[cross], send_sem=ks, recv_sem=kr,
            device_id=dev(slab, others(dc)), device_id_type=MESH,
        ).start()
    for b in range(3):
        EBR[2, cross, b] = EB[mine, b]
    KR[cross] = KP[mine]

    for s in range(2):
        for c in range(2):
            f0 = 0 if s == 0 else nx + 2
            when_all([side[s]], lambda: landed(F.at[c, pl.ds(f0, 2), own], 12 + 2 * s + c))
    for w in range(2):

        def put():
            landed(YF.at[w], 16 + w)
            r0 = TILE - 2 if w == 0 else TILE + ny
            F[:, 2 : 2 + nx, r0 : r0 + 2, :] = YF[w]

        when_all([wall[w]], put)
        for s in range(2):

            def put():
                landed(CF.at[w, s], 18 + 2 * w + s)
                r0 = TILE - 2 if w == 0 else TILE + ny
                p0 = 1 if s == 0 else nx + 2
                F[:, p0 : p0 + 1, r0 : r0 + 2, :] = CF[w, s]

            when_all([wall[w], side[s]], put)

    def scaled(i, _):
        p, t = i // nt, i % nt
        at = pl.ds(pl.multiple_of(t * TILE, TILE), TILE)
        d = DI[p, at, :]
        for c in range(2):
            Y0[c, p, at, :] = d * F[c, p, at, :]
        return 0

    def neighbours(field, c, p, t, fields_plane):
        at = pl.ds(pl.multiple_of(t * TILE, TILE), TILE)
        a, au, ad = rows(field, (c, fields_plane), t, nt - 1)
        return a, au, ad, field[c, fields_plane + 1, at, :], field[c, fields_plane - 1, at, :]

    def faces(p, t):
        at = pl.ds(pl.multiple_of(t * TILE, TILE), TILE)
        v, vyp, vym = rows(V, (p + 3,), t, nt - 1)
        d = DI[p + 2, at, :]
        return (
            d * (v + vyp), d * (v + vym), d * (v + V[p + 4, at, :]), d * (v + V[p + 2, at, :]),
            d * (v + zshift(v, 1)), d * (v + zshift(v, -1)),
        )

    def once(i, _):
        p, t = i // nt, i % nt
        at = pl.ds(pl.multiple_of(t * TILE, TILE), TILE)
        yp, ym, xp, xm, zp, zm = faces(p - 1, t)
        for c in range(2):
            a, au, ad, ax, bx = neighbours(Y0, c, p, t, p + 1)
            t1 = yp * au + ym * ad + xp * ax + xm * bx + zp * zshift(a, 1) + zm * zshift(a, -1)
            Z[c, p, at, :] = w1 * a + w2 * t1
        return 0

    def twice(i, _):
        p, t = i // inner, i % inner + 1
        at = pl.ds(pl.multiple_of(t * TILE, TILE), TILE)
        to = pl.ds(pl.multiple_of(t * TILE - TILE, TILE), TILE)
        yp, ym, xp, xm, zp, zm = faces(p, t)
        for c in range(2):
            a, au, ad, ax, bx = neighbours(Z, c, p, t, p + 1)
            t2 = yp * au + ym * ad + xp * ax + xm * bx + zp * zshift(a, 1) + zm * zshift(a, -1)
            BASE[c, p, to, :] = w0 * Y0[c, p + 2, at, :] + t2
        return 0

    lax.fori_loop(0, (nx + 4) * nt, scaled, 0)
    lax.fori_loop(0, (nx + 2) * nt, once, 0)
    lax.fori_loop(0, nx * inner, twice, 0)

    e_mine = cn - 1
    for ds in range(-2, 3):
        src = -ds

        def wait():
            n = cn - 1 if ds == 0 else cn
            ref = EBR.at[2 + src, pl.ds(0, n), span(ds)]
            pltpu.make_async_copy(ref, ref, br.at[2 + src]).wait()

        when_all([there(src)], wait)
    pltpu.make_async_copy(KR.at[pl.ds(0, e_mine)], KR.at[pl.ds(0, e_mine)], kr).wait()
    WINB = WIN.at[:, 0 : 2 * LANES]
    WINB[3 * nx :, :] = jnp.zeros((nx, 2 * LANES), f32)
    for t in range(-1, 2):
        WINB[(t + 1) * nx : (t + 2) * nx, :] = jnp.zeros((nx, 2 * LANES), f32)

        def gather():
            for b in range(-1, 2):
                src = t - b

                def take():
                    total = EBR[2 + src, 0, b + 1]
                    for c in range(1, cn):
                        total = total + EBR[2 + src, c, b + 1]
                    WINB[(t + 1) * nx : (t + 2) * nx, :] += total

                when_all([there(src)], take)

        when_all([there(t)], gather)
    for n in range(len(ALL)):
        total = KR[0, n]
        for c in range(1, cn):
            total = total + KR[c, n]
        KS[n] = total

    def columns(q):
        for c, grad in enumerate((q - ring(q, 1, 0), q - ring(q, 1, 1))):
            for dz in range(-2, 3):
                QS[dz + 2, c] = ring(grad, dz, 1)[:, 0:LANES]
        out = []
        for c in range(2):
            total = None
            for n, (dx, dz) in enumerate(ALL):
                a = KS[n] * QS[dz + 2, c, nx + dx : 2 * nx + dx, :]
                total = a if total is None else total + a
            out.append(total)
        return out

    q = WINB[...]
    c1 = columns(q)
    me = slab * ng + mine
    A1[me, 0] = q[nx : 2 * nx, 0:LANES]
    A1[me, 1] = c1[0]
    A1[me, 2] = c1[1]
    for k in range(1, steps):
        greeted(k)
        if k + 1 < steps:
            greet(k + 1)

    def share(buf, ssem, rsem):
        order = [0, 1, sn - 1] + list(range(2, sn - 1))
        for ds in list(dict.fromkeys(d % sn for d in order)):
            for dg in range(ng):
                if ds == 0 and dg == 0:
                    continue
                to = lax.rem(mine + dg, ng) * per + lax.rem(cross, per)
                pltpu.make_async_remote_copy(
                    src_ref=buf.at[me], dst_ref=buf.at[me], send_sem=ssem, recv_sem=rsem.at[slab],
                    device_id=dev(lax.rem(slab + ds, sn), to), device_id_type=MESH,
                ).start()

    def shared(buf, rsem, s, n):
        ref = buf.at[pl.ds(0, n)]
        pltpu.make_async_copy(ref, ref, rsem.at[s]).wait()

    share(A1, as1, ar1)

    if ng > 1:
        shared(A1, ar1, slab, ng - 1)
    for ds in (-1, 1):
        when_all([there(ds)], lambda: shared(A1, ar1, slab + ds, ng))
    FRAME[...] = jnp.zeros_like(FRAME)
    for t in range(-1, 2):

        def fill():
            for g in range(ng):
                for a in range(3):
                    FRAME[a, (t + 1) * nx : (t + 2) * nx, g * LANES : (g + 1) * LANES] = A1[(slab + t) * ng + g, a]

        when_all([there(t)], fill)
    gwin = FRAME[0]
    cx, cz = FRAME[1], FRAME[2]
    sg = cx - pltpu.roll(cx, 1, 0) + cz - zshift(cz, -1)
    trow = lax.broadcasted_iota(jnp.int32, sg.shape, 0)
    known = (trow < 3 * nx) & ((trow < 2 * nx) | right) & ((trow >= nx) | left)
    sg = jnp.where(known, sg, 0.0)
    WIN[:, 0:LANES] = jnp.zeros((4 * nx, LANES), f32)
    WIN[:, LANES + nz :] = jnp.zeros((4 * nx, LANES), f32)
    WIN[:, LANES : LANES + nz] = sg
    main, halo = wide(lambda i: WIN[:, pl.ds(pl.multiple_of(i * LANES, LANES), LANES)], mine)
    c2 = columns(jnp.concatenate([main, halo], 1))
    A2[me, 0] = c2[0]
    A2[me, 1] = c2[1]
    share(A2, as2, ar2)

    for ds in range(2, sn - 1):
        s = lax.rem(slab + ds, sn)
        shared(A1, ar1, s, ng)
    for ds in (1, -1):
        when_all([jnp.logical_not(there(ds))], lambda: shared(A1, ar1, lax.rem(slab + ds + sn, sn), ng))

    def whole(buf, a, into):
        for s in range(sn):
            for g in range(ng):
                FULL[into, s * nx : (s + 1) * nx, g * LANES : (g + 1) * LANES] = buf[s * ng + g, a]

    def below(a):
        row = lax.broadcasted_iota(jnp.int32, a.shape, 0)
        return jnp.where(row == 0, 0.0, pltpu.roll(a, 1, 0))

    for a in range(3):
        whole(A1, a, a)
    g = FULL[0]
    s1 = FULL[1] - below(FULL[1]) + FULL[2] - zshift(FULL[2], -1)
    rr = jnp.sum(g * g)
    alpha0 = rr / jnp.sum(g * s1)
    resid = g - alpha0 * s1
    fresh = jnp.sum(resid * resid)
    beta = fresh / rr
    dirn = resid + beta * g
    FULL[3] = s1
    FULL[4] = dirn

    dwin = gwin - alpha0 * sg + beta * gwin
    last = (slab == sn - 1) & (trow == 2 * nx - 1)
    kcol = lax.broadcasted_iota(jnp.int32, sg.shape, 1)
    for i, q in enumerate((alpha0 * gwin, dwin)):
        ahead = jnp.where(last, 0.0, ring(q, 1, 0))
        for c, grad in enumerate((q - ahead, q - zshift(q, 1))):
            for dz in range(-2, 3):
                a = grad if dz == 0 else zshift(grad, dz)
                for r in range(nx - 2, 2 * nx + 2):
                    GSR[i, dz + 2, c, r] = a[r : r + 1]

    def apply(i, _):
        p, t = i // inner, i % inner
        at = pl.ds(pl.multiple_of(t * TILE, TILE), TILE)
        base = [BASE[c, p, at, :] for c in range(2)]
        second = [jnp.zeros((TILE, nz), f32) for c in range(2)]
        for n, (dx, dz) in enumerate(ALL):
            m = M[n, p, at, :]
            for c in range(2):
                base[c] = base[c] - m * GSR[0, dz + 2, c, p + nx + dx]
                second[c] = second[c] + m * GSR[1, dz + 2, c, p + nx + dx]
        for c in range(2):
            BASE[c, p, at, :] = base[c]
            FD[c, p, at, :] = second[c]
        return 0

    lax.fori_loop(0, nx * inner, apply, 0)

    width = press.shape[1]
    slot = lax.broadcasted_iota(jnp.int32, (width, nz), 0) + cross * width
    onehot = (jnp.broadcast_to(owner[...], (width, nz)) == slot).astype(f32)

    def ordered(a):
        return lax.dot_general(
            a, onehot, (((1,), (1,)), ((), ())), precision=lax.Precision.HIGHEST, preferred_element_type=f32
        )

    p0 = ordered(alpha0 * gwin[nx : 2 * nx])
    p1 = ordered(dwin[nx : 2 * nx])

    if ng > 1:
        shared(A2, ar2, slab, ng - 1)
    for ds in range(1, sn):
        shared(A2, ar2, lax.rem(slab + ds, sn), ng)
    for a in range(2):
        whole(A2, a, a)
    s2 = FULL[0] - below(FULL[0]) + FULL[1] - zshift(FULL[1], -1)
    s1 = FULL[3]
    image = s1 - alpha0 * s2 + beta * s1
    alpha1 = fresh / jnp.sum(FULL[4] * image)
    press[...] = p0 + alpha1 * p1

    outs = []
    for p in range(nx):

        def finish(t, _):
            at = pl.ds(pl.multiple_of(t * TILE, TILE), TILE)
            for c in range(2):
                BASE[c, p, at, :] = BASE[c, p, at, :] - alpha1 * FD[c, p, at, :]
            return 0

        lax.fori_loop(0, inner, finish, 0)
        out = pltpu.make_async_copy(BASE.at[:, p], vel.at[:, p], osem.at[p])
        out.start()
        outs.append(out)
    for out in outs:
        out.wait()

    for conds, make in viscous + forces:
        when_all(conds, lambda: make().wait_send())
    for ds in range(-2, 3):

        def left_here():
            ref = EBR.at[2 - ds, pl.ds(0, cn - 1 if ds == 0 else cn), span(ds)]
            pltpu.make_async_copy(ref, ref, bs.at[ds + 2]).wait()

        when_all([there(ds)], left_here)
    pltpu.make_async_copy(KR.at[pl.ds(0, cn - 1)], KR.at[pl.ds(0, cn - 1)], ks).wait()
    for buf, sem in ((A1, as1), (A2, as2)):
        ref = buf.at[pl.ds(0, sn * ng - 1)]
        pltpu.make_async_copy(ref, ref, sem).wait()


def stokes(forcing, viscosity, owner, sn, cn):
    nx, ny, nz = viscosity.shape
    f32 = jnp.float32
    ng, _ = chunks(cn, nz)
    no = len(ALL)
    ye = ny + 2 * TILE
    vmem = pl.BlockSpec(memory_space=pltpu.VMEM)
    anywhere = pl.BlockSpec(memory_space=pl.ANY)
    dma = pltpu.SemaphoreType.DMA

    def buf(*shape):
        return pltpu.VMEM(shape, f32)

    return pl.pallas_call(
        functools.partial(stokes_body, sn, cn),
        out_shape=(
            jax.ShapeDtypeStruct(forcing.shape, f32),
            jax.ShapeDtypeStruct((nx, nz // cn), f32),
        ),
        in_specs=[anywhere, anywhere, vmem],
        out_specs=(anywhere, vmem),
        scratch_shapes=[
            buf(nx + 6, ye, nz),
            buf(2, nx + 4, ye, nz),
            buf(2, nx, 4, nz),
            buf(2, 2, nx, 2, nz),
            buf(2, nx, 4, nz),
            buf(2, 2, 2, 4, nz),
            buf(2, 2, nx, 2, nz),
            buf(2, 2, 2, 1, 2, nz),
            buf(nx + 4, ye, nz),
            buf(5, nx + 2, ye, nz),
            buf(no, nx, ny, nz),
            buf(2, nx + 4, ye, nz),
            buf(2, nx + 2, ye, nz),
            buf(2, nx, ny, nz),
            buf(2, nx, ny, nz),
            buf(no, nx, nz),
            buf(no, 2, nx, nz),
            buf(3, 4 * nx, nz),
            buf(ng, no, nx, LANES),
            buf(cn, no, nx, LANES),
            buf(ng, 3, nx, 2 * LANES),
            buf(5, cn, 3, nx, 2 * LANES),
            buf(sn * ng, 3, nx, LANES),
            buf(sn * ng, 2, nx, LANES),
            buf(4 * nx, nz + 2 * LANES),
            buf(5, 2, 4 * nx, LANES),
            buf(no, nx, LANES),
            buf(2, 5, 2, 4 * nx, 1, nz),
            buf(5, sn * nx, nz),
            dma((2,)),
            dma((22,)),
            dma((22,)),
            dma((5,)),
            dma((5,)),
            dma,
            dma,
            dma,
            dma((sn,)),
            dma,
            dma((sn,)),
            dma((nx,)),
            pltpu.SemaphoreType.REGULAR((max(1, (sn - 2).bit_length()),)),
        ],
        compiler_params=pltpu.CompilerParams(
            collective_id=0, has_side_effects=True, vmem_limit_bytes=56 * 2**20
        ),
        name="stokes",
    )(viscosity, forcing, owner)


def shards(forcing, viscosity, owner_slot):
    sn, cn = lax.axis_size("slab"), lax.axis_size("cross")
    return stokes(forcing, viscosity, owner_slot.reshape(1, -1), sn, cn)


def solution(mesh):
    in_specs = (P(None, "slab", "cross", None), P("slab", "cross", None), P())
    out_specs = (P(None, "slab", "cross", None), P("slab", "cross"))
    return jax.shard_map(shards, mesh=mesh, in_specs=in_specs, out_specs=out_specs, check_vma=False)
```

```python
import functools

import jax
import jax.numpy as jnp
from jax import lax
from jax.experimental import pallas as pl
from jax.experimental.pallas import tpu as pltpu
from jax.sharding import PartitionSpec as P

MESH = pl.DeviceIdType.MESH

DEGREE = 3
LANES = 128
TILE = 8

cheb_theta = 1.025
cheb_delta = 0.975


def cheb_weights():
    sigma = cheb_theta / cheb_delta
    solved = [1.0 / cheb_theta] + [0.0] * (DEGREE - 1)
    change = list(solved)
    rho_prev = 1.0 / sigma
    for step in range(DEGREE - 1):
        resid = [(1.0 if k == 0 else solved[k - 1]) - solved[k] for k in range(DEGREE)]
        rho = 1.0 / (2.0 * sigma - rho_prev)
        change = [rho * rho_prev * c + 2.0 * rho / cheb_delta * r for c, r in zip(change, resid)]
        solved = [s + c for s, c in zip(solved, change)]
        rho_prev = rho
    return solved


NEAR = [(0, 0), (1, 0), (-1, 0), (0, 1), (0, -1)]
ALL = [(dx, dz) for dx in range(-2, 3) for dz in range(-2, 3) if abs(dx) + abs(dz) <= 2]


def chunks(cn, nz):
    n = min(cn, nz // LANES)
    return n, cn // n


def zshift(a, d):
    n = a.shape[-1]
    k = lax.broadcasted_iota(jnp.int32, a.shape, a.ndim - 1)
    keep = (k < n - d) if d > 0 else (k >= -d)
    return jnp.where(keep, pltpu.roll(a, (-d) % n, a.ndim - 1), 0.0)


def ring(a, d, axis):
    return a if d == 0 else pltpu.roll(a, (-d) % a.shape[axis], axis)


def rows(ref, lead, t, last):
    def tile(i):
        return ref[lead + (pl.ds(pl.multiple_of(i * TILE, TILE), TILE), slice(None))]

    cur = tile(t)
    row = lax.broadcasted_iota(jnp.int32, cur.shape, 0)
    up = pltpu.roll(jnp.where(row == 0, tile(jnp.minimum(t + 1, last)), cur), TILE - 1, 0)
    down = pltpu.roll(jnp.where(row == TILE - 1, tile(jnp.maximum(t - 1, 0)), cur), 1, 0)
    return cur, up, down


def stokes_body(
    sn, cn, visc, forc, owner, vel, press,
    V, F, ypk, fpk, YV, CV, YF, CF, DI, U, M, Y0, Z, BASE, FD,
    KF, CS, FRAME, KP, KR, EB, EBR, A1, A2, WIN, QS, KS, GSR, FULL,
    lsem, hs, hr, bs, br, ks, kr, as1, ar1, as2, ar2, osem, hop,
):
    slab, cross = lax.axis_index("slab"), lax.axis_index("cross")
    nx, ny, nz = visc.shape
    nt = ny // TILE + 2
    ng, per = chunks(cn, nz)
    mine = cross // per
    f32 = jnp.float32
    w0, w1, w2 = [2.0 * w for w in cheb_weights()]

    def dev(s, c):
        return {"slab": s, "cross": c}

    def there(ds):
        return (slab + ds >= 0) & (slab + ds < sn)

    def others(dc):
        return lax.rem(cross + dc, cn)

    left, right = slab > 0, slab < sn - 1
    up, down = cross > 0, cross < cn - 1
    side, wall = (left, right), (up, down)
    own = pl.ds(TILE, ny)

    load_v = pltpu.make_async_copy(visc, V.at[pl.ds(3, nx), own], lsem.at[0])
    load_f = pltpu.make_async_copy(forc, F.at[:, pl.ds(2, nx), own], lsem.at[1])
    load_v.start()
    load_f.start()
    barrier = pltpu.get_barrier_semaphore()
    for ds in (0, 1, -1):
        for dc in range(cn):
            if ds == 0 and dc == 0:
                continue
            if ds == 0:
                pl.semaphore_signal(barrier, inc=1, device_id=dev(slab, others(dc)), device_id_type=MESH)
            else:

                @pl.when(there(ds))
                def _():
                    pl.semaphore_signal(barrier, inc=1, device_id=dev(slab + ds, others(dc)), device_id_type=MESH)

    zero_v = jnp.zeros((nx + 6, TILE, nz), f32)
    V[:, 0:TILE, :] = zero_v
    V[:, TILE + ny : 2 * TILE + ny, :] = zero_v
    zero_f = jnp.zeros((2, nx + 4, TILE, nz), f32)
    F[:, :, 0:TILE, :] = zero_f
    F[:, :, TILE + ny : 2 * TILE + ny, :] = zero_f
    for s in range(2):

        @pl.when(jnp.logical_not(side[s]))
        def _():
            v0, f0 = (0, 0) if s == 0 else (nx + 3, nx + 2)
            V[v0 : v0 + 3, TILE : TILE + ny, :] = jnp.zeros((3, ny, nz), f32)
            F[:, f0 : f0 + 2, TILE : TILE + ny, :] = jnp.zeros((2, 2, ny, nz), f32)

    load_v.wait()
    ypk[0] = V[3 : 3 + nx, TILE : TILE + 4, :]
    ypk[1] = V[3 : 3 + nx, TILE + ny - 4 : TILE + ny, :]
    load_f.wait()
    fpk[0] = F[:, 2 : 2 + nx, TILE : TILE + 2, :]
    fpk[1] = F[:, 2 : 2 + nx, TILE + ny - 2 : TILE + ny, :]
    count = (cn - 1) + cn * (jnp.where(left, 1, 0) + jnp.where(right, 1, 0))
    pl.semaphore_wait(barrier, count)

    steps = max(0, (sn - 2).bit_length())

    def greet(k):
        for d in (-(2**k), 2**k):

            @pl.when(there(d))
            def _():
                pl.semaphore_signal(hop.at[k], inc=1, device_id=dev(slab + d, cross), device_id_type=MESH)

    def greeted(k):
        pl.semaphore_wait(hop.at[k], jnp.where(there(-(2**k)), 1, 0) + jnp.where(there(2**k), 1, 0))

    def send(src, dst, out, into, s, c):
        return pltpu.make_async_remote_copy(
            src_ref=src, dst_ref=dst, send_sem=hs.at[out], recv_sem=hr.at[into], device_id=dev(s, c),
            device_id_type=MESH,
        )

    def vx(s, k):
        src = visc.at[k if s == 0 else nx - 1 - k]
        dst = V.at[nx + 3 + k if s == 0 else 2 - k, own]
        return send(src, dst, s * 3 + k, (1 - s) * 3 + k, slab + (2 * s - 1), cross)

    def vy(w):
        return send(ypk.at[w], YV.at[1 - w], 6 + w, 7 - w, slab, cross + (2 * w - 1))

    def vc(w, s):
        src = ypk.at[w, pl.ds(0 if s == 0 else nx - 2, 2)]
        return send(src, CV.at[1 - w, 1 - s], 8 + 2 * w + s, 8 + 2 * (1 - w) + 1 - s, slab + (2 * s - 1), cross + (2 * w - 1))

    def fx(s, c):
        src = forc.at[c, pl.ds(0 if s == 0 else nx - 2, 2)]
        dst = F.at[c, pl.ds(nx + 2 if s == 0 else 0, 2), own]
        return send(src, dst, 12 + 2 * s + c, 12 + 2 * (1 - s) + c, slab + (2 * s - 1), cross)

    def fy(w):
        return send(fpk.at[w], YF.at[1 - w], 16 + w, 17 - w, slab, cross + (2 * w - 1))

    def fc(w, s):
        src = fpk.at[w, :, pl.ds(0 if s == 0 else nx - 1, 1)]
        return send(src, CF.at[1 - w, 1 - s], 18 + 2 * w + s, 18 + 2 * (1 - w) + 1 - s, slab + (2 * s - 1), cross + (2 * w - 1))

    def landed(ref, into):
        pltpu.make_async_copy(ref, ref, hr.at[into]).wait()

    def when_all(conds, run):
        cond = conds[0]
        for c in conds[1:]:
            cond = cond & c
        pl.when(cond)(run)

    viscous, forces = [], []
    for s in range(2):
        viscous.append(([side[s]], functools.partial(vx, s, 0)))
    for w in range(2):
        viscous.append(([wall[w]], functools.partial(vy, w)))
    for w in range(2):
        for s in range(2):
            viscous.append(([wall[w], side[s]], functools.partial(vc, w, s)))
    for k in (1, 2):
        for s in range(2):
            viscous.append(([side[s]], functools.partial(vx, s, k)))
    for w in range(2):
        forces.append(([wall[w]], functools.partial(fy, w)))
    for w in range(2):
        for s in range(2):
            forces.append(([wall[w], side[s]], functools.partial(fc, w, s)))
    for s in range(2):
        for c in range(2):
            forces.append(([side[s]], functools.partial(fx, s, c)))

    for conds, make in viscous + forces:
        when_all(conds, lambda: make().start())
    if steps > 0:
        greet(0)

    inner = nt - 2

    def sweep(lo, n, body, k=2):
        while n % k:
            k -= 1

        def step(i, _):
            for j in range(k):
                body(lo + i * k + j)
            return 0

        lax.fori_loop(0, n // k, step, 0)

    def tile(t):
        return pl.ds(t * TILE if isinstance(t, int) else pl.multiple_of(t * TILE, TILE), TILE)

    def inside(plane, t):
        ok = ((t > 0) | up) & ((t < nt - 1) | down)
        if plane < 0:
            ok = ok & left
        if plane >= nx:
            ok = ok & right
        return jnp.where(ok, 1.0, 0.0)

    def diagonal(planes, t):
        for p in planes:
            c, yp, ym = rows(V, (p + 3,), t, nt - 1)
            diag = V[p + 4, tile(t), :] + V[p + 2, tile(t), :] + yp + ym + zshift(c, 1) + zshift(c, -1) + 6.0 * c
            DI[p + 2, tile(t), :] = inside(p, t) * (1.0 / jnp.maximum(diag, 1e-30))

    def near(planes, comps, t):
        for p in planes:
            at = tile(t)
            v, vyp, vym = rows(V, (p + 3,), t, nt - 1)
            d, dyp, dym = rows(DI, (p + 2,), t, nt - 1)
            wd = w2 * d
            if 0 in comps:
                U[0, p + 1, at, :] = wd * ((v + vyp) * dyp + (v + vym) * dym) + w1 * d
            if 1 in comps:
                U[1, p + 1, at, :] = wd * ((v + V[p + 4, at, :]) * DI[p + 3, at, :])
            if 2 in comps:
                U[2, p + 1, at, :] = wd * ((v + V[p + 2, at, :]) * DI[p + 1, at, :])
            if 3 in comps:
                U[3, p + 1, at, :] = wd * ((v + zshift(v, 1)) * zshift(d, 1))
                U[4, p + 1, at, :] = wd * ((v + zshift(v, -1)) * zshift(d, -1))

    def coefficients(planes, t):
        for p in planes:
            at, to = tile(t), tile(t - 1)
            v, vyp, vym = rows(V, (p + 3,), t, nt - 1)
            d = DI[p + 2, at, :]
            yp, ym = d * (v + vyp), d * (v + vym)
            xp, xm = d * (v + V[p + 4, at, :]), d * (v + V[p + 2, at, :])
            zp, zm = d * (v + zshift(v, 1)), d * (v + zshift(v, -1))
            acc = {(0, 0): w0 * d}

            def add(o, a):
                acc[o] = acc[o] + a if o in acc else a

            for n, (dx, dz) in enumerate(NEAR):
                c, cu, cd = rows(U, (n, p + 1), t, nt - 1)
                add((dx, dz), yp * cu + ym * cd)
                if dx < 1:
                    add((dx + 1, dz), xp * U[n, p + 2, at, :])
                if dx > -1:
                    add((dx - 1, dz), xm * U[n, p, at, :])
                add((dx, dz + 1), zp * zshift(c, 1))
                add((dx, dz - 1), zm * zshift(c, -1))
            for o in acc:
                M[ALL.index(o), p, to, :] = acc[o]

    def far(pairs, t):
        for p, d in pairs:
            at = tile(t)
            v0, v1, v2 = [V[p + 3 + d * k, at, :] for k in range(3)]
            d0, d1, d2 = [DI[p + 2 + d * k, at, :] for k in range(3)]
            M[ALL.index((2 * d, 0)), p, tile(t - 1), :] = w2 * (d0 * (v0 + v1)) * (d1 * (v1 + v2)) * d2

    prow = lax.broadcasted_iota(jnp.int32, (nx, nz), 0)
    KF[...] = jnp.zeros_like(KF)
    CS[...] = jnp.zeros_like(CS)

    def sums(p, offsets):
        for o in offsets:
            n = ALL.index(o)
            acc = None
            for t in range(inner):
                m = M[n, p, tile(t), :]
                new = (m, m * F[0, p + 2, tile(t + 1), :], m * F[1, p + 2, tile(t + 1), :])
                acc = new if acc is None else [a + b for a, b in zip(acc, new)]
            here = prow == p
            for ref, a in zip((KF.at[n], CS.at[n, 0], CS.at[n, 1]), acc):
                ref[...] = jnp.where(here, jnp.sum(a, axis=0, keepdims=True), ref[...])

    short = [o for o in ALL if abs(o[0]) < 2]
    mids, ends = list(range(1, nx - 1)), [0, nx - 1]

    def plane_sums(first, stride, n):
        def step(i, _):
            sums(first + i * stride, short)
            return 0

        lax.fori_loop(0, n, step, 0)

    sweep(2, inner - 2, lambda t: diagonal(mids, t))
    for s in range(2):
        when_all([side[s]], lambda: landed(V.at[nx + 3 if s == 1 else 2, own], s * 3))
    for w in range(2):

        def put():
            landed(YV.at[w], 6 + w)
            r0 = 4 if w == 0 else TILE + ny
            V[3 : 3 + nx, r0 : r0 + 4, :] = YV[w]

        when_all([wall[w]], put)
    for t in (0, 1, nt - 2, nt - 1):
        diagonal(mids, t)
    sweep(1, inner, lambda t: diagonal(ends, t))
    for w in range(2):
        for s in range(2):

            def put():
                landed(CV.at[w, s], 8 + 2 * w + s)
                r0 = 4 if w == 0 else TILE + ny
                p0 = 1 if s == 0 else nx + 3
                V[p0 : p0 + 2, r0 : r0 + 4, :] = CV[w, s]

            when_all([wall[w], side[s]], put)
    for t in (0, nt - 1):
        diagonal(ends, t)
    sweep(0, nt, lambda t: near(mids, (0, 1, 2, 3), t))
    sweep(0, nt, lambda t: (near([0], (0, 1, 3), t), near([nx - 1], (0, 2, 3), t)))
    sweep(1, inner, lambda t: coefficients(mids, t), 1)
    plane_sums(1, 1, nx - 2)
    for s in range(2):
        when_all([side[s]], lambda: landed(V.at[nx + 4 if s == 1 else 1, own], s * 3 + 1))
    sweep(0, nt, lambda t: diagonal([-1, nx], t))
    sweep(0, nt, lambda t: (near([-1], (0, 1, 3), t), near([nx], (0, 2, 3), t), near([0], (2,), t), near([nx - 1], (1,), t)))
    sweep(1, inner, lambda t: coefficients(ends, t), 1)
    plane_sums(0, nx - 1, 2)
    ready = [(p, d) for p in range(nx) for d in (1, -1) if 0 <= p + d < nx]
    sweep(1, inner, lambda t: far(ready, t), 1)
    for p, d in ready:
        sums(p, [(2 * d, 0)])
    for s in range(2):
        when_all([side[s]], lambda: landed(V.at[nx + 5 if s == 1 else 0, own], s * 3 + 2))
    sweep(1, inner, lambda t: diagonal([-2, nx + 1], t))
    sweep(1, inner, lambda t: far([(0, -1), (nx - 1, 1)], t))
    sums(0, [(-2, 0)])
    sums(nx - 1, [(2, 0)])

    FRAME[...] = jnp.zeros_like(FRAME)
    for c in range(2):
        for dx in range(-2, 3):
            total = None
            for n, o in enumerate(ALL):
                if o[0] == dx:
                    a = CS[n, c]
                    a = a if o[1] == 0 else zshift(a, -o[1])
                    total = a if total is None else total + a
            FRAME[c, nx + dx : 2 * nx + dx, :] += total
    cx, cz = FRAME[0], FRAME[1]
    e = cx - pltpu.roll(cx, 1, 0) + cz - zshift(cz, -1)
    WIN[:, 0:LANES] = jnp.zeros((4 * nx, LANES), f32)
    WIN[:, LANES + nz :] = jnp.zeros((4 * nx, LANES), f32)
    WIN[:, LANES : LANES + nz] = e

    def wide(get, g):
        main, before, after = get(g + 1), get(g), get(g + 2)
        lane = lax.broadcasted_iota(jnp.int32, main.shape, 1)
        return main, jnp.where(lane < LANES // 2, after, before)

    for g in range(ng):
        main, halo = wide(lambda i: WIN[:, i * LANES : (i + 1) * LANES], g)
        for b in range(3):
            EB[g, b, :, 0:LANES] = main[b * nx : (b + 1) * nx]
            EB[g, b, :, LANES : 2 * LANES] = halo[b * nx : (b + 1) * nx]
        for n in range(len(ALL)):
            KP[g, n] = KF[n, :, g * LANES : (g + 1) * LANES]

    if steps > 0:
        greeted(0)
        if steps > 1:
            greet(1)

    def span(ds):
        return pl.ds(max(0, ds), 3 - abs(ds))

    def e_copy(ds, dc):
        return pltpu.make_async_remote_copy(
            src_ref=EB.at[others(dc) // per, span(ds)], dst_ref=EBR.at[2 - ds, cross, span(ds)],
            send_sem=bs.at[ds + 2], recv_sem=br.at[2 - ds], device_id=dev(slab + ds, others(dc)), device_id_type=MESH,
        )

    for ds in (0, 1, -1, 2, -2):

        def start():
            for dc in range(1 if ds == 0 else 0, cn):
                e_copy(ds, dc).start()

        when_all([there(ds)], start)
    for dc in range(1, cn):
        pltpu.make_async_remote_copy(
            src_ref=KP.at[others(dc) // per], dst_ref=KR.at[cross], send_sem=ks, recv_sem=kr,
            device_id=dev(slab, others(dc)), device_id_type=MESH,
        ).start()
    for b in range(3):
        EBR[2, cross, b] = EB[mine, b]
    KR[cross] = KP[mine]

    for s in range(2):
        for c in range(2):
            f0 = 0 if s == 0 else nx + 2
            when_all([side[s]], lambda: landed(F.at[c, pl.ds(f0, 2), own], 12 + 2 * s + c))
    for w in range(2):

        def put():
            landed(YF.at[w], 16 + w)
            r0 = TILE - 2 if w == 0 else TILE + ny
            F[:, 2 : 2 + nx, r0 : r0 + 2, :] = YF[w]

        when_all([wall[w]], put)
        for s in range(2):

            def put():
                landed(CF.at[w, s], 18 + 2 * w + s)
                r0 = TILE - 2 if w == 0 else TILE + ny
                p0 = 1 if s == 0 else nx + 2
                F[:, p0 : p0 + 1, r0 : r0 + 2, :] = CF[w, s]

            when_all([wall[w], side[s]], put)

    def scaled(t):
        for p in range(nx + 4):
            d = DI[p, tile(t), :]
            for c in range(2):
                Y0[c, p, tile(t), :] = d * F[c, p, tile(t), :]

    def faces(p, t):
        at = tile(t)
        v, vyp, vym = rows(V, (p + 3,), t, nt - 1)
        d = DI[p + 2, at, :]
        return (
            d * (v + vyp), d * (v + vym), d * (v + V[p + 4, at, :]), d * (v + V[p + 2, at, :]),
            d * (v + zshift(v, 1)), d * (v + zshift(v, -1)),
        )

    def carried(field, c, p, t, face):
        yp, ym, xp, xm, zp, zm = face
        a, au, ad = rows(field, (c, p), t, nt - 1)
        near_by = yp * au + ym * ad + xp * field[c, p + 1, tile(t), :] + xm * field[c, p - 1, tile(t), :]
        return a, near_by + zp * zshift(a, 1) + zm * zshift(a, -1)

    def once(planes, t):
        for p in planes:
            face = faces(p, t)
            for c in range(2):
                a, t1 = carried(Y0, c, p + 2, t, face)
                Z[c, p + 1, tile(t), :] = w1 * a + w2 * t1

    def twice(planes, t):
        for p in planes:
            face = faces(p, t)
            for c in range(2):
                a, t2 = carried(Z, c, p + 1, t, face)
                BASE[c, p, tile(t - 1), :] = w0 * Y0[c, p + 2, tile(t), :] + t2

    sweep(0, nt, scaled)
    sweep(0, nt, lambda t: once(range(-1, nx + 1), t), 1)

    e_mine = cn - 1
    for ds in range(-2, 3):
        src = -ds

        def wait():
            n = cn - 1 if ds == 0 else cn
            ref = EBR.at[2 + src, pl.ds(0, n), span(ds)]
            pltpu.make_async_copy(ref, ref, br.at[2 + src]).wait()

        when_all([there(src)], wait)
    pltpu.make_async_copy(KR.at[pl.ds(0, e_mine)], KR.at[pl.ds(0, e_mine)], kr).wait()
    WINB = WIN.at[:, 0 : 2 * LANES]
    WINB[3 * nx :, :] = jnp.zeros((nx, 2 * LANES), f32)
    for t in range(-1, 2):
        WINB[(t + 1) * nx : (t + 2) * nx, :] = jnp.zeros((nx, 2 * LANES), f32)

        def gather():
            for b in range(-1, 2):
                src = t - b

                def take():
                    total = EBR[2 + src, 0, b + 1]
                    for c in range(1, cn):
                        total = total + EBR[2 + src, c, b + 1]
                    WINB[(t + 1) * nx : (t + 2) * nx, :] += total

                when_all([there(src)], take)

        when_all([there(t)], gather)
    for n in range(len(ALL)):
        total = KR[0, n]
        for c in range(1, cn):
            total = total + KR[c, n]
        KS[n] = total

    def columns(q):
        for c, grad in enumerate((q - ring(q, 1, 0), q - ring(q, 1, 1))):
            for dz in range(-2, 3):
                QS[dz + 2, c] = ring(grad, dz, 1)[:, 0:LANES]
        out = []
        for c in range(2):
            total = None
            for n, (dx, dz) in enumerate(ALL):
                a = KS[n] * QS[dz + 2, c, nx + dx : 2 * nx + dx, :]
                total = a if total is None else total + a
            out.append(total)
        return out

    q = WINB[...]
    c1 = columns(q)
    me = slab * ng + mine
    A1[me, 0] = q[nx : 2 * nx, 0:LANES]
    A1[me, 1] = c1[0]
    A1[me, 2] = c1[1]
    for k in range(1, steps):
        greeted(k)
        if k + 1 < steps:
            greet(k + 1)

    def share(buf, ssem, rsem):
        order = [0, 1, sn - 1] + list(range(2, sn - 1))
        for ds in list(dict.fromkeys(d % sn for d in order)):
            for dg in range(ng):
                if ds == 0 and dg == 0:
                    continue
                to = lax.rem(mine + dg, ng) * per + lax.rem(cross, per)
                pltpu.make_async_remote_copy(
                    src_ref=buf.at[me], dst_ref=buf.at[me], send_sem=ssem, recv_sem=rsem.at[slab],
                    device_id=dev(lax.rem(slab + ds, sn), to), device_id_type=MESH,
                ).start()

    def shared(buf, rsem, s, n):
        ref = buf.at[pl.ds(0, n)]
        pltpu.make_async_copy(ref, ref, rsem.at[s]).wait()

    share(A1, as1, ar1)
    sweep(1, inner, lambda t: twice(range(nx), t), 1)

    if ng > 1:
        shared(A1, ar1, slab, ng - 1)
    for ds in (-1, 1):
        when_all([there(ds)], lambda: shared(A1, ar1, slab + ds, ng))
    FRAME[...] = jnp.zeros_like(FRAME)
    for t in range(-1, 2):

        def fill():
            for g in range(ng):
                for a in range(3):
                    FRAME[a, (t + 1) * nx : (t + 2) * nx, g * LANES : (g + 1) * LANES] = A1[(slab + t) * ng + g, a]

        when_all([there(t)], fill)
    gwin = FRAME[0]
    cx, cz = FRAME[1], FRAME[2]
    sg = cx - pltpu.roll(cx, 1, 0) + cz - zshift(cz, -1)
    trow = lax.broadcasted_iota(jnp.int32, sg.shape, 0)
    known = (trow < 3 * nx) & ((trow < 2 * nx) | right) & ((trow >= nx) | left)
    sg = jnp.where(known, sg, 0.0)
    WIN[:, 0:LANES] = jnp.zeros((4 * nx, LANES), f32)
    WIN[:, LANES + nz :] = jnp.zeros((4 * nx, LANES), f32)
    WIN[:, LANES : LANES + nz] = sg
    main, halo = wide(lambda i: WIN[:, pl.ds(pl.multiple_of(i * LANES, LANES), LANES)], mine)
    c2 = columns(jnp.concatenate([main, halo], 1))
    A2[me, 0] = c2[0]
    A2[me, 1] = c2[1]
    share(A2, as2, ar2)

    for ds in range(2, sn - 1):
        s = lax.rem(slab + ds, sn)
        shared(A1, ar1, s, ng)
    for ds in (1, -1):
        when_all([jnp.logical_not(there(ds))], lambda: shared(A1, ar1, lax.rem(slab + ds + sn, sn), ng))

    def whole(buf, a, into):
        for s in range(sn):
            for g in range(ng):
                FULL[into, s * nx : (s + 1) * nx, g * LANES : (g + 1) * LANES] = buf[s * ng + g, a]

    def below(a):
        row = lax.broadcasted_iota(jnp.int32, a.shape, 0)
        return jnp.where(row == 0, 0.0, pltpu.roll(a, 1, 0))

    for a in range(3):
        whole(A1, a, a)
    g = FULL[0]
    s1 = FULL[1] - below(FULL[1]) + FULL[2] - zshift(FULL[2], -1)
    rr = jnp.sum(g * g)
    alpha0 = rr / jnp.sum(g * s1)
    resid = g - alpha0 * s1
    fresh = jnp.sum(resid * resid)
    beta = fresh / rr
    dirn = resid + beta * g
    FULL[3] = s1
    FULL[4] = dirn

    dwin = gwin - alpha0 * sg + beta * gwin
    last = (slab == sn - 1) & (trow == 2 * nx - 1)
    kcol = lax.broadcasted_iota(jnp.int32, sg.shape, 1)
    for i, q in enumerate((alpha0 * gwin, dwin)):
        ahead = jnp.where(last, 0.0, ring(q, 1, 0))
        for c, grad in enumerate((q - ahead, q - zshift(q, 1))):
            for dz in range(-2, 3):
                a = grad if dz == 0 else zshift(grad, dz)
                for r in range(nx - 2, 2 * nx + 2):
                    GSR[i, dz + 2, c, r] = a[r : r + 1]

    def apply(i, _):
        p, t = i // inner, i % inner
        at = pl.ds(pl.multiple_of(t * TILE, TILE), TILE)
        base = [BASE[c, p, at, :] for c in range(2)]
        second = [jnp.zeros((TILE, nz), f32) for c in range(2)]
        for n, (dx, dz) in enumerate(ALL):
            m = M[n, p, at, :]
            for c in range(2):
                base[c] = base[c] - m * GSR[0, dz + 2, c, p + nx + dx]
                second[c] = second[c] + m * GSR[1, dz + 2, c, p + nx + dx]
        for c in range(2):
            BASE[c, p, at, :] = base[c]
            FD[c, p, at, :] = second[c]
        return 0

    lax.fori_loop(0, nx * inner, apply, 0)

    width = press.shape[1]
    slot = lax.broadcasted_iota(jnp.int32, (width, nz), 0) + cross * width
    onehot = (jnp.broadcast_to(owner[...], (width, nz)) == slot).astype(f32)

    def ordered(a):
        return lax.dot_general(
            a, onehot, (((1,), (1,)), ((), ())), precision=lax.Precision.HIGHEST, preferred_element_type=f32
        )

    p0 = ordered(alpha0 * gwin[nx : 2 * nx])
    p1 = ordered(dwin[nx : 2 * nx])

    if ng > 1:
        shared(A2, ar2, slab, ng - 1)
    for ds in range(1, sn):
        shared(A2, ar2, lax.rem(slab + ds, sn), ng)
    for a in range(2):
        whole(A2, a, a)
    s2 = FULL[0] - below(FULL[0]) + FULL[1] - zshift(FULL[1], -1)
    s1 = FULL[3]
    image = s1 - alpha0 * s2 + beta * s1
    alpha1 = fresh / jnp.sum(FULL[4] * image)
    press[...] = p0 + alpha1 * p1

    outs = []
    for p in range(nx):

        def finish(t, _):
            at = pl.ds(pl.multiple_of(t * TILE, TILE), TILE)
            for c in range(2):
                BASE[c, p, at, :] = BASE[c, p, at, :] - alpha1 * FD[c, p, at, :]
            return 0

        lax.fori_loop(0, inner, finish, 0)
        out = pltpu.make_async_copy(BASE.at[:, p], vel.at[:, p], osem.at[p])
        out.start()
        outs.append(out)
    for out in outs:
        out.wait()

    for conds, make in viscous + forces:
        when_all(conds, lambda: make().wait_send())
    for ds in range(-2, 3):

        def left_here():
            ref = EBR.at[2 - ds, pl.ds(0, cn - 1 if ds == 0 else cn), span(ds)]
            pltpu.make_async_copy(ref, ref, bs.at[ds + 2]).wait()

        when_all([there(ds)], left_here)
    pltpu.make_async_copy(KR.at[pl.ds(0, cn - 1)], KR.at[pl.ds(0, cn - 1)], ks).wait()
    for buf, sem in ((A1, as1), (A2, as2)):
        ref = buf.at[pl.ds(0, sn * ng - 1)]
        pltpu.make_async_copy(ref, ref, sem).wait()


def stokes(forcing, viscosity, owner, sn, cn):
    nx, ny, nz = viscosity.shape
    f32 = jnp.float32
    ng, _ = chunks(cn, nz)
    no = len(ALL)
    ye = ny + 2 * TILE
    vmem = pl.BlockSpec(memory_space=pltpu.VMEM)
    anywhere = pl.BlockSpec(memory_space=pl.ANY)
    dma = pltpu.SemaphoreType.DMA

    def buf(*shape):
        return pltpu.VMEM(shape, f32)

    return pl.pallas_call(
        functools.partial(stokes_body, sn, cn),
        out_shape=(
            jax.ShapeDtypeStruct(forcing.shape, f32),
            jax.ShapeDtypeStruct((nx, nz // cn), f32),
        ),
        in_specs=[anywhere, anywhere, vmem],
        out_specs=(anywhere, vmem),
        scratch_shapes=[
            buf(nx + 6, ye, nz),
            buf(2, nx + 4, ye, nz),
            buf(2, nx, 4, nz),
            buf(2, 2, nx, 2, nz),
            buf(2, nx, 4, nz),
            buf(2, 2, 2, 4, nz),
            buf(2, 2, nx, 2, nz),
            buf(2, 2, 2, 1, 2, nz),
            buf(nx + 4, ye, nz),
            buf(5, nx + 2, ye, nz),
            buf(no, nx, ny, nz),
            buf(2, nx + 4, ye, nz),
            buf(2, nx + 2, ye, nz),
            buf(2, nx, ny, nz),
            buf(2, nx, ny, nz),
            buf(no, nx, nz),
            buf(no, 2, nx, nz),
            buf(3, 4 * nx, nz),
            buf(ng, no, nx, LANES),
            buf(cn, no, nx, LANES),
            buf(ng, 3, nx, 2 * LANES),
            buf(5, cn, 3, nx, 2 * LANES),
            buf(sn * ng, 3, nx, LANES),
            buf(sn * ng, 2, nx, LANES),
            buf(4 * nx, nz + 2 * LANES),
            buf(5, 2, 4 * nx, LANES),
            buf(no, nx, LANES),
            buf(2, 5, 2, 4 * nx, 1, nz),
            buf(5, sn * nx, nz),
            dma((2,)),
            dma((22,)),
            dma((22,)),
            dma((5,)),
            dma((5,)),
            dma,
            dma,
            dma,
            dma((sn,)),
            dma,
            dma((sn,)),
            dma((nx,)),
            pltpu.SemaphoreType.REGULAR((max(1, (sn - 2).bit_length()),)),
        ],
        compiler_params=pltpu.CompilerParams(
            collective_id=0, has_side_effects=True, vmem_limit_bytes=56 * 2**20
        ),
        name="stokes",
    )(viscosity, forcing, owner)


def shards(forcing, viscosity, owner_slot):
    sn, cn = lax.axis_size("slab"), lax.axis_size("cross")
    return stokes(forcing, viscosity, owner_slot.reshape(1, -1), sn, cn)


def solution(mesh):
    in_specs = (P(None, "slab", "cross", None), P("slab", "cross", None), P())
    out_specs = (P(None, "slab", "cross", None), P("slab", "cross"))
    return jax.shard_map(shards, mesh=mesh, in_specs=in_specs, out_specs=out_specs, check_vma=False)
```

```python
import functools

import jax
import jax.numpy as jnp
from jax import lax
from jax.experimental import pallas as pl
from jax.experimental.pallas import tpu as pltpu
from jax.sharding import PartitionSpec as P

MESH = pl.DeviceIdType.MESH

DEGREE = 3
LANES = 128
TILE = 8

cheb_theta = 1.025
cheb_delta = 0.975


def cheb_weights():
    sigma = cheb_theta / cheb_delta
    solved = [1.0 / cheb_theta] + [0.0] * (DEGREE - 1)
    change = list(solved)
    rho_prev = 1.0 / sigma
    for step in range(DEGREE - 1):
        resid = [(1.0 if k == 0 else solved[k - 1]) - solved[k] for k in range(DEGREE)]
        rho = 1.0 / (2.0 * sigma - rho_prev)
        change = [rho * rho_prev * c + 2.0 * rho / cheb_delta * r for c, r in zip(change, resid)]
        solved = [s + c for s, c in zip(solved, change)]
        rho_prev = rho
    return solved


NEAR = [(0, 0), (1, 0), (-1, 0), (0, 1), (0, -1)]
ALL = [(dx, dz) for dx in range(-2, 3) for dz in range(-2, 3) if abs(dx) + abs(dz) <= 2]


def chunks(cn, nz):
    n = min(cn, nz // LANES)
    return n, cn // n


def zshift(a, d):
    n = a.shape[-1]
    k = lax.broadcasted_iota(jnp.int32, a.shape, a.ndim - 1)
    keep = (k < n - d) if d > 0 else (k >= -d)
    return jnp.where(keep, pltpu.roll(a, (-d) % n, a.ndim - 1), 0.0)


def ring(a, d, axis):
    return a if d == 0 else pltpu.roll(a, (-d) % a.shape[axis], axis)


def rows(ref, lead, t, last):
    def tile(i):
        return ref[lead + (pl.ds(pl.multiple_of(i * TILE, TILE), TILE), slice(None))]

    cur = tile(t)
    row = lax.broadcasted_iota(jnp.int32, cur.shape, 0)
    up = pltpu.roll(jnp.where(row == 0, tile(jnp.minimum(t + 1, last)), cur), TILE - 1, 0)
    down = pltpu.roll(jnp.where(row == TILE - 1, tile(jnp.maximum(t - 1, 0)), cur), 1, 0)
    return cur, up, down


def stokes_body(
    sn, cn, visc, forc, owner, base, second, small,
    V, F, ypk, fpk, YV, CV, YF, CF, DI, U, M, Y0, Z, BASE, FD,
    KF, CS, FRAME, KP, KR, EB, EBR, A1, A2, WIN, QS, KS, GSR, FULL,
    lsem, hs, hr, bs, br, ks, kr, as1, ar1, as2, ar2, osem, hop,
):
    slab, cross = lax.axis_index("slab"), lax.axis_index("cross")
    nx, ny, nz = visc.shape
    nt = ny // TILE + 2
    ng, per = chunks(cn, nz)
    mine = cross // per
    f32 = jnp.float32
    w0, w1, w2 = [2.0 * w for w in cheb_weights()]

    def dev(s, c):
        return {"slab": s, "cross": c}

    def there(ds):
        return (slab + ds >= 0) & (slab + ds < sn)

    def others(dc):
        return lax.rem(cross + dc, cn)

    left, right = slab > 0, slab < sn - 1
    up, down = cross > 0, cross < cn - 1
    side, wall = (left, right), (up, down)
    own = pl.ds(TILE, ny)

    load_v = pltpu.make_async_copy(visc, V.at[pl.ds(3, nx), own], lsem.at[0])
    load_f = pltpu.make_async_copy(forc, F.at[:, pl.ds(2, nx), own], lsem.at[1])
    load_v.start()
    load_f.start()
    barrier = pltpu.get_barrier_semaphore()
    for ds in (0, 1, -1):
        for dc in range(cn):
            if ds == 0 and dc == 0:
                continue
            if ds == 0:
                pl.semaphore_signal(barrier, inc=1, device_id=dev(slab, others(dc)), device_id_type=MESH)
            else:

                @pl.when(there(ds))
                def _():
                    pl.semaphore_signal(barrier, inc=1, device_id=dev(slab + ds, others(dc)), device_id_type=MESH)

    zero_v = jnp.zeros((nx + 6, TILE, nz), f32)
    V[:, 0:TILE, :] = zero_v
    V[:, TILE + ny : 2 * TILE + ny, :] = zero_v
    zero_f = jnp.zeros((2, nx + 4, TILE, nz), f32)
    F[:, :, 0:TILE, :] = zero_f
    F[:, :, TILE + ny : 2 * TILE + ny, :] = zero_f
    for s in range(2):

        @pl.when(jnp.logical_not(side[s]))
        def _():
            v0, f0 = (0, 0) if s == 0 else (nx + 3, nx + 2)
            V[v0 : v0 + 3, TILE : TILE + ny, :] = jnp.zeros((3, ny, nz), f32)
            F[:, f0 : f0 + 2, TILE : TILE + ny, :] = jnp.zeros((2, 2, ny, nz), f32)

    count = (cn - 1) + cn * (jnp.where(left, 1, 0) + jnp.where(right, 1, 0))
    pl.semaphore_wait(barrier, count)

    steps = max(0, (sn - 2).bit_length())

    def greet(k):
        for d in (-(2**k), 2**k):

            @pl.when(there(d))
            def _():
                pl.semaphore_signal(hop.at[k], inc=1, device_id=dev(slab + d, cross), device_id_type=MESH)

    def greeted(k):
        pl.semaphore_wait(hop.at[k], jnp.where(there(-(2**k)), 1, 0) + jnp.where(there(2**k), 1, 0))

    def send(src, dst, out, into, s, c):
        return pltpu.make_async_remote_copy(
            src_ref=src, dst_ref=dst, send_sem=hs.at[out], recv_sem=hr.at[into], device_id=dev(s, c),
            device_id_type=MESH,
        )

    def vx(s, k):
        src = visc.at[k if s == 0 else nx - 1 - k]
        dst = V.at[nx + 3 + k if s == 0 else 2 - k, own]
        return send(src, dst, s * 3 + k, (1 - s) * 3 + k, slab + (2 * s - 1), cross)

    def vy(w):
        return send(ypk.at[w], YV.at[1 - w], 6 + w, 7 - w, slab, cross + (2 * w - 1))

    def vc(w, s):
        src = ypk.at[w, pl.ds(0 if s == 0 else nx - 2, 2)]
        return send(src, CV.at[1 - w, 1 - s], 8 + 2 * w + s, 8 + 2 * (1 - w) + 1 - s, slab + (2 * s - 1), cross + (2 * w - 1))

    def fx(s, k):
        src = forc.at[:, k if s == 0 else nx - 1 - k]
        dst = F.at[:, nx + 2 + k if s == 0 else 1 - k, own]
        return send(src, dst, 12 + 2 * s + k, 12 + 2 * (1 - s) + k, slab + (2 * s - 1), cross)

    def fy(w):
        return send(fpk.at[w], YF.at[1 - w], 16 + w, 17 - w, slab, cross + (2 * w - 1))

    def fc(w, s):
        src = fpk.at[w, :, pl.ds(0 if s == 0 else nx - 1, 1)]
        return send(src, CF.at[1 - w, 1 - s], 18 + 2 * w + s, 18 + 2 * (1 - w) + 1 - s, slab + (2 * s - 1), cross + (2 * w - 1))

    def landed(ref, into):
        pltpu.make_async_copy(ref, ref, hr.at[into]).wait()

    def when_all(conds, run):
        cond = conds[0]
        for c in conds[1:]:
            cond = cond & c
        pl.when(cond)(run)

    first = [([side[s]], functools.partial(vx, s, 0)) for s in range(2)]
    walls = [([wall[w]], functools.partial(vy, w)) for w in range(2)]
    corners = [([wall[w], side[s]], functools.partial(vc, w, s)) for w in range(2) for s in range(2)]
    later = [([side[s]], functools.partial(vx, s, k)) for k in (1, 2) for s in range(2)]
    forces = [([wall[w]], functools.partial(fy, w)) for w in range(2)]
    forces += [([wall[w], side[s]], functools.partial(fc, w, s)) for w in range(2) for s in range(2)]
    bulk = [([side[s]], functools.partial(fx, s, k)) for k in range(2) for s in range(2)]

    def begin(sends):
        for conds, make in sends:
            when_all(conds, lambda: make().start())

    begin(first)
    load_v.wait()
    ypk[0] = V[3 : 3 + nx, TILE : TILE + 4, :]
    ypk[1] = V[3 : 3 + nx, TILE + ny - 4 : TILE + ny, :]
    begin(walls + corners + later)
    load_f.wait()
    fpk[0] = F[:, 2 : 2 + nx, TILE : TILE + 2, :]
    fpk[1] = F[:, 2 : 2 + nx, TILE + ny - 2 : TILE + ny, :]
    begin(forces + bulk[:2])
    if steps > 0:
        greet(0)

    inner = nt - 2

    def sweep(lo, n, body, k=2):
        while n % k:
            k -= 1

        def step(i, _):
            for j in range(k):
                body(lo + i * k + j)
            return 0

        lax.fori_loop(0, n // k, step, 0)

    def tile(t):
        return pl.ds(t * TILE if isinstance(t, int) else pl.multiple_of(t * TILE, TILE), TILE)

    def inside(plane, t):
        ok = ((t > 0) | up) & ((t < nt - 1) | down)
        if plane < 0:
            ok = ok & left
        if plane >= nx:
            ok = ok & right
        return jnp.where(ok, 1.0, 0.0)

    def diagonal(planes, t):
        for p in planes:
            c, yp, ym = rows(V, (p + 3,), t, nt - 1)
            diag = V[p + 4, tile(t), :] + V[p + 2, tile(t), :] + yp + ym + zshift(c, 1) + zshift(c, -1) + 6.0 * c
            DI[p + 2, tile(t), :] = inside(p, t) * (1.0 / jnp.maximum(diag, 1e-30))

    def near(planes, comps, t):
        for p in planes:
            at = tile(t)
            v, vyp, vym = rows(V, (p + 3,), t, nt - 1)
            d, dyp, dym = rows(DI, (p + 2,), t, nt - 1)
            wd = w2 * d
            if 0 in comps:
                U[0, p + 1, at, :] = wd * ((v + vyp) * dyp + (v + vym) * dym) + w1 * d
            if 1 in comps:
                U[1, p + 1, at, :] = wd * ((v + V[p + 4, at, :]) * DI[p + 3, at, :])
            if 2 in comps:
                U[2, p + 1, at, :] = wd * ((v + V[p + 2, at, :]) * DI[p + 1, at, :])
            if 3 in comps:
                U[3, p + 1, at, :] = wd * ((v + zshift(v, 1)) * zshift(d, 1))
                U[4, p + 1, at, :] = wd * ((v + zshift(v, -1)) * zshift(d, -1))

    def coefficients(planes, t):
        for p in planes:
            at, to = tile(t), tile(t - 1)
            v, vyp, vym = rows(V, (p + 3,), t, nt - 1)
            d = DI[p + 2, at, :]
            yp, ym = d * (v + vyp), d * (v + vym)
            xp, xm = d * (v + V[p + 4, at, :]), d * (v + V[p + 2, at, :])
            zp, zm = d * (v + zshift(v, 1)), d * (v + zshift(v, -1))
            acc = {(0, 0): w0 * d}

            def add(o, a):
                acc[o] = acc[o] + a if o in acc else a

            for n, (dx, dz) in enumerate(NEAR):
                c, cu, cd = rows(U, (n, p + 1), t, nt - 1)
                add((dx, dz), yp * cu + ym * cd)
                if dx < 1:
                    add((dx + 1, dz), xp * U[n, p + 2, at, :])
                if dx > -1:
                    add((dx - 1, dz), xm * U[n, p, at, :])
                add((dx, dz + 1), zp * zshift(c, 1))
                add((dx, dz - 1), zm * zshift(c, -1))
            for o in acc:
                M[ALL.index(o), p, to, :] = acc[o]

    def far(pairs, t):
        for p, d in pairs:
            at = tile(t)
            v0, v1, v2 = [V[p + 3 + d * k, at, :] for k in range(3)]
            d0, d1, d2 = [DI[p + 2 + d * k, at, :] for k in range(3)]
            M[ALL.index((2 * d, 0)), p, tile(t - 1), :] = w2 * (d0 * (v0 + v1)) * (d1 * (v1 + v2)) * d2

    prow = lax.broadcasted_iota(jnp.int32, (nx, nz), 0)
    KF[...] = jnp.zeros_like(KF)
    CS[...] = jnp.zeros_like(CS)

    def sums(p, offsets):
        for o in offsets:
            n = ALL.index(o)
            acc = None
            for t in range(inner):
                m = M[n, p, tile(t), :]
                new = (m, m * F[0, p + 2, tile(t + 1), :], m * F[1, p + 2, tile(t + 1), :])
                acc = new if acc is None else [a + b for a, b in zip(acc, new)]
            here = prow == p
            for ref, a in zip((KF.at[n], CS.at[n, 0], CS.at[n, 1]), acc):
                ref[...] = jnp.where(here, jnp.sum(a, axis=0, keepdims=True), ref[...])

    short = [o for o in ALL if abs(o[0]) < 2]
    mids, ends = list(range(1, nx - 1)), [0, nx - 1]

    def plane_sums(first, stride, n):
        def step(i, _):
            sums(first + i * stride, short)
            return 0

        lax.fori_loop(0, n, step, 0)

    sweep(2, inner - 2, lambda t: diagonal(mids, t))
    for s in range(2):
        when_all([side[s]], lambda: landed(V.at[nx + 3 if s == 1 else 2, own], s * 3))
    for w in range(2):

        def put():
            landed(YV.at[w], 6 + w)
            r0 = 4 if w == 0 else TILE + ny
            V[3 : 3 + nx, r0 : r0 + 4, :] = YV[w]

        when_all([wall[w]], put)
    for t in (0, 1, nt - 2, nt - 1):
        diagonal(mids, t)
    sweep(1, inner, lambda t: diagonal(ends, t))
    for w in range(2):
        for s in range(2):

            def put():
                landed(CV.at[w, s], 8 + 2 * w + s)
                r0 = 4 if w == 0 else TILE + ny
                p0 = 1 if s == 0 else nx + 3
                V[p0 : p0 + 2, r0 : r0 + 4, :] = CV[w, s]

            when_all([wall[w], side[s]], put)
    for t in (0, nt - 1):
        diagonal(ends, t)
    sweep(0, nt, lambda t: near(mids, (0, 1, 2, 3), t))
    sweep(0, nt, lambda t: (near([0], (0, 1, 3), t), near([nx - 1], (0, 2, 3), t)))
    sweep(1, inner, lambda t: coefficients(mids, t), 1)
    plane_sums(1, 1, nx - 2)
    for s in range(2):
        when_all([side[s]], lambda: landed(V.at[nx + 4 if s == 1 else 1, own], s * 3 + 1))
    sweep(0, nt, lambda t: diagonal([-1, nx], t))
    sweep(0, nt, lambda t: (near([-1], (0, 1, 3), t), near([nx], (0, 2, 3), t), near([0], (2,), t), near([nx - 1], (1,), t)))
    sweep(1, inner, lambda t: coefficients(ends, t), 1)
    plane_sums(0, nx - 1, 2)
    ready = [(p, d) for p in range(nx) for d in (1, -1) if 0 <= p + d < nx]
    sweep(1, inner, lambda t: far(ready, t), 1)
    for p, d in ready:
        sums(p, [(2 * d, 0)])
    for s in range(2):
        when_all([side[s]], lambda: landed(V.at[nx + 5 if s == 1 else 0, own], s * 3 + 2))
    sweep(1, inner, lambda t: diagonal([-2, nx + 1], t))
    sweep(1, inner, lambda t: far([(0, -1), (nx - 1, 1)], t))
    sums(0, [(-2, 0)])
    sums(nx - 1, [(2, 0)])

    FRAME[...] = jnp.zeros_like(FRAME)
    for c in range(2):
        for dx in range(-2, 3):
            total = None
            for n, o in enumerate(ALL):
                if o[0] == dx:
                    a = CS[n, c]
                    a = a if o[1] == 0 else zshift(a, -o[1])
                    total = a if total is None else total + a
            FRAME[c, nx + dx : 2 * nx + dx, :] += total
    cx, cz = FRAME[0], FRAME[1]
    e = cx - pltpu.roll(cx, 1, 0) + cz - zshift(cz, -1)
    WIN[:, 0:LANES] = jnp.zeros((4 * nx, LANES), f32)
    WIN[:, LANES + nz :] = jnp.zeros((4 * nx, LANES), f32)
    WIN[:, LANES : LANES + nz] = e

    def wide(get, g):
        main, before, after = get(g + 1), get(g), get(g + 2)
        lane = lax.broadcasted_iota(jnp.int32, main.shape, 1)
        return main, jnp.where(lane < LANES // 2, after, before)

    for g in range(ng):
        main, halo = wide(lambda i: WIN[:, i * LANES : (i + 1) * LANES], g)
        for b in range(3):
            EB[g, b, :, 0:LANES] = main[b * nx : (b + 1) * nx]
            EB[g, b, :, LANES : 2 * LANES] = halo[b * nx : (b + 1) * nx]
        for n in range(len(ALL)):
            KP[g, n] = KF[n, :, g * LANES : (g + 1) * LANES]

    if steps > 0:
        greeted(0)
        if steps > 1:
            greet(1)

    def span(ds):
        return pl.ds(max(0, ds), 3 - abs(ds))

    def e_copy(ds, dc):
        return pltpu.make_async_remote_copy(
            src_ref=EB.at[others(dc) // per, span(ds)], dst_ref=EBR.at[2 - ds, cross, span(ds)],
            send_sem=bs.at[ds + 2], recv_sem=br.at[2 - ds], device_id=dev(slab + ds, others(dc)), device_id_type=MESH,
        )

    for ds in (0, 1, -1, 2, -2):

        def start():
            for dc in range(1 if ds == 0 else 0, cn):
                e_copy(ds, dc).start()

        when_all([there(ds)], start)
    for dc in range(1, cn):
        pltpu.make_async_remote_copy(
            src_ref=KP.at[others(dc) // per], dst_ref=KR.at[cross], send_sem=ks, recv_sem=kr,
            device_id=dev(slab, others(dc)), device_id_type=MESH,
        ).start()
    for b in range(3):
        EBR[2, cross, b] = EB[mine, b]
    KR[cross] = KP[mine]

    begin(bulk[2:])

    def forced(k):
        for s in range(2):
            when_all([side[s]], lambda: landed(F.at[:, nx + 2 + k if s == 1 else 1 - k, own], 12 + 2 * s + k))

    forced(0)
    for w in range(2):

        def put():
            landed(YF.at[w], 16 + w)
            r0 = TILE - 2 if w == 0 else TILE + ny
            F[:, 2 : 2 + nx, r0 : r0 + 2, :] = YF[w]

        when_all([wall[w]], put)
        for s in range(2):

            def put():
                landed(CF.at[w, s], 18 + 2 * w + s)
                r0 = TILE - 2 if w == 0 else TILE + ny
                p0 = 1 if s == 0 else nx + 2
                F[:, p0 : p0 + 1, r0 : r0 + 2, :] = CF[w, s]

            when_all([wall[w], side[s]], put)

    def scaled(planes, t):
        for p in planes:
            d = DI[p, tile(t), :]
            for c in range(2):
                Y0[c, p, tile(t), :] = d * F[c, p, tile(t), :]

    def faces(p, t):
        at = tile(t)
        v, vyp, vym = rows(V, (p + 3,), t, nt - 1)
        d = DI[p + 2, at, :]
        return (
            d * (v + vyp), d * (v + vym), d * (v + V[p + 4, at, :]), d * (v + V[p + 2, at, :]),
            d * (v + zshift(v, 1)), d * (v + zshift(v, -1)),
        )

    def carried(field, c, p, t, face):
        yp, ym, xp, xm, zp, zm = face
        a, au, ad = rows(field, (c, p), t, nt - 1)
        near_by = yp * au + ym * ad + xp * field[c, p + 1, tile(t), :] + xm * field[c, p - 1, tile(t), :]
        return a, near_by + zp * zshift(a, 1) + zm * zshift(a, -1)

    def once(planes, t):
        for p in planes:
            face = faces(p, t)
            for c in range(2):
                a, t1 = carried(Y0, c, p + 2, t, face)
                Z[c, p + 1, tile(t), :] = w1 * a + w2 * t1

    def twice(planes, t):
        for p in planes:
            face = faces(p, t)
            for c in range(2):
                a, t2 = carried(Z, c, p + 1, t, face)
                BASE[c, p, tile(t - 1), :] = w0 * Y0[c, p + 2, tile(t), :] + t2

    sweep(0, nt, lambda t: scaled(range(1, nx + 3), t))
    sweep(0, nt, lambda t: once(range(nx), t), 1)
    sweep(1, inner, lambda t: twice(mids, t), 1)

    e_mine = cn - 1
    for ds in range(-2, 3):
        src = -ds

        def wait():
            n = cn - 1 if ds == 0 else cn
            ref = EBR.at[2 + src, pl.ds(0, n), span(ds)]
            pltpu.make_async_copy(ref, ref, br.at[2 + src]).wait()

        when_all([there(src)], wait)
    pltpu.make_async_copy(KR.at[pl.ds(0, e_mine)], KR.at[pl.ds(0, e_mine)], kr).wait()
    WINB = WIN.at[:, 0 : 2 * LANES]
    WINB[3 * nx :, :] = jnp.zeros((nx, 2 * LANES), f32)
    for t in range(-1, 2):
        WINB[(t + 1) * nx : (t + 2) * nx, :] = jnp.zeros((nx, 2 * LANES), f32)

        def gather():
            for b in range(-1, 2):
                src = t - b

                def take():
                    total = EBR[2 + src, 0, b + 1]
                    for c in range(1, cn):
                        total = total + EBR[2 + src, c, b + 1]
                    WINB[(t + 1) * nx : (t + 2) * nx, :] += total

                when_all([there(src)], take)

        when_all([there(t)], gather)
    for n in range(len(ALL)):
        total = KR[0, n]
        for c in range(1, cn):
            total = total + KR[c, n]
        KS[n] = total

    def columns(q):
        for c, grad in enumerate((q - ring(q, 1, 0), q - ring(q, 1, 1))):
            for dz in range(-2, 3):
                QS[dz + 2, c] = ring(grad, dz, 1)[:, 0:LANES]
        out = []
        for c in range(2):
            total = None
            for n, (dx, dz) in enumerate(ALL):
                a = KS[n] * QS[dz + 2, c, nx + dx : 2 * nx + dx, :]
                total = a if total is None else total + a
            out.append(total)
        return out

    q = WINB[...]
    c1 = columns(q)
    me = slab * ng + mine
    A1[me, 0] = q[nx : 2 * nx, 0:LANES]
    A1[me, 1] = c1[0]
    A1[me, 2] = c1[1]
    for k in range(1, steps):
        greeted(k)
        if k + 1 < steps:
            greet(k + 1)

    def share(buf, ssem, rsem):
        order = [0, 1, sn - 1] + list(range(2, sn - 1))
        for ds in list(dict.fromkeys(d % sn for d in order)):
            for dg in range(ng):
                if ds == 0 and dg == 0:
                    continue
                to = lax.rem(mine + dg, ng) * per + lax.rem(cross, per)
                pltpu.make_async_remote_copy(
                    src_ref=buf.at[me], dst_ref=buf.at[me], send_sem=ssem, recv_sem=rsem.at[slab],
                    device_id=dev(lax.rem(slab + ds, sn), to), device_id_type=MESH,
                ).start()

    def shared(buf, rsem, s, n):
        ref = buf.at[pl.ds(0, n)]
        pltpu.make_async_copy(ref, ref, rsem.at[s]).wait()

    share(A1, as1, ar1)
    forced(1)
    sweep(0, nt, lambda t: scaled([0, nx + 3], t))
    sweep(0, nt, lambda t: once([-1, nx], t), 1)
    sweep(1, inner, lambda t: twice(ends, t), 1)

    if ng > 1:
        shared(A1, ar1, slab, ng - 1)
    for ds in (-1, 1):
        when_all([there(ds)], lambda: shared(A1, ar1, slab + ds, ng))
    FRAME[...] = jnp.zeros_like(FRAME)
    for t in range(-1, 2):

        def fill():
            for g in range(ng):
                for a in range(3):
                    FRAME[a, (t + 1) * nx : (t + 2) * nx, g * LANES : (g + 1) * LANES] = A1[(slab + t) * ng + g, a]

        when_all([there(t)], fill)
    gwin = FRAME[0]
    cx, cz = FRAME[1], FRAME[2]
    sg = cx - pltpu.roll(cx, 1, 0) + cz - zshift(cz, -1)
    trow = lax.broadcasted_iota(jnp.int32, sg.shape, 0)
    known = (trow < 3 * nx) & ((trow < 2 * nx) | right) & ((trow >= nx) | left)
    sg = jnp.where(known, sg, 0.0)
    WIN[:, 0:LANES] = jnp.zeros((4 * nx, LANES), f32)
    WIN[:, LANES + nz :] = jnp.zeros((4 * nx, LANES), f32)
    WIN[:, LANES : LANES + nz] = sg
    main, halo = wide(lambda i: WIN[:, pl.ds(pl.multiple_of(i * LANES, LANES), LANES)], mine)
    c2 = columns(jnp.concatenate([main, halo], 1))
    A2[me, 0] = c2[0]
    A2[me, 1] = c2[1]
    share(A2, as2, ar2)

    for i, q in enumerate((gwin, sg)):
        for c, grad in enumerate((q - ring(q, 1, 0), q - zshift(q, 1))):
            for dz in range(-2, 3):
                a = grad if dz == 0 else zshift(grad, dz)
                for r in range(nx - 2, 2 * nx + 2):
                    GSR[i, dz + 2, c, r] = a[r : r + 1]

    def apply(i, _):
        p, t = i // inner, i % inner
        at = tile(t)
        total = [[None, None], [None, None]]
        for n, (dx, dz) in enumerate(ALL):
            m = M[n, p, at, :]
            for j in range(2):
                for c in range(2):
                    a = m * GSR[j, dz + 2, c, p + nx + dx]
                    total[j][c] = a if total[j][c] is None else total[j][c] + a
        for j in range(2):
            for c in range(2):
                FD[j, c, p, at, :] = total[j][c]
        return 0

    lax.fori_loop(0, nx * inner, apply, 0)

    width = nz // cn
    slot = lax.broadcasted_iota(jnp.int32, (width, nz), 0) + cross * width
    onehot = (jnp.broadcast_to(owner[...], (width, nz)) == slot).astype(f32).astype(jnp.bfloat16)
    rest = jnp.concatenate([gwin[nx : 2 * nx], sg[nx : 2 * nx]], 0)
    ordered = jnp.zeros((2 * nx, width), f32)
    for _ in range(3):
        piece = rest.astype(jnp.bfloat16)
        rest = rest - piece.astype(f32)
        ordered = ordered + lax.dot_general(
            piece, onehot, (((1,), (1,)), ((), ())), preferred_element_type=f32
        )

    for ds in range(2, sn - 1):
        s = lax.rem(slab + ds, sn)
        shared(A1, ar1, s, ng)
    for ds in (1, -1):
        when_all([jnp.logical_not(there(ds))], lambda: shared(A1, ar1, lax.rem(slab + ds + sn, sn), ng))

    def whole(buf, a, into):
        for s in range(sn):
            for g in range(ng):
                FULL[into, s * nx : (s + 1) * nx, g * LANES : (g + 1) * LANES] = buf[s * ng + g, a]

    def below(a):
        row = lax.broadcasted_iota(jnp.int32, a.shape, 0)
        return jnp.where(row == 0, 0.0, pltpu.roll(a, 1, 0))

    for a in range(3):
        whole(A1, a, a)
    g = FULL[0]
    s1 = FULL[1] - below(FULL[1]) + FULL[2] - zshift(FULL[2], -1)
    rr = jnp.sum(g * g)
    alpha0 = rr / jnp.sum(g * s1)
    resid = g - alpha0 * s1
    fresh = jnp.sum(resid * resid)
    beta = fresh / rr
    dirn = resid + beta * g
    FULL[3] = s1
    FULL[4] = dirn

    outs = []
    for p in range(nx):

        def combine(t, _):
            at = tile(t)
            for c in range(2):
                a, b = FD[0, c, p, at, :], FD[1, c, p, at, :]
                BASE[c, p, at, :] = BASE[c, p, at, :] - alpha0 * a
                FD[0, c, p, at, :] = a - alpha0 * b + beta * a
            return 0

        lax.fori_loop(0, inner, combine, 0)
        for i, (a, b) in enumerate(((BASE.at[:, p], base.at[:, p]), (FD.at[0, :, p], second.at[:, p]))):
            out = pltpu.make_async_copy(a, b, osem.at[i, p])
            out.start()
            outs.append(out)
    pg, ps = ordered[:nx], ordered[nx:]
    small[0:nx, :] = alpha0 * pg
    small[nx : 2 * nx, :] = pg - alpha0 * ps + beta * pg

    if ng > 1:
        shared(A2, ar2, slab, ng - 1)
    for ds in range(1, sn):
        shared(A2, ar2, lax.rem(slab + ds, sn), ng)
    for a in range(2):
        whole(A2, a, a)
    s2 = FULL[0] - below(FULL[0]) + FULL[1] - zshift(FULL[1], -1)
    s1 = FULL[3]
    image = s1 - alpha0 * s2 + beta * s1
    alpha1 = fresh / jnp.sum(FULL[4] * image)
    small[2 * nx : 3 * nx, :] = jnp.full((nx, width), alpha1, f32)
    for out in outs:
        out.wait()

    for conds, make in first + walls + corners + later + forces + bulk:
        when_all(conds, lambda: make().wait_send())
    for ds in range(-2, 3):

        def left_here():
            ref = EBR.at[2 - ds, pl.ds(0, cn - 1 if ds == 0 else cn), span(ds)]
            pltpu.make_async_copy(ref, ref, bs.at[ds + 2]).wait()

        when_all([there(ds)], left_here)
    pltpu.make_async_copy(KR.at[pl.ds(0, cn - 1)], KR.at[pl.ds(0, cn - 1)], ks).wait()
    for buf, sem in ((A1, as1), (A2, as2)):
        ref = buf.at[pl.ds(0, sn * ng - 1)]
        pltpu.make_async_copy(ref, ref, sem).wait()


def stokes(forcing, viscosity, owner, sn, cn):
    nx, ny, nz = viscosity.shape
    f32 = jnp.float32
    ng, _ = chunks(cn, nz)
    no = len(ALL)
    ye = ny + 2 * TILE
    vmem = pl.BlockSpec(memory_space=pltpu.VMEM)
    anywhere = pl.BlockSpec(memory_space=pl.ANY)
    dma = pltpu.SemaphoreType.DMA

    def buf(*shape):
        return pltpu.VMEM(shape, f32)

    return pl.pallas_call(
        functools.partial(stokes_body, sn, cn),
        out_shape=(
            jax.ShapeDtypeStruct(forcing.shape, f32),
            jax.ShapeDtypeStruct(forcing.shape, f32),
            jax.ShapeDtypeStruct((3 * nx, nz // cn), f32),
        ),
        in_specs=[anywhere, anywhere, vmem],
        out_specs=(anywhere, anywhere, vmem),
        scratch_shapes=[
            buf(nx + 6, ye, nz),
            buf(2, nx + 4, ye, nz),
            buf(2, nx, 4, nz),
            buf(2, 2, nx, 2, nz),
            buf(2, nx, 4, nz),
            buf(2, 2, 2, 4, nz),
            buf(2, 2, nx, 2, nz),
            buf(2, 2, 2, 1, 2, nz),
            buf(nx + 4, ye, nz),
            buf(5, nx + 2, ye, nz),
            buf(no, nx, ny, nz),
            buf(2, nx + 4, ye, nz),
            buf(2, nx + 2, ye, nz),
            buf(2, nx, ny, nz),
            buf(2, 2, nx, ny, nz),
            buf(no, nx, nz),
            buf(no, 2, nx, nz),
            buf(3, 4 * nx, nz),
            buf(ng, no, nx, LANES),
            buf(cn, no, nx, LANES),
            buf(ng, 3, nx, 2 * LANES),
            buf(5, cn, 3, nx, 2 * LANES),
            buf(sn * ng, 3, nx, LANES),
            buf(sn * ng, 2, nx, LANES),
            buf(4 * nx, nz + 2 * LANES),
            buf(5, 2, 4 * nx, LANES),
            buf(no, nx, LANES),
            buf(2, 5, 2, 4 * nx, 1, nz),
            buf(5, sn * nx, nz),
            dma((2,)),
            dma((22,)),
            dma((22,)),
            dma((5,)),
            dma((5,)),
            dma,
            dma,
            dma,
            dma((sn,)),
            dma,
            dma((sn,)),
            dma((2, nx)),
            pltpu.SemaphoreType.REGULAR((max(1, (sn - 2).bit_length()),)),
        ],
        compiler_params=pltpu.CompilerParams(
            collective_id=0, has_side_effects=True, vmem_limit_bytes=56 * 2**20
        ),
        name="stokes",
    )(viscosity, forcing, owner)


def finish_body(base, second, small, vel, press, A, B, rsem, wsem):
    comps, nx, ny, nz = base.shape
    parts = [(c, p) for p in range(nx) for c in range(comps)]

    def reads(n):
        c, p = parts[n]
        return [
            pltpu.make_async_copy(src.at[c, p], dst.at[c, p], rsem.at[i, n])
            for i, (src, dst) in enumerate(((base, A), (second, B)))
        ]

    for n in range(len(parts)):
        for copy in reads(n):
            copy.start()
    alpha = small[2 * nx : 2 * nx + 1, 0:1]
    press[...] = small[0:nx, :] + alpha * small[nx : 2 * nx, :]
    writes = []
    for n, (c, p) in enumerate(parts):
        for copy in reads(n):
            copy.wait()
        A[c, p] = A[c, p] - alpha * B[c, p]
        copy = pltpu.make_async_copy(A.at[c, p], vel.at[c, p], wsem.at[n])
        copy.start()
        writes.append(copy)
    for copy in writes:
        copy.wait()


def finish(base, second, small):
    comps, nx, ny, nz = base.shape
    f32 = jnp.float32
    vmem = pl.BlockSpec(memory_space=pltpu.VMEM)
    anywhere = pl.BlockSpec(memory_space=pl.ANY)
    dma = pltpu.SemaphoreType.DMA
    return pl.pallas_call(
        finish_body,
        out_shape=(
            jax.ShapeDtypeStruct(base.shape, f32),
            jax.ShapeDtypeStruct((nx, small.shape[1]), f32),
        ),
        in_specs=[anywhere, anywhere, vmem],
        out_specs=(anywhere, vmem),
        scratch_shapes=[
            pltpu.VMEM(base.shape, f32),
            pltpu.VMEM(base.shape, f32),
            dma((2, comps * nx)),
            dma((comps * nx,)),
        ],
        compiler_params=pltpu.CompilerParams(vmem_limit_bytes=56 * 2**20),
        name="finish",
    )(base, second, small)


def shards(forcing, viscosity, owner_slot):
    sn, cn = lax.axis_size("slab"), lax.axis_size("cross")
    return finish(*stokes(forcing, viscosity, owner_slot.reshape(1, -1), sn, cn))


def solution(mesh):
    in_specs = (P(None, "slab", "cross", None), P("slab", "cross", None), P())
    out_specs = (P(None, "slab", "cross", None), P("slab", "cross"))
    return jax.shard_map(shards, mesh=mesh, in_specs=in_specs, out_specs=out_specs, check_vma=False)
```

```python
import functools

import jax
import jax.numpy as jnp
from jax import lax
from jax.experimental import pallas as pl
from jax.experimental.pallas import tpu as pltpu
from jax.sharding import PartitionSpec as P

MESH = pl.DeviceIdType.MESH

DEGREE = 3
LANES = 128
TILE = 8

cheb_theta = 1.025
cheb_delta = 0.975


def cheb_weights():
    sigma = cheb_theta / cheb_delta
    solved = [1.0 / cheb_theta] + [0.0] * (DEGREE - 1)
    change = list(solved)
    rho_prev = 1.0 / sigma
    for step in range(DEGREE - 1):
        resid = [(1.0 if k == 0 else solved[k - 1]) - solved[k] for k in range(DEGREE)]
        rho = 1.0 / (2.0 * sigma - rho_prev)
        change = [rho * rho_prev * c + 2.0 * rho / cheb_delta * r for c, r in zip(change, resid)]
        solved = [s + c for s, c in zip(solved, change)]
        rho_prev = rho
    return solved


NEAR = [(0, 0), (1, 0), (-1, 0), (0, 1), (0, -1)]
ALL = [(dx, dz) for dx in range(-2, 3) for dz in range(-2, 3) if abs(dx) + abs(dz) <= 2]


def chunks(cn, nz):
    n = min(cn, nz // LANES)
    return n, cn // n


def zshift(a, d):
    n = a.shape[-1]
    k = lax.broadcasted_iota(jnp.int32, a.shape, a.ndim - 1)
    keep = (k < n - d) if d > 0 else (k >= -d)
    return jnp.where(keep, pltpu.roll(a, (-d) % n, a.ndim - 1), 0.0)


def ring(a, d, axis):
    return a if d == 0 else pltpu.roll(a, (-d) % a.shape[axis], axis)


def rows(ref, lead, t, last):
    def tile(i):
        return ref[lead + (pl.ds(pl.multiple_of(i * TILE, TILE), TILE), slice(None))]

    cur = tile(t)
    row = lax.broadcasted_iota(jnp.int32, cur.shape, 0)
    up = pltpu.roll(jnp.where(row == 0, tile(jnp.minimum(t + 1, last)), cur), TILE - 1, 0)
    down = pltpu.roll(jnp.where(row == TILE - 1, tile(jnp.maximum(t - 1, 0)), cur), 1, 0)
    return cur, up, down


def stokes_body(
    sn, cn, visc, forc, owner, vel, press,
    V, F, ypk, fpk, YV, CV, YF, CF, DI, U, M, Y0, Z, BASE, FD,
    KF, CS, FRAME, KP, KR, EB, EBR, A1, A2, WIN, QS, KS, GSR, FULL,
    lsem, hs, hr, bs, br, ks, kr, as1, ar1, as2, ar2, hop,
):
    slab, cross = lax.axis_index("slab"), lax.axis_index("cross")
    nx, ny, nz = visc.shape
    nt = ny // TILE + 2
    ng, per = chunks(cn, nz)
    mine = cross // per
    f32 = jnp.float32
    w0, w1, w2 = [2.0 * w for w in cheb_weights()]

    def dev(s, c):
        return {"slab": s, "cross": c}

    def there(ds):
        return (slab + ds >= 0) & (slab + ds < sn)

    def others(dc):
        return lax.rem(cross + dc, cn)

    left, right = slab > 0, slab < sn - 1
    up, down = cross > 0, cross < cn - 1
    side, wall = (left, right), (up, down)
    own = pl.ds(TILE, ny)

    load_v = pltpu.make_async_copy(visc, V.at[pl.ds(3, nx), own], lsem.at[0])
    load_f = pltpu.make_async_copy(forc, F.at[:, pl.ds(2, nx), own], lsem.at[1])
    load_v.start()
    load_f.start()
    barrier = pltpu.get_barrier_semaphore()
    for ds in (0, 1, -1):
        for dc in range(cn):
            if ds == 0 and dc == 0:
                continue
            if ds == 0:
                pl.semaphore_signal(barrier, inc=1, device_id=dev(slab, others(dc)), device_id_type=MESH)
            else:

                @pl.when(there(ds))
                def _():
                    pl.semaphore_signal(barrier, inc=1, device_id=dev(slab + ds, others(dc)), device_id_type=MESH)

    zero_v = jnp.zeros((nx + 6, TILE, nz), f32)
    V[:, 0:TILE, :] = zero_v
    V[:, TILE + ny : 2 * TILE + ny, :] = zero_v
    zero_f = jnp.zeros((2, nx + 4, TILE, nz), f32)
    F[:, :, 0:TILE, :] = zero_f
    F[:, :, TILE + ny : 2 * TILE + ny, :] = zero_f
    for s in range(2):

        @pl.when(jnp.logical_not(side[s]))
        def _():
            v0, f0 = (0, 0) if s == 0 else (nx + 3, nx + 2)
            V[v0 : v0 + 3, TILE : TILE + ny, :] = jnp.zeros((3, ny, nz), f32)
            F[:, f0 : f0 + 2, TILE : TILE + ny, :] = jnp.zeros((2, 2, ny, nz), f32)

    count = (cn - 1) + cn * (jnp.where(left, 1, 0) + jnp.where(right, 1, 0))
    pl.semaphore_wait(barrier, count)

    steps = max(0, (sn - 2).bit_length())

    def greet(k):
        for d in (-(2**k), 2**k):

            @pl.when(there(d))
            def _():
                pl.semaphore_signal(hop.at[k], inc=1, device_id=dev(slab + d, cross), device_id_type=MESH)

    def greeted(k):
        pl.semaphore_wait(hop.at[k], jnp.where(there(-(2**k)), 1, 0) + jnp.where(there(2**k), 1, 0))

    def send(src, dst, out, into, s, c):
        return pltpu.make_async_remote_copy(
            src_ref=src, dst_ref=dst, send_sem=hs.at[out], recv_sem=hr.at[into], device_id=dev(s, c),
            device_id_type=MESH,
        )

    def vx(s, k):
        src = visc.at[k if s == 0 else nx - 1 - k]
        dst = V.at[nx + 3 + k if s == 0 else 2 - k, own]
        return send(src, dst, s * 3 + k, (1 - s) * 3 + k, slab + (2 * s - 1), cross)

    def vy(w):
        return send(ypk.at[w], YV.at[1 - w], 6 + w, 7 - w, slab, cross + (2 * w - 1))

    def vc(w, s):
        src = ypk.at[w, pl.ds(0 if s == 0 else nx - 2, 2)]
        return send(src, CV.at[1 - w, 1 - s], 8 + 2 * w + s, 8 + 2 * (1 - w) + 1 - s, slab + (2 * s - 1), cross + (2 * w - 1))

    def fx(s, k):
        src = forc.at[:, k if s == 0 else nx - 1 - k]
        dst = F.at[:, nx + 2 + k if s == 0 else 1 - k, own]
        return send(src, dst, 12 + 2 * s + k, 12 + 2 * (1 - s) + k, slab + (2 * s - 1), cross)

    def fy(w):
        return send(fpk.at[w], YF.at[1 - w], 16 + w, 17 - w, slab, cross + (2 * w - 1))

    def fc(w, s):
        src = fpk.at[w, :, pl.ds(0 if s == 0 else nx - 1, 1)]
        return send(src, CF.at[1 - w, 1 - s], 18 + 2 * w + s, 18 + 2 * (1 - w) + 1 - s, slab + (2 * s - 1), cross + (2 * w - 1))

    def landed(ref, into):
        pltpu.make_async_copy(ref, ref, hr.at[into]).wait()

    def when_all(conds, run):
        cond = conds[0]
        for c in conds[1:]:
            cond = cond & c
        pl.when(cond)(run)

    first = [([side[s]], functools.partial(vx, s, 0)) for s in range(2)]
    walls = [([wall[w]], functools.partial(vy, w)) for w in range(2)]
    corners = [([wall[w], side[s]], functools.partial(vc, w, s)) for w in range(2) for s in range(2)]
    later = [([side[s]], functools.partial(vx, s, k)) for k in (1, 2) for s in range(2)]
    forces = [([wall[w]], functools.partial(fy, w)) for w in range(2)]
    forces += [([wall[w], side[s]], functools.partial(fc, w, s)) for w in range(2) for s in range(2)]
    bulk = [([side[s]], functools.partial(fx, s, k)) for k in range(2) for s in range(2)]

    def begin(sends):
        for conds, make in sends:
            when_all(conds, lambda: make().start())

    begin(first)
    load_v.wait()
    ypk[0] = V[3 : 3 + nx, TILE : TILE + 4, :]
    ypk[1] = V[3 : 3 + nx, TILE + ny - 4 : TILE + ny, :]
    begin(walls + corners + later)
    load_f.wait()
    fpk[0] = F[:, 2 : 2 + nx, TILE : TILE + 2, :]
    fpk[1] = F[:, 2 : 2 + nx, TILE + ny - 2 : TILE + ny, :]
    begin(forces + bulk[:2])
    if steps > 0:
        greet(0)

    inner = nt - 2

    def sweep(lo, n, body, k=2):
        while n % k:
            k -= 1

        def step(i, _):
            for j in range(k):
                body(lo + i * k + j)
            return 0

        lax.fori_loop(0, n // k, step, 0)

    def tile(t):
        return pl.ds(t * TILE if isinstance(t, int) else pl.multiple_of(t * TILE, TILE), TILE)

    def inside(plane, t):
        ok = ((t > 0) | up) & ((t < nt - 1) | down)
        if plane < 0:
            ok = ok & left
        if plane >= nx:
            ok = ok & right
        return jnp.where(ok, 1.0, 0.0)

    def diagonal(planes, t):
        for p in planes:
            c, yp, ym = rows(V, (p + 3,), t, nt - 1)
            diag = V[p + 4, tile(t), :] + V[p + 2, tile(t), :] + yp + ym + zshift(c, 1) + zshift(c, -1) + 6.0 * c
            DI[p + 2, tile(t), :] = inside(p, t) * (1.0 / jnp.maximum(diag, 1e-30))

    def near(planes, comps, t):
        for p in planes:
            at = tile(t)
            v, vyp, vym = rows(V, (p + 3,), t, nt - 1)
            d, dyp, dym = rows(DI, (p + 2,), t, nt - 1)
            wd = w2 * d
            if 0 in comps:
                U[0, p + 1, at, :] = wd * ((v + vyp) * dyp + (v + vym) * dym) + w1 * d
            if 1 in comps:
                U[1, p + 1, at, :] = wd * ((v + V[p + 4, at, :]) * DI[p + 3, at, :])
            if 2 in comps:
                U[2, p + 1, at, :] = wd * ((v + V[p + 2, at, :]) * DI[p + 1, at, :])
            if 3 in comps:
                U[3, p + 1, at, :] = wd * ((v + zshift(v, 1)) * zshift(d, 1))
                U[4, p + 1, at, :] = wd * ((v + zshift(v, -1)) * zshift(d, -1))

    def coefficients(planes, t):
        for p in planes:
            at, to = tile(t), tile(t - 1)
            v, vyp, vym = rows(V, (p + 3,), t, nt - 1)
            d = DI[p + 2, at, :]
            yp, ym = d * (v + vyp), d * (v + vym)
            xp, xm = d * (v + V[p + 4, at, :]), d * (v + V[p + 2, at, :])
            zp, zm = d * (v + zshift(v, 1)), d * (v + zshift(v, -1))
            acc = {(0, 0): w0 * d}

            def add(o, a):
                acc[o] = acc[o] + a if o in acc else a

            for n, (dx, dz) in enumerate(NEAR):
                c, cu, cd = rows(U, (n, p + 1), t, nt - 1)
                add((dx, dz), yp * cu + ym * cd)
                if dx < 1:
                    add((dx + 1, dz), xp * U[n, p + 2, at, :])
                if dx > -1:
                    add((dx - 1, dz), xm * U[n, p, at, :])
                add((dx, dz + 1), zp * zshift(c, 1))
                add((dx, dz - 1), zm * zshift(c, -1))
            for o in acc:
                M[ALL.index(o), p, to, :] = acc[o]

    def far(pairs, t):
        for p, d in pairs:
            at = tile(t)
            v0, v1, v2 = [V[p + 3 + d * k, at, :] for k in range(3)]
            d0, d1, d2 = [DI[p + 2 + d * k, at, :] for k in range(3)]
            M[ALL.index((2 * d, 0)), p, tile(t - 1), :] = w2 * (d0 * (v0 + v1)) * (d1 * (v1 + v2)) * d2

    prow = lax.broadcasted_iota(jnp.int32, (nx, nz), 0)
    KF[...] = jnp.zeros_like(KF)
    CS[...] = jnp.zeros_like(CS)

    def sums(p, offsets):
        for o in offsets:
            n = ALL.index(o)
            acc = None
            for t in range(inner):
                m = M[n, p, tile(t), :]
                new = (m, m * F[0, p + 2, tile(t + 1), :], m * F[1, p + 2, tile(t + 1), :])
                acc = new if acc is None else [a + b for a, b in zip(acc, new)]
            here = prow == p
            for ref, a in zip((KF.at[n], CS.at[n, 0], CS.at[n, 1]), acc):
                ref[...] = jnp.where(here, jnp.sum(a, axis=0, keepdims=True), ref[...])

    short = [o for o in ALL if abs(o[0]) < 2]
    mids, ends = list(range(1, nx - 1)), [0, nx - 1]

    def plane_sums(first, stride, n):
        def step(i, _):
            sums(first + i * stride, short)
            return 0

        lax.fori_loop(0, n, step, 0)

    sweep(2, inner - 2, lambda t: diagonal(mids, t))
    for s in range(2):
        when_all([side[s]], lambda: landed(V.at[nx + 3 if s == 1 else 2, own], s * 3))
    for w in range(2):

        def put():
            landed(YV.at[w], 6 + w)
            r0 = 4 if w == 0 else TILE + ny
            V[3 : 3 + nx, r0 : r0 + 4, :] = YV[w]

        when_all([wall[w]], put)
    for t in (0, 1, nt - 2, nt - 1):
        diagonal(mids, t)
    sweep(1, inner, lambda t: diagonal(ends, t))
    for w in range(2):
        for s in range(2):

            def put():
                landed(CV.at[w, s], 8 + 2 * w + s)
                r0 = 4 if w == 0 else TILE + ny
                p0 = 1 if s == 0 else nx + 3
                V[p0 : p0 + 2, r0 : r0 + 4, :] = CV[w, s]

            when_all([wall[w], side[s]], put)
    for t in (0, nt - 1):
        diagonal(ends, t)
    sweep(0, nt, lambda t: near(mids, (0, 1, 2, 3), t))
    sweep(0, nt, lambda t: (near([0], (0, 1, 3), t), near([nx - 1], (0, 2, 3), t)))
    sweep(1, inner, lambda t: coefficients(mids, t), 1)
    plane_sums(1, 1, nx - 2)
    for s in range(2):
        when_all([side[s]], lambda: landed(V.at[nx + 4 if s == 1 else 1, own], s * 3 + 1))
    sweep(0, nt, lambda t: diagonal([-1, nx], t))
    sweep(0, nt, lambda t: (near([-1], (0, 1, 3), t), near([nx], (0, 2, 3), t), near([0], (2,), t), near([nx - 1], (1,), t)))
    sweep(1, inner, lambda t: coefficients(ends, t), 1)
    plane_sums(0, nx - 1, 2)
    ready = [(p, d) for p in range(nx) for d in (1, -1) if 0 <= p + d < nx]
    sweep(1, inner, lambda t: far(ready, t), 1)
    for p, d in ready:
        sums(p, [(2 * d, 0)])
    for s in range(2):
        when_all([side[s]], lambda: landed(V.at[nx + 5 if s == 1 else 0, own], s * 3 + 2))
    sweep(1, inner, lambda t: diagonal([-2, nx + 1], t))
    sweep(1, inner, lambda t: far([(0, -1), (nx - 1, 1)], t))
    sums(0, [(-2, 0)])
    sums(nx - 1, [(2, 0)])

    FRAME[...] = jnp.zeros_like(FRAME)
    for c in range(2):
        for dx in range(-2, 3):
            total = None
            for n, o in enumerate(ALL):
                if o[0] == dx:
                    a = CS[n, c]
                    a = a if o[1] == 0 else zshift(a, -o[1])
                    total = a if total is None else total + a
            FRAME[c, nx + dx : 2 * nx + dx, :] += total
    cx, cz = FRAME[0], FRAME[1]
    e = cx - pltpu.roll(cx, 1, 0) + cz - zshift(cz, -1)
    WIN[:, 0:LANES] = jnp.zeros((4 * nx, LANES), f32)
    WIN[:, LANES + nz :] = jnp.zeros((4 * nx, LANES), f32)
    WIN[:, LANES : LANES + nz] = e

    def wide(get, g):
        main, before, after = get(g + 1), get(g), get(g + 2)
        lane = lax.broadcasted_iota(jnp.int32, main.shape, 1)
        return main, jnp.where(lane < LANES // 2, after, before)

    for g in range(ng):
        main, halo = wide(lambda i: WIN[:, i * LANES : (i + 1) * LANES], g)
        for b in range(3):
            EB[g, b, :, 0:LANES] = main[b * nx : (b + 1) * nx]
            EB[g, b, :, LANES : 2 * LANES] = halo[b * nx : (b + 1) * nx]
        for n in range(len(ALL)):
            KP[g, n] = KF[n, :, g * LANES : (g + 1) * LANES]

    if steps > 0:
        greeted(0)
        if steps > 1:
            greet(1)

    def span(ds):
        return pl.ds(max(0, ds), 3 - abs(ds))

    def e_copy(ds, dc):
        return pltpu.make_async_remote_copy(
            src_ref=EB.at[others(dc) // per, span(ds)], dst_ref=EBR.at[2 - ds, cross, span(ds)],
            send_sem=bs.at[ds + 2], recv_sem=br.at[2 - ds], device_id=dev(slab + ds, others(dc)), device_id_type=MESH,
        )

    for ds in (0, 1, -1, 2, -2):

        def start():
            for dc in range(1 if ds == 0 else 0, cn):
                e_copy(ds, dc).start()

        when_all([there(ds)], start)
    for dc in range(1, cn):
        pltpu.make_async_remote_copy(
            src_ref=KP.at[others(dc) // per], dst_ref=KR.at[cross], send_sem=ks, recv_sem=kr,
            device_id=dev(slab, others(dc)), device_id_type=MESH,
        ).start()
    for b in range(3):
        EBR[2, cross, b] = EB[mine, b]
    KR[cross] = KP[mine]

    begin(bulk[2:])

    def forced(k):
        for s in range(2):
            when_all([side[s]], lambda: landed(F.at[:, nx + 2 + k if s == 1 else 1 - k, own], 12 + 2 * s + k))

    forced(0)
    for w in range(2):

        def put():
            landed(YF.at[w], 16 + w)
            r0 = TILE - 2 if w == 0 else TILE + ny
            F[:, 2 : 2 + nx, r0 : r0 + 2, :] = YF[w]

        when_all([wall[w]], put)
        for s in range(2):

            def put():
                landed(CF.at[w, s], 18 + 2 * w + s)
                r0 = TILE - 2 if w == 0 else TILE + ny
                p0 = 1 if s == 0 else nx + 2
                F[:, p0 : p0 + 1, r0 : r0 + 2, :] = CF[w, s]

            when_all([wall[w], side[s]], put)

    def scaled(planes, t):
        for p in planes:
            d = DI[p, tile(t), :]
            for c in range(2):
                Y0[c, p, tile(t), :] = d * F[c, p, tile(t), :]

    def faces(p, t):
        at = tile(t)
        v, vyp, vym = rows(V, (p + 3,), t, nt - 1)
        d = DI[p + 2, at, :]
        return (
            d * (v + vyp), d * (v + vym), d * (v + V[p + 4, at, :]), d * (v + V[p + 2, at, :]),
            d * (v + zshift(v, 1)), d * (v + zshift(v, -1)),
        )

    def carried(field, c, p, t, face):
        yp, ym, xp, xm, zp, zm = face
        a, au, ad = rows(field, (c, p), t, nt - 1)
        near_by = yp * au + ym * ad + xp * field[c, p + 1, tile(t), :] + xm * field[c, p - 1, tile(t), :]
        return a, near_by + zp * zshift(a, 1) + zm * zshift(a, -1)

    def once(planes, t):
        for p in planes:
            face = faces(p, t)
            for c in range(2):
                a, t1 = carried(Y0, c, p + 2, t, face)
                Z[c, p + 1, tile(t), :] = w1 * a + w2 * t1

    def twice(planes, t):
        for p in planes:
            face = faces(p, t)
            for c in range(2):
                a, t2 = carried(Z, c, p + 1, t, face)
                BASE[c, p, tile(t - 1), :] = w0 * Y0[c, p + 2, tile(t), :] + t2

    sweep(0, nt, lambda t: scaled(range(1, nx + 3), t))
    sweep(0, nt, lambda t: once(range(nx), t), 1)
    sweep(1, inner, lambda t: twice(mids, t), 1)

    e_mine = cn - 1
    for ds in range(-2, 3):
        src = -ds

        def wait():
            n = cn - 1 if ds == 0 else cn
            ref = EBR.at[2 + src, pl.ds(0, n), span(ds)]
            pltpu.make_async_copy(ref, ref, br.at[2 + src]).wait()

        when_all([there(src)], wait)
    pltpu.make_async_copy(KR.at[pl.ds(0, e_mine)], KR.at[pl.ds(0, e_mine)], kr).wait()
    WINB = WIN.at[:, 0 : 2 * LANES]
    WINB[3 * nx :, :] = jnp.zeros((nx, 2 * LANES), f32)
    for t in range(-1, 2):
        WINB[(t + 1) * nx : (t + 2) * nx, :] = jnp.zeros((nx, 2 * LANES), f32)

        def gather():
            for b in range(-1, 2):
                src = t - b

                def take():
                    total = EBR[2 + src, 0, b + 1]
                    for c in range(1, cn):
                        total = total + EBR[2 + src, c, b + 1]
                    WINB[(t + 1) * nx : (t + 2) * nx, :] += total

                when_all([there(src)], take)

        when_all([there(t)], gather)
    for n in range(len(ALL)):
        total = KR[0, n]
        for c in range(1, cn):
            total = total + KR[c, n]
        KS[n] = total

    def columns(q):
        for c, grad in enumerate((q - ring(q, 1, 0), q - ring(q, 1, 1))):
            for dz in range(-2, 3):
                QS[dz + 2, c] = ring(grad, dz, 1)[:, 0:LANES]
        out = []
        for c in range(2):
            total = None
            for n, (dx, dz) in enumerate(ALL):
                a = KS[n] * QS[dz + 2, c, nx + dx : 2 * nx + dx, :]
                total = a if total is None else total + a
            out.append(total)
        return out

    q = WINB[...]
    c1 = columns(q)
    me = slab * ng + mine
    A1[me, 0] = q[nx : 2 * nx, 0:LANES]
    A1[me, 1] = c1[0]
    A1[me, 2] = c1[1]
    for k in range(1, steps):
        greeted(k)
        if k + 1 < steps:
            greet(k + 1)

    def share(buf, ssem, rsem):
        order = [0, 1, sn - 1] + list(range(2, sn - 1))
        for ds in list(dict.fromkeys(d % sn for d in order)):
            for dg in range(ng):
                if ds == 0 and dg == 0:
                    continue
                to = lax.rem(mine + dg, ng) * per + lax.rem(cross, per)
                pltpu.make_async_remote_copy(
                    src_ref=buf.at[me], dst_ref=buf.at[me], send_sem=ssem, recv_sem=rsem.at[slab],
                    device_id=dev(lax.rem(slab + ds, sn), to), device_id_type=MESH,
                ).start()

    def shared(buf, rsem, s, n):
        ref = buf.at[pl.ds(0, n)]
        pltpu.make_async_copy(ref, ref, rsem.at[s]).wait()

    share(A1, as1, ar1)
    forced(1)
    sweep(0, nt, lambda t: scaled([0, nx + 3], t))
    sweep(0, nt, lambda t: once([-1, nx], t), 1)
    sweep(1, inner, lambda t: twice(ends, t), 1)

    if ng > 1:
        shared(A1, ar1, slab, ng - 1)
    for ds in (-1, 1):
        when_all([there(ds)], lambda: shared(A1, ar1, slab + ds, ng))
    FRAME[...] = jnp.zeros_like(FRAME)
    for t in range(-1, 2):

        def fill():
            for g in range(ng):
                for a in range(3):
                    FRAME[a, (t + 1) * nx : (t + 2) * nx, g * LANES : (g + 1) * LANES] = A1[(slab + t) * ng + g, a]

        when_all([there(t)], fill)
    gwin = FRAME[0]
    cx, cz = FRAME[1], FRAME[2]
    sg = cx - pltpu.roll(cx, 1, 0) + cz - zshift(cz, -1)
    trow = lax.broadcasted_iota(jnp.int32, sg.shape, 0)
    known = (trow < 3 * nx) & ((trow < 2 * nx) | right) & ((trow >= nx) | left)
    sg = jnp.where(known, sg, 0.0)
    WIN[:, 0:LANES] = jnp.zeros((4 * nx, LANES), f32)
    WIN[:, LANES + nz :] = jnp.zeros((4 * nx, LANES), f32)
    WIN[:, LANES : LANES + nz] = sg
    main, halo = wide(lambda i: WIN[:, pl.ds(pl.multiple_of(i * LANES, LANES), LANES)], mine)
    c2 = columns(jnp.concatenate([main, halo], 1))
    A2[me, 0] = c2[0]
    A2[me, 1] = c2[1]
    share(A2, as2, ar2)

    for i, q in enumerate((gwin, sg)):
        for c, grad in enumerate((q - ring(q, 1, 0), q - zshift(q, 1))):
            for dz in range(-2, 3):
                a = grad if dz == 0 else zshift(grad, dz)
                for r in range(nx - 2, 2 * nx + 2):
                    GSR[i, dz + 2, c, r] = a[r : r + 1]

    def apply(i, _):
        p, t = i // inner, i % inner
        at = tile(t)
        total = [[None, None], [None, None]]
        for n, (dx, dz) in enumerate(ALL):
            m = M[n, p, at, :]
            for j in range(2):
                for c in range(2):
                    a = m * GSR[j, dz + 2, c, p + nx + dx]
                    total[j][c] = a if total[j][c] is None else total[j][c] + a
        for j in range(2):
            for c in range(2):
                FD[j, c, p, at, :] = total[j][c]
        return 0

    lax.fori_loop(0, nx * inner, apply, 0)

    width = nz // cn
    slot = lax.broadcasted_iota(jnp.int32, (width, nz), 0) + cross * width
    onehot = (jnp.broadcast_to(owner[...], (width, nz)) == slot).astype(f32).astype(jnp.bfloat16)
    rest = jnp.concatenate([gwin[nx : 2 * nx], sg[nx : 2 * nx]], 0)
    ordered = jnp.zeros((2 * nx, width), f32)
    for _ in range(3):
        piece = rest.astype(jnp.bfloat16)
        rest = rest - piece.astype(f32)
        ordered = ordered + lax.dot_general(
            piece, onehot, (((1,), (1,)), ((), ())), preferred_element_type=f32
        )

    for ds in range(2, sn - 1):
        s = lax.rem(slab + ds, sn)
        shared(A1, ar1, s, ng)
    for ds in (1, -1):
        when_all([jnp.logical_not(there(ds))], lambda: shared(A1, ar1, lax.rem(slab + ds + sn, sn), ng))

    def whole(buf, a, into):
        for s in range(sn):
            for g in range(ng):
                FULL[into, s * nx : (s + 1) * nx, g * LANES : (g + 1) * LANES] = buf[s * ng + g, a]

    def below(a):
        row = lax.broadcasted_iota(jnp.int32, a.shape, 0)
        return jnp.where(row == 0, 0.0, pltpu.roll(a, 1, 0))

    for a in range(3):
        whole(A1, a, a)
    g = FULL[0]
    s1 = FULL[1] - below(FULL[1]) + FULL[2] - zshift(FULL[2], -1)
    rr = jnp.sum(g * g)
    alpha0 = rr / jnp.sum(g * s1)
    resid = g - alpha0 * s1
    fresh = jnp.sum(resid * resid)
    beta = fresh / rr
    dirn = resid + beta * g
    FULL[3] = s1
    FULL[4] = dirn

    def combine(t):
        for p in range(nx):
            for c in range(2):
                a, b = FD[0, c, p, tile(t), :], FD[1, c, p, tile(t), :]
                BASE[c, p, tile(t), :] = BASE[c, p, tile(t), :] - alpha0 * a
                FD[0, c, p, tile(t), :] = a - alpha0 * b + beta * a

    sweep(0, inner, combine)
    pg, ps = ordered[:nx], ordered[nx:]

    if ng > 1:
        shared(A2, ar2, slab, ng - 1)
    for ds in range(1, sn):
        shared(A2, ar2, lax.rem(slab + ds, sn), ng)
    for a in range(2):
        whole(A2, a, a)
    s2 = FULL[0] - below(FULL[0]) + FULL[1] - zshift(FULL[1], -1)
    s1 = FULL[3]
    image = s1 - alpha0 * s2 + beta * s1
    alpha1 = fresh / jnp.sum(FULL[4] * image)
    press[...] = alpha0 * pg + alpha1 * (pg - alpha0 * ps + beta * pg)

    def finish(t):
        for p in range(nx):
            for c in range(2):
                vel[c, p, tile(t), :] = BASE[c, p, tile(t), :] - alpha1 * FD[0, c, p, tile(t), :]

    sweep(0, inner, finish)

    for conds, make in first + walls + corners + later + forces + bulk:
        when_all(conds, lambda: make().wait_send())
    for ds in range(-2, 3):

        def left_here():
            ref = EBR.at[2 - ds, pl.ds(0, cn - 1 if ds == 0 else cn), span(ds)]
            pltpu.make_async_copy(ref, ref, bs.at[ds + 2]).wait()

        when_all([there(ds)], left_here)
    pltpu.make_async_copy(KR.at[pl.ds(0, cn - 1)], KR.at[pl.ds(0, cn - 1)], ks).wait()
    for buf, sem in ((A1, as1), (A2, as2)):
        ref = buf.at[pl.ds(0, sn * ng - 1)]
        pltpu.make_async_copy(ref, ref, sem).wait()


def stokes(forcing, viscosity, owner, sn, cn):
    nx, ny, nz = viscosity.shape
    f32 = jnp.float32
    ng, _ = chunks(cn, nz)
    no = len(ALL)
    ye = ny + 2 * TILE
    vmem = pl.BlockSpec(memory_space=pltpu.VMEM)
    anywhere = pl.BlockSpec(memory_space=pl.ANY)
    dma = pltpu.SemaphoreType.DMA

    def buf(*shape):
        return pltpu.VMEM(shape, f32)

    return pl.pallas_call(
        functools.partial(stokes_body, sn, cn),
        out_shape=(
            pltpu.VMEM(forcing.shape, f32),
            pltpu.VMEM((nx, nz // cn), f32),
        ),
        in_specs=[anywhere, anywhere, vmem],
        out_specs=(vmem, vmem),
        scratch_shapes=[
            buf(nx + 6, ye, nz),
            buf(2, nx + 4, ye, nz),
            buf(2, nx, 4, nz),
            buf(2, 2, nx, 2, nz),
            buf(2, nx, 4, nz),
            buf(2, 2, 2, 4, nz),
            buf(2, 2, nx, 2, nz),
            buf(2, 2, 2, 1, 2, nz),
            buf(nx + 4, ye, nz),
            buf(5, nx + 2, ye, nz),
            buf(no, nx, ny, nz),
            buf(2, nx + 4, ye, nz),
            buf(2, nx + 2, ye, nz),
            buf(2, nx, ny, nz),
            buf(2, 2, nx, ny, nz),
            buf(no, nx, nz),
            buf(no, 2, nx, nz),
            buf(3, 4 * nx, nz),
            buf(ng, no, nx, LANES),
            buf(cn, no, nx, LANES),
            buf(ng, 3, nx, 2 * LANES),
            buf(5, cn, 3, nx, 2 * LANES),
            buf(sn * ng, 3, nx, LANES),
            buf(sn * ng, 2, nx, LANES),
            buf(4 * nx, nz + 2 * LANES),
            buf(5, 2, 4 * nx, LANES),
            buf(no, nx, LANES),
            buf(2, 5, 2, 4 * nx, 1, nz),
            buf(5, sn * nx, nz),
            dma((2,)),
            dma((22,)),
            dma((22,)),
            dma((5,)),
            dma((5,)),
            dma,
            dma,
            dma,
            dma((sn,)),
            dma,
            dma((sn,)),
            pltpu.SemaphoreType.REGULAR((max(1, (sn - 2).bit_length()),)),
        ],
        compiler_params=pltpu.CompilerParams(
            collective_id=0, has_side_effects=True, vmem_limit_bytes=56 * 2**20
        ),
        name="stokes",
    )(viscosity, forcing, owner)


def shards(forcing, viscosity, owner_slot):
    sn, cn = lax.axis_size("slab"), lax.axis_size("cross")
    return stokes(forcing, viscosity, owner_slot.reshape(1, -1), sn, cn)


def solution(mesh):
    in_specs = (P(None, "slab", "cross", None), P("slab", "cross", None), P())
    out_specs = (P(None, "slab", "cross", None), P("slab", "cross"))
    return jax.shard_map(shards, mesh=mesh, in_specs=in_specs, out_specs=out_specs, check_vma=False)
```

```python
import functools

import jax
import jax.numpy as jnp
from jax import lax
from jax.experimental import pallas as pl
from jax.experimental.pallas import tpu as pltpu
from jax.sharding import PartitionSpec as P

MESH = pl.DeviceIdType.MESH

DEGREE = 3
LANES = 128
TILE = 8

cheb_theta = 1.025
cheb_delta = 0.975


def cheb_weights():
    sigma = cheb_theta / cheb_delta
    solved = [1.0 / cheb_theta] + [0.0] * (DEGREE - 1)
    change = list(solved)
    rho_prev = 1.0 / sigma
    for step in range(DEGREE - 1):
        resid = [(1.0 if k == 0 else solved[k - 1]) - solved[k] for k in range(DEGREE)]
        rho = 1.0 / (2.0 * sigma - rho_prev)
        change = [rho * rho_prev * c + 2.0 * rho / cheb_delta * r for c, r in zip(change, resid)]
        solved = [s + c for s, c in zip(solved, change)]
        rho_prev = rho
    return solved


SHORT = [(dx, dz) for dx in range(-1, 2) for dz in range(-2, 3) if abs(dx) + abs(dz) <= 2]
ALL = SHORT + [(-2, 0), (2, 0)]


def chunks(cn, nz):
    n = min(cn, nz // LANES)
    return n, cn // n


def zshift(a, d):
    n = a.shape[-1]
    k = lax.broadcasted_iota(jnp.int32, a.shape, a.ndim - 1)
    keep = (k < n - d) if d > 0 else (k >= -d)
    return jnp.where(keep, pltpu.roll(a, (-d) % n, a.ndim - 1), 0.0)


def ring(a, d, axis):
    return a if d == 0 else pltpu.roll(a, (-d) % a.shape[axis], axis)


def rows(ref, lead, t, last):
    def tile(i):
        return ref[lead + (pl.ds(pl.multiple_of(i * TILE, TILE), TILE), slice(None))]

    cur = tile(t)
    row = lax.broadcasted_iota(jnp.int32, cur.shape, 0)
    up = pltpu.roll(jnp.where(row == 0, tile(jnp.minimum(t + 1, last)), cur), TILE - 1, 0)
    down = pltpu.roll(jnp.where(row == TILE - 1, tile(jnp.maximum(t - 1, 0)), cur), 1, 0)
    return cur, up, down


def stokes_body(
    sn, cn, visc, forc, owner, vel, press,
    V, F, ypk, fpk, YV, CV, YF, CF, ZF, DI, U, M, Y0, Z, BASE, FD,
    KF, CS, FRAME, KP, KR, EB, EBR, A1, A2, WIN, QS, KS, GSR, FULL,
    lsem, hs, hr, bs, br, ks, kr, as1, ar1, as2, ar2, hop,
):
    slab, cross = lax.axis_index("slab"), lax.axis_index("cross")
    nx, ny, nz = visc.shape
    nt = ny // TILE + 2
    ng, per = chunks(cn, nz)
    mine = cross // per
    f32 = jnp.float32
    w0, w1, w2 = [2.0 * w for w in cheb_weights()]

    def dev(s, c):
        return {"slab": s, "cross": c}

    def there(ds):
        return (slab + ds >= 0) & (slab + ds < sn)

    def others(dc):
        return lax.rem(cross + dc, cn)

    left, right = slab > 0, slab < sn - 1
    up, down = cross > 0, cross < cn - 1
    side, wall = (left, right), (up, down)
    own = pl.ds(TILE, ny)

    load_v = pltpu.make_async_copy(visc, V.at[pl.ds(3, nx), own], lsem.at[0])
    load_f = pltpu.make_async_copy(forc, F.at[:, pl.ds(2, nx), own], lsem.at[1])
    load_v.start()
    load_f.start()
    barrier = pltpu.get_barrier_semaphore()
    for ds in (0, 1, -1):
        for dc in range(cn):
            if ds == 0 and dc == 0:
                continue
            if ds == 0:
                pl.semaphore_signal(barrier, inc=1, device_id=dev(slab, others(dc)), device_id_type=MESH)
            else:

                @pl.when(there(ds))
                def _():
                    pl.semaphore_signal(barrier, inc=1, device_id=dev(slab + ds, others(dc)), device_id_type=MESH)

    zero_v = jnp.zeros((nx + 6, TILE, nz), f32)
    V[:, 0:TILE, :] = zero_v
    V[:, TILE + ny : 2 * TILE + ny, :] = zero_v
    zero_f = jnp.zeros((2, nx + 4, TILE, nz), f32)
    F[:, :, 0:TILE, :] = zero_f
    F[:, :, TILE + ny : 2 * TILE + ny, :] = zero_f
    for s in range(2):

        @pl.when(jnp.logical_not(side[s]))
        def _():
            v0, f0 = (0, 0) if s == 0 else (nx + 3, nx + 2)
            V[v0 : v0 + 3, TILE : TILE + ny, :] = jnp.zeros((3, ny, nz), f32)
            F[:, f0 : f0 + 2, TILE : TILE + ny, :] = jnp.zeros((2, 2, ny, nz), f32)

    count = (cn - 1) + cn * (jnp.where(left, 1, 0) + jnp.where(right, 1, 0))
    pl.semaphore_wait(barrier, count)

    steps = max(0, (sn - 2).bit_length())

    def greet(k):
        for d in (-(2**k), 2**k):

            @pl.when(there(d))
            def _():
                pl.semaphore_signal(hop.at[k], inc=1, device_id=dev(slab + d, cross), device_id_type=MESH)

    def greeted(k):
        pl.semaphore_wait(hop.at[k], jnp.where(there(-(2**k)), 1, 0) + jnp.where(there(2**k), 1, 0))

    def send(src, dst, out, into, s, c):
        return pltpu.make_async_remote_copy(
            src_ref=src, dst_ref=dst, send_sem=hs.at[out], recv_sem=hr.at[into], device_id=dev(s, c),
            device_id_type=MESH,
        )

    def vx(s, k):
        src = visc.at[k if s == 0 else nx - 1 - k]
        dst = V.at[nx + 3 + k if s == 0 else 2 - k, own]
        return send(src, dst, s * 3 + k, (1 - s) * 3 + k, slab + (2 * s - 1), cross)

    def vy(w):
        return send(ypk.at[w], YV.at[1 - w], 6 + w, 7 - w, slab, cross + (2 * w - 1))

    def vc(w, s):
        src = ypk.at[w, pl.ds(0 if s == 0 else nx - 2, 2)]
        return send(src, CV.at[1 - w, 1 - s], 8 + 2 * w + s, 8 + 2 * (1 - w) + 1 - s, slab + (2 * s - 1), cross + (2 * w - 1))

    def fx(s, k):
        src = forc.at[:, k if s == 0 else nx - 1 - k]
        dst = F.at[:, nx + 2 + k if s == 0 else 1 - k, own]
        return send(src, dst, 12 + 2 * s + k, 12 + 2 * (1 - s) + k, slab + (2 * s - 1), cross)

    def fy(w):
        return send(fpk.at[w], YF.at[1 - w], 16 + w, 17 - w, slab, cross + (2 * w - 1))

    def fc(w, s):
        src = fpk.at[w, :, pl.ds(0 if s == 0 else nx - 1, 1)]
        return send(src, CF.at[1 - w, 1 - s], 18 + 2 * w + s, 18 + 2 * (1 - w) + 1 - s, slab + (2 * s - 1), cross + (2 * w - 1))

    def landed(ref, into):
        pltpu.make_async_copy(ref, ref, hr.at[into]).wait()

    def when_all(conds, run):
        cond = conds[0]
        for c in conds[1:]:
            cond = cond & c
        pl.when(cond)(run)

    first = [([side[s]], functools.partial(vx, s, 0)) for s in range(2)]
    walls = [([wall[w]], functools.partial(vy, w)) for w in range(2)]
    corners = [([wall[w], side[s]], functools.partial(vc, w, s)) for w in range(2) for s in range(2)]
    later = [([side[s]], functools.partial(vx, s, k)) for k in (1, 2) for s in range(2)]
    forces = [([wall[w]], functools.partial(fy, w)) for w in range(2)]
    forces += [([wall[w], side[s]], functools.partial(fc, w, s)) for w in range(2) for s in range(2)]
    bulk = [([side[s]], functools.partial(fx, s, k)) for k in range(2) for s in range(2)]

    def begin(sends):
        for conds, make in sends:
            when_all(conds, lambda: make().start())

    begin(first)
    load_v.wait()
    ypk[0] = V[3 : 3 + nx, TILE : TILE + 4, :]
    ypk[1] = V[3 : 3 + nx, TILE + ny - 4 : TILE + ny, :]
    begin(walls + corners + later)
    load_f.wait()
    fpk[0] = F[:, 2 : 2 + nx, TILE : TILE + 2, :]
    fpk[1] = F[:, 2 : 2 + nx, TILE + ny - 2 : TILE + ny, :]
    begin(forces + bulk[:2])
    if steps > 0:
        greet(0)

    inner = nt - 2

    def sweep(lo, n, body, k=5):
        while n % k:
            k -= 1

        def step(i, _):
            for j in range(k):
                body(lo + i * k + j)
            return 0

        lax.fori_loop(0, n // k, step, 0)

    def tile(t):
        return pl.ds(t * TILE if isinstance(t, int) else pl.multiple_of(t * TILE, TILE), TILE)

    def inside(plane, t):
        ok = ((t > 0) | up) & ((t < nt - 1) | down)
        if plane < 0:
            ok = ok & left
        if plane >= nx:
            ok = ok & right
        return jnp.where(ok, 1.0, 0.0)

    def zsides(v):
        return v + zshift(v, 1), v + zshift(v, -1)

    def zfaces(planes, t):
        for p in planes:
            ZF[0, p + 2, tile(t), :], ZF[1, p + 2, tile(t), :] = zsides(V[p + 3, tile(t), :])

    def diagonal(planes, t):
        for p in planes:
            c, yp, ym = rows(V, (p + 3,), t, nt - 1)
            zp, zm = zsides(c) if p < -1 or p > nx else (ZF[0, p + 2, tile(t), :], ZF[1, p + 2, tile(t), :])
            diag = V[p + 4, tile(t), :] + V[p + 2, tile(t), :] + yp + ym + zp + zm + 4.0 * c
            DI[p + 2, tile(t), :] = inside(p, t) * (1.0 / jnp.maximum(diag, 1e-30))

    def near(planes, comps, t):
        for p in planes:
            at = tile(t)
            d = DI[p + 2, at, :]
            wd = w2 * d
            if 0 in comps:
                v, vyp, vym = rows(V, (p + 3,), t, nt - 1)
                _, dyp, dym = rows(DI, (p + 2,), t, nt - 1)
                U[0, p + 1, at, :] = wd * ((v + vyp) * dyp + (v + vym) * dym) + w1 * d
            if 1 in comps:
                a = wd * ((V[p + 3, at, :] + V[p + 4, at, :]) * DI[p + 3, at, :])
                U[1, p + 1, at, :] = a
                U[2, p + 1, at, :] = zshift(a, 1)
                U[5, p + 1, at, :] = zshift(a, -1)
            if 3 in comps:
                U[3, p + 1, at, :] = wd * (ZF[0, p + 2, at, :] * zshift(d, 1))
                U[4, p + 1, at, :] = wd * (ZF[1, p + 2, at, :] * zshift(d, -1))

    def coefficients(planes, t):
        for p in planes:
            at, to = tile(t), tile(t - 1)
            v, vyp, vym = rows(V, (p + 3,), t, nt - 1)
            d = DI[p + 2, at, :]
            yp, ym = d * (v + vyp), d * (v + vym)
            xp, xm = d * (v + V[p + 4, at, :]), d * (v + V[p + 2, at, :])
            zp, zm = d * ZF[0, p + 2, at, :], d * ZF[1, p + 2, at, :]

            def put(o, a):
                M[ALL.index(o), p, to, :] = a

            def along(n, plane):
                a, au, ad = rows(U, (n, plane + 1), t, nt - 1)
                return a, yp * au + ym * ad

            def at_plane(n, plane):
                return U[n, plane + 1, at, :]

            u0, y0 = along(0, p)
            u1, y1 = along(1, p)
            b1, y2 = along(1, p - 1)
            u3, y3 = along(3, p)
            u4, y4 = along(4, p)
            put((0, 0), w0 * d + y0 + xp * u1 + xm * b1 + zp * u3 + zm * u4)
            put((1, 0), y1 + xp * at_plane(0, p + 1))
            put((-1, 0), y2 + xm * at_plane(0, p - 1))
            put((0, 1), y3 + zp * zshift(u0, 1))
            put((0, -1), y4 + zm * zshift(u0, -1))
            put((1, 1), xp * at_plane(3, p + 1) + zp * at_plane(2, p))
            put((1, -1), xp * at_plane(4, p + 1) + zm * at_plane(5, p))
            put((-1, 1), xm * at_plane(3, p - 1) + zp * at_plane(2, p - 1))
            put((-1, -1), xm * at_plane(4, p - 1) + zm * at_plane(5, p - 1))
            put((0, 2), zp * zshift(u3, 1))
            put((0, -2), zm * zshift(u4, -1))

    def far(pairs, t):
        for p, d in pairs:
            at = tile(t)
            v0, v1, v2 = [V[p + 3 + d * k, at, :] for k in range(3)]
            d0, d1, d2 = [DI[p + 2 + d * k, at, :] for k in range(3)]
            M[ALL.index((2 * d, 0)), p, tile(t - 1), :] = w2 * (d0 * (v0 + v1)) * (d1 * (v1 + v2)) * d2

    prow = lax.broadcasted_iota(jnp.int32, (nx, nz), 0)
    KF[...] = jnp.zeros_like(KF)
    CS[...] = jnp.zeros_like(CS)

    def sums(p, offsets):
        for o in offsets:
            n = ALL.index(o)
            acc = None
            for t in range(inner):
                m = M[n, p, tile(t), :]
                new = (m, m * F[0, p + 2, tile(t + 1), :], m * F[1, p + 2, tile(t + 1), :])
                acc = new if acc is None else [a + b for a, b in zip(acc, new)]
            here = prow == p
            for ref, a in zip((KF.at[n], CS.at[n, 0], CS.at[n, 1]), acc):
                for shift in (4, 2, 1):
                    a = a + pltpu.roll(a, shift, 0)
                ref[...] = jnp.where(here, a[0:nx], ref[...])

    mids, ends = list(range(1, nx - 1)), [0, nx - 1]

    def plane_sums(first, stride, n):
        def step(i, _):
            sums(first + i * stride, SHORT)
            return 0

        lax.fori_loop(0, n, step, 0)

    sweep(1, inner, lambda t: zfaces(range(nx), t))
    sweep(2, inner - 2, lambda t: diagonal(mids, t))

    parts = ((0, len(SHORT)), (len(SHORT), 2))

    def give_k(part):
        first, n = parts[part]
        for g in range(ng):
            for i in range(first, first + n):
                KP[g, i] = KF[i, :, g * LANES : (g + 1) * LANES]
        for dc in range(1, cn):
            pltpu.make_async_remote_copy(
                src_ref=KP.at[others(dc) // per, pl.ds(first, n)], dst_ref=KR.at[cross, pl.ds(first, n)],
                send_sem=ks.at[part], recv_sem=kr.at[part], device_id=dev(slab, others(dc)), device_id_type=MESH,
            ).start()

    def k_moved(sem, part):
        ref = KR.at[pl.ds(0, cn - 1), pl.ds(*parts[part])]
        pltpu.make_async_copy(ref, ref, sem.at[part]).wait()

    for s in range(2):
        when_all([side[s]], lambda: landed(V.at[nx + 3 if s == 1 else 2, own], s * 3))
    for w in range(2):

        def put():
            landed(YV.at[w], 6 + w)
            r0 = 4 if w == 0 else TILE + ny
            V[3 : 3 + nx, r0 : r0 + 4, :] = YV[w]

        when_all([wall[w]], put)
    for t in (0, nt - 1):
        zfaces(range(nx), t)
    for t in (0, 1, nt - 2, nt - 1):
        diagonal(mids, t)
    sweep(1, inner, lambda t: diagonal(ends, t))
    for w in range(2):
        for s in range(2):

            def put():
                landed(CV.at[w, s], 8 + 2 * w + s)
                r0 = 4 if w == 0 else TILE + ny
                p0 = 1 if s == 0 else nx + 3
                V[p0 : p0 + 2, r0 : r0 + 4, :] = CV[w, s]

            when_all([wall[w], side[s]], put)
    for t in (0, nt - 1):
        diagonal(ends, t)
    sweep(0, nt, lambda t: near(mids, (0, 1, 3), t))
    sweep(0, nt, lambda t: (near([0], (0, 1, 3), t), near([nx - 1], (0, 3), t)))
    sweep(1, inner, lambda t: coefficients(mids, t), 2)
    plane_sums(1, 1, nx - 2)
    for s in range(2):
        when_all([side[s]], lambda: landed(V.at[nx + 4 if s == 1 else 1, own], s * 3 + 1))
    sweep(0, nt, lambda t: (zfaces([-1, nx], t), diagonal([-1, nx], t)))
    sweep(0, nt, lambda t: (near([-1], (1,), t), near([nx - 1], (1,), t)))
    sweep(1, inner, lambda t: near([-1, nx], (0, 3), t))
    sweep(1, inner, lambda t: coefficients(ends, t), 2)
    plane_sums(0, nx - 1, 2)
    give_k(0)
    ready = [(p, d) for p in range(nx) for d in (1, -1) if 0 <= p + d < nx]
    sweep(1, inner, lambda t: far(ready, t), 2)
    for p, d in ready:
        sums(p, [(2 * d, 0)])
    for s in range(2):
        when_all([side[s]], lambda: landed(V.at[nx + 5 if s == 1 else 0, own], s * 3 + 2))
    sweep(1, inner, lambda t: diagonal([-2, nx + 1], t))
    sweep(1, inner, lambda t: far([(0, -1), (nx - 1, 1)], t))
    sums(0, [(-2, 0)])
    sums(nx - 1, [(2, 0)])

    FRAME[...] = jnp.zeros_like(FRAME)
    for c in range(2):
        for dx in range(-2, 3):
            total = None
            for n, o in enumerate(ALL):
                if o[0] == dx:
                    a = CS[n, c]
                    a = a if o[1] == 0 else zshift(a, -o[1])
                    total = a if total is None else total + a
            FRAME[c, nx + dx : 2 * nx + dx, :] += total
    cx, cz = FRAME[0], FRAME[1]
    e = cx - pltpu.roll(cx, 1, 0) + cz - zshift(cz, -1)
    WIN[:, 0:LANES] = jnp.zeros((4 * nx, LANES), f32)
    WIN[:, LANES + nz :] = jnp.zeros((4 * nx, LANES), f32)
    WIN[:, LANES : LANES + nz] = e

    def wide(get, g):
        main, before, after = get(g + 1), get(g), get(g + 2)
        lane = lax.broadcasted_iota(jnp.int32, main.shape, 1)
        return main, jnp.where(lane < LANES // 2, after, before)

    for g in range(ng):
        main, halo = wide(lambda i: WIN[:, i * LANES : (i + 1) * LANES], g)
        for b in range(3):
            EB[g, b, :, 0:LANES] = main[b * nx : (b + 1) * nx]
            EB[g, b, :, LANES : 2 * LANES] = halo[b * nx : (b + 1) * nx]

    if steps > 0:
        greeted(0)
        if steps > 1:
            greet(1)

    def span(ds):
        return pl.ds(max(0, ds), 3 - abs(ds))

    def e_copy(ds, dc):
        return pltpu.make_async_remote_copy(
            src_ref=EB.at[others(dc) // per, span(ds)], dst_ref=EBR.at[2 - ds, cross, span(ds)],
            send_sem=bs.at[ds + 2], recv_sem=br.at[2 - ds], device_id=dev(slab + ds, others(dc)), device_id_type=MESH,
        )

    for ds in (0, 1, -1, 2, -2):

        def start():
            for dc in range(1 if ds == 0 else 0, cn):
                e_copy(ds, dc).start()

        when_all([there(ds)], start)
    give_k(1)
    for b in range(3):
        EBR[2, cross, b] = EB[mine, b]
    KR[cross] = KP[mine]

    begin(bulk[2:])

    def forced(k):
        for s in range(2):
            when_all([side[s]], lambda: landed(F.at[:, nx + 2 + k if s == 1 else 1 - k, own], 12 + 2 * s + k))

    forced(0)
    for w in range(2):

        def put():
            landed(YF.at[w], 16 + w)
            r0 = TILE - 2 if w == 0 else TILE + ny
            F[:, 2 : 2 + nx, r0 : r0 + 2, :] = YF[w]

        when_all([wall[w]], put)
        for s in range(2):

            def put():
                landed(CF.at[w, s], 18 + 2 * w + s)
                r0 = TILE - 2 if w == 0 else TILE + ny
                p0 = 1 if s == 0 else nx + 2
                F[:, p0 : p0 + 1, r0 : r0 + 2, :] = CF[w, s]

            when_all([wall[w], side[s]], put)

    def scaled(planes, t):
        for p in planes:
            d = DI[p, tile(t), :]
            for c in range(2):
                Y0[c, p, tile(t), :] = d * F[c, p, tile(t), :]

    def faces(p, t):
        at = tile(t)
        v, vyp, vym = rows(V, (p + 3,), t, nt - 1)
        d = DI[p + 2, at, :]
        return (
            d * (v + vyp), d * (v + vym), d * (v + V[p + 4, at, :]), d * (v + V[p + 2, at, :]),
            d * ZF[0, p + 2, at, :], d * ZF[1, p + 2, at, :],
        )

    def carried(field, c, p, t, face):
        yp, ym, xp, xm, zp, zm = face
        a, au, ad = rows(field, (c, p), t, nt - 1)
        near_by = yp * au + ym * ad + xp * field[c, p + 1, tile(t), :] + xm * field[c, p - 1, tile(t), :]
        return a, near_by + zp * zshift(a, 1) + zm * zshift(a, -1)

    def once(planes, t):
        for p in planes:
            face = faces(p, t)
            for c in range(2):
                a, t1 = carried(Y0, c, p + 2, t, face)
                Z[c, p + 1, tile(t), :] = w1 * a + w2 * t1

    def twice(planes, t):
        for p in planes:
            face = faces(p, t)
            for c in range(2):
                a, t2 = carried(Z, c, p + 1, t, face)
                BASE[c, p, tile(t - 1), :] = w0 * Y0[c, p + 2, tile(t), :] + t2

    sweep(0, nt, lambda t: scaled(range(1, nx + 3), t))
    sweep(0, nt, lambda t: once(range(nx), t), 1)
    sweep(1, inner, lambda t: twice(mids, t), 1)

    for ds in range(-2, 3):
        src = -ds

        def wait():
            n = cn - 1 if ds == 0 else cn
            ref = EBR.at[2 + src, pl.ds(0, n), span(ds)]
            pltpu.make_async_copy(ref, ref, br.at[2 + src]).wait()

        when_all([there(src)], wait)
    for part in range(2):
        k_moved(kr, part)
    WINB = WIN.at[:, 0 : 2 * LANES]
    WINB[3 * nx :, :] = jnp.zeros((nx, 2 * LANES), f32)
    for t in range(-1, 2):
        WINB[(t + 1) * nx : (t + 2) * nx, :] = jnp.zeros((nx, 2 * LANES), f32)

        def gather():
            for b in range(-1, 2):
                src = t - b

                def take():
                    total = EBR[2 + src, 0, b + 1]
                    for c in range(1, cn):
                        total = total + EBR[2 + src, c, b + 1]
                    WINB[(t + 1) * nx : (t + 2) * nx, :] += total

                when_all([there(src)], take)

        when_all([there(t)], gather)
    for n in range(len(ALL)):
        total = KR[0, n]
        for c in range(1, cn):
            total = total + KR[c, n]
        KS[n] = total

    def columns(q):
        for c, grad in enumerate((q - ring(q, 1, 0), q - ring(q, 1, 1))):
            for dz in range(-2, 3):
                QS[dz + 2, c] = ring(grad, dz, 1)[:, 0:LANES]
        out = []
        for c in range(2):
            total = None
            for n, (dx, dz) in enumerate(ALL):
                a = KS[n] * QS[dz + 2, c, nx + dx : 2 * nx + dx, :]
                total = a if total is None else total + a
            out.append(total)
        return out

    q = WINB[...]
    c1 = columns(q)
    me = slab * ng + mine
    A1[me, 0] = q[nx : 2 * nx, 0:LANES]
    A1[me, 1] = c1[0]
    A1[me, 2] = c1[1]
    for k in range(1, steps):
        greeted(k)
        if k + 1 < steps:
            greet(k + 1)

    def share(buf, ssem, rsem):
        order = [0, 1, sn - 1] + list(range(2, sn - 1))
        for ds in list(dict.fromkeys(d % sn for d in order)):
            for dg in range(ng):
                if ds == 0 and dg == 0:
                    continue
                to = lax.rem(mine + dg, ng) * per + lax.rem(cross, per)
                pltpu.make_async_remote_copy(
                    src_ref=buf.at[me], dst_ref=buf.at[me], send_sem=ssem, recv_sem=rsem.at[slab],
                    device_id=dev(lax.rem(slab + ds, sn), to), device_id_type=MESH,
                ).start()

    def shared(buf, rsem, s, n):
        ref = buf.at[pl.ds(0, n)]
        pltpu.make_async_copy(ref, ref, rsem.at[s]).wait()

    share(A1, as1, ar1)
    forced(1)
    sweep(0, nt, lambda t: scaled([0, nx + 3], t))
    sweep(0, nt, lambda t: once([-1, nx], t), 1)
    sweep(1, inner, lambda t: twice(ends, t), 1)

    if ng > 1:
        shared(A1, ar1, slab, ng - 1)
    for ds in (-1, 1):
        when_all([there(ds)], lambda: shared(A1, ar1, slab + ds, ng))
    FRAME[...] = jnp.zeros_like(FRAME)
    for t in range(-1, 2):

        def fill():
            for g in range(ng):
                for a in range(3):
                    FRAME[a, (t + 1) * nx : (t + 2) * nx, g * LANES : (g + 1) * LANES] = A1[(slab + t) * ng + g, a]

        when_all([there(t)], fill)
    gwin = FRAME[0]
    cx, cz = FRAME[1], FRAME[2]
    sg = cx - pltpu.roll(cx, 1, 0) + cz - zshift(cz, -1)
    trow = lax.broadcasted_iota(jnp.int32, sg.shape, 0)
    known = (trow < 3 * nx) & ((trow < 2 * nx) | right) & ((trow >= nx) | left)
    sg = jnp.where(known, sg, 0.0)
    WIN[:, 0:LANES] = jnp.zeros((4 * nx, LANES), f32)
    WIN[:, LANES + nz :] = jnp.zeros((4 * nx, LANES), f32)
    WIN[:, LANES : LANES + nz] = sg
    main, halo = wide(lambda i: WIN[:, pl.ds(pl.multiple_of(i * LANES, LANES), LANES)], mine)
    c2 = columns(jnp.concatenate([main, halo], 1))
    A2[me, 0] = c2[0]
    A2[me, 1] = c2[1]
    share(A2, as2, ar2)

    for i, q in enumerate((gwin, sg)):
        for c, grad in enumerate((q - ring(q, 1, 0), q - zshift(q, 1))):
            for dz in range(-2, 3):
                a = grad if dz == 0 else zshift(grad, dz)
                for r in range(nx - 2, 2 * nx + 2):
                    GSR[i, dz + 2, c, r] = a[r : r + 1]

    def apply(i, _):
        p, t = i // inner, i % inner
        at = tile(t)
        total = [[None, None], [None, None]]
        for n, (dx, dz) in enumerate(ALL):
            m = M[n, p, at, :]
            for j in range(2):
                for c in range(2):
                    a = m * GSR[j, dz + 2, c, p + nx + dx]
                    total[j][c] = a if total[j][c] is None else total[j][c] + a
        for j in range(2):
            for c in range(2):
                FD[j, c, p, at, :] = total[j][c]
        return 0

    lax.fori_loop(0, nx * inner, apply, 0)

    width = nz // cn
    slot = lax.broadcasted_iota(jnp.int32, (width, nz), 0) + cross * width
    onehot = (jnp.broadcast_to(owner[...], (width, nz)) == slot).astype(f32).astype(jnp.bfloat16)
    rest = jnp.concatenate([gwin[nx : 2 * nx], sg[nx : 2 * nx]], 0)
    ordered = jnp.zeros((2 * nx, width), f32)
    for _ in range(3):
        piece = rest.astype(jnp.bfloat16)
        rest = rest - piece.astype(f32)
        ordered = ordered + lax.dot_general(
            piece, onehot, (((1,), (1,)), ((), ())), preferred_element_type=f32
        )

    for ds in range(2, sn - 1):
        s = lax.rem(slab + ds, sn)
        shared(A1, ar1, s, ng)
    for ds in (1, -1):
        when_all([jnp.logical_not(there(ds))], lambda: shared(A1, ar1, lax.rem(slab + ds + sn, sn), ng))

    def whole(buf, a, into):
        for s in range(sn):
            for g in range(ng):
                FULL[into, s * nx : (s + 1) * nx, g * LANES : (g + 1) * LANES] = buf[s * ng + g, a]

    def below(a):
        row = lax.broadcasted_iota(jnp.int32, a.shape, 0)
        return jnp.where(row == 0, 0.0, pltpu.roll(a, 1, 0))

    for a in range(3):
        whole(A1, a, a)
    g = FULL[0]
    s1 = FULL[1] - below(FULL[1]) + FULL[2] - zshift(FULL[2], -1)
    rr = jnp.sum(g * g)
    alpha0 = rr / jnp.sum(g * s1)
    resid = g - alpha0 * s1
    fresh = jnp.sum(resid * resid)
    beta = fresh / rr
    dirn = resid + beta * g
    FULL[3] = s1
    FULL[4] = dirn

    def combine(t):
        for p in range(nx):
            for c in range(2):
                a, b = FD[0, c, p, tile(t), :], FD[1, c, p, tile(t), :]
                BASE[c, p, tile(t), :] = BASE[c, p, tile(t), :] - alpha0 * a
                FD[0, c, p, tile(t), :] = a - alpha0 * b + beta * a

    sweep(0, inner, combine)
    pg, ps = ordered[:nx], ordered[nx:]

    if ng > 1:
        shared(A2, ar2, slab, ng - 1)
    for ds in range(1, sn):
        shared(A2, ar2, lax.rem(slab + ds, sn), ng)
    for a in range(2):
        whole(A2, a, a)
    s2 = FULL[0] - below(FULL[0]) + FULL[1] - zshift(FULL[1], -1)
    s1 = FULL[3]
    image = s1 - alpha0 * s2 + beta * s1
    alpha1 = fresh / jnp.sum(FULL[4] * image)
    press[...] = alpha0 * pg + alpha1 * (pg - alpha0 * ps + beta * pg)

    def finish(t):
        for p in range(nx):
            for c in range(2):
                vel[c, p, tile(t), :] = BASE[c, p, tile(t), :] - alpha1 * FD[0, c, p, tile(t), :]

    sweep(0, inner, finish)

    for conds, make in first + walls + corners + later + forces + bulk:
        when_all(conds, lambda: make().wait_send())
    for ds in range(-2, 3):

        def left_here():
            ref = EBR.at[2 - ds, pl.ds(0, cn - 1 if ds == 0 else cn), span(ds)]
            pltpu.make_async_copy(ref, ref, bs.at[ds + 2]).wait()

        when_all([there(ds)], left_here)
    for part in range(2):
        k_moved(ks, part)
    for buf, sem in ((A1, as1), (A2, as2)):
        ref = buf.at[pl.ds(0, sn * ng - 1)]
        pltpu.make_async_copy(ref, ref, sem).wait()


def stokes(forcing, viscosity, owner, sn, cn):
    nx, ny, nz = viscosity.shape
    f32 = jnp.float32
    ng, _ = chunks(cn, nz)
    no = len(ALL)
    ye = ny + 2 * TILE
    vmem = pl.BlockSpec(memory_space=pltpu.VMEM)
    anywhere = pl.BlockSpec(memory_space=pl.ANY)
    dma = pltpu.SemaphoreType.DMA

    def buf(*shape):
        return pltpu.VMEM(shape, f32)

    return pl.pallas_call(
        functools.partial(stokes_body, sn, cn),
        out_shape=(
            pltpu.VMEM(forcing.shape, f32),
            pltpu.VMEM((nx, nz // cn), f32),
        ),
        in_specs=[anywhere, anywhere, vmem],
        out_specs=(vmem, vmem),
        scratch_shapes=[
            buf(nx + 6, ye, nz),
            buf(2, nx + 4, ye, nz),
            buf(2, nx, 4, nz),
            buf(2, 2, nx, 2, nz),
            buf(2, nx, 4, nz),
            buf(2, 2, 2, 4, nz),
            buf(2, 2, nx, 2, nz),
            buf(2, 2, 2, 1, 2, nz),
            buf(2, nx + 4, ye, nz),
            buf(nx + 4, ye, nz),
            buf(6, nx + 2, ye, nz),
            buf(no, nx, ny, nz),
            buf(2, nx + 4, ye, nz),
            buf(2, nx + 2, ye, nz),
            buf(2, nx, ny, nz),
            buf(2, 2, nx, ny, nz),
            buf(no, nx, nz),
            buf(no, 2, nx, nz),
            buf(3, 4 * nx, nz),
            buf(ng, no, nx, LANES),
            buf(cn, no, nx, LANES),
            buf(ng, 3, nx, 2 * LANES),
            buf(5, cn, 3, nx, 2 * LANES),
            buf(sn * ng, 3, nx, LANES),
            buf(sn * ng, 2, nx, LANES),
            buf(4 * nx, nz + 2 * LANES),
            buf(5, 2, 4 * nx, LANES),
            buf(no, nx, LANES),
            buf(2, 5, 2, 4 * nx, 1, nz),
            buf(5, sn * nx, nz),
            dma((2,)),
            dma((22,)),
            dma((22,)),
            dma((5,)),
            dma((5,)),
            dma((2,)),
            dma((2,)),
            dma,
            dma((sn,)),
            dma,
            dma((sn,)),
            pltpu.SemaphoreType.REGULAR((max(1, (sn - 2).bit_length()),)),
        ],
        compiler_params=pltpu.CompilerParams(
            collective_id=0, has_side_effects=True, vmem_limit_bytes=56 * 2**20
        ),
        name="stokes",
    )(viscosity, forcing, owner)


def shards(forcing, viscosity, owner_slot):
    sn, cn = lax.axis_size("slab"), lax.axis_size("cross")
    return stokes(forcing, viscosity, owner_slot.reshape(1, -1), sn, cn)


def solution(mesh):
    in_specs = (P(None, "slab", "cross", None), P("slab", "cross", None), P())
    out_specs = (P(None, "slab", "cross", None), P("slab", "cross"))
    return jax.shard_map(shards, mesh=mesh, in_specs=in_specs, out_specs=out_specs, check_vma=False)
```

```python
import functools

import jax
import jax.numpy as jnp
from jax import lax
from jax.experimental import pallas as pl
from jax.experimental.pallas import tpu as pltpu
from jax.sharding import PartitionSpec as P

MESH = pl.DeviceIdType.MESH

DEGREE = 3
LANES = 128
TILE = 8

cheb_theta = 1.025
cheb_delta = 0.975


def cheb_weights():
    sigma = cheb_theta / cheb_delta
    solved = [1.0 / cheb_theta] + [0.0] * (DEGREE - 1)
    change = list(solved)
    rho_prev = 1.0 / sigma
    for step in range(DEGREE - 1):
        resid = [(1.0 if k == 0 else solved[k - 1]) - solved[k] for k in range(DEGREE)]
        rho = 1.0 / (2.0 * sigma - rho_prev)
        change = [rho * rho_prev * c + 2.0 * rho / cheb_delta * r for c, r in zip(change, resid)]
        solved = [s + c for s, c in zip(solved, change)]
        rho_prev = rho
    return solved


SHORT = [(dx, dz) for dx in range(-1, 2) for dz in range(-2, 3) if abs(dx) + abs(dz) <= 2]
ALL = SHORT + [(-2, 0), (2, 0)]


def chunks(cn, nz):
    n = min(cn, nz // LANES)
    return n, cn // n


def zshift(a, d):
    n = a.shape[-1]
    k = lax.broadcasted_iota(jnp.int32, a.shape, a.ndim - 1)
    keep = (k < n - d) if d > 0 else (k >= -d)
    return jnp.where(keep, pltpu.roll(a, (-d) % n, a.ndim - 1), 0.0)


def ring(a, d, axis):
    return a if d == 0 else pltpu.roll(a, (-d) % a.shape[axis], axis)


def rows(ref, lead, t, last):
    def tile(i):
        return ref[lead + (pl.ds(pl.multiple_of(i * TILE, TILE), TILE), slice(None))]

    cur = tile(t)
    row = lax.broadcasted_iota(jnp.int32, cur.shape, 0)
    up = pltpu.roll(jnp.where(row == 0, tile(jnp.minimum(t + 1, last)), cur), TILE - 1, 0)
    down = pltpu.roll(jnp.where(row == TILE - 1, tile(jnp.maximum(t - 1, 0)), cur), 1, 0)
    return cur, up, down


def stokes_body(
    sn, cn, visc, forc, owner, vel, press,
    V, F, ypk, fpk, YV, CV, YF, CF, ZF, DI, U, M, Y0, Z, BASE, FD,
    KF, CS, FRAME, KP, KR, EB, EBR, A1, A2, WIN, QS, KS, GSR, FULL, GD,
    lsem, hs, hr, bs, br, ks, kr, as1, ar1, as2, ar2, hop,
):
    slab, cross = lax.axis_index("slab"), lax.axis_index("cross")
    nx, ny, nz = visc.shape
    nt = ny // TILE + 2
    ng, per = chunks(cn, nz)
    mine = cross // per
    f32 = jnp.float32
    w0, w1, w2 = [2.0 * w for w in cheb_weights()]

    def dev(s, c):
        return {"slab": s, "cross": c}

    def there(ds):
        return (slab + ds >= 0) & (slab + ds < sn)

    def others(dc):
        return lax.rem(cross + dc, cn)

    left, right = slab > 0, slab < sn - 1
    up, down = cross > 0, cross < cn - 1
    side, wall = (left, right), (up, down)
    own = pl.ds(TILE, ny)

    load_v = pltpu.make_async_copy(visc, V.at[pl.ds(3, nx), own], lsem.at[0])
    load_f = pltpu.make_async_copy(forc, F.at[:, pl.ds(2, nx), own], lsem.at[1])
    load_v.start()
    load_f.start()
    barrier = pltpu.get_barrier_semaphore()
    for ds in (0, 1, -1):
        for dc in range(cn):
            if ds == 0 and dc == 0:
                continue
            if ds == 0:
                pl.semaphore_signal(barrier, inc=1, device_id=dev(slab, others(dc)), device_id_type=MESH)
            else:

                @pl.when(there(ds))
                def _():
                    pl.semaphore_signal(barrier, inc=1, device_id=dev(slab + ds, others(dc)), device_id_type=MESH)

    zero_v = jnp.zeros((nx + 6, TILE, nz), f32)
    V[:, 0:TILE, :] = zero_v
    V[:, TILE + ny : 2 * TILE + ny, :] = zero_v
    zero_f = jnp.zeros((2, nx + 4, TILE, nz), f32)
    F[:, :, 0:TILE, :] = zero_f
    F[:, :, TILE + ny : 2 * TILE + ny, :] = zero_f
    for s in range(2):

        @pl.when(jnp.logical_not(side[s]))
        def _():
            v0, f0 = (0, 0) if s == 0 else (nx + 3, nx + 2)
            V[v0 : v0 + 3, TILE : TILE + ny, :] = jnp.zeros((3, ny, nz), f32)
            F[:, f0 : f0 + 2, TILE : TILE + ny, :] = jnp.zeros((2, 2, ny, nz), f32)

    count = (cn - 1) + cn * (jnp.where(left, 1, 0) + jnp.where(right, 1, 0))
    pl.semaphore_wait(barrier, count)

    steps = max(0, (sn - 2).bit_length())

    def greet(k):
        for d in (-(2**k), 2**k):

            @pl.when(there(d))
            def _():
                pl.semaphore_signal(hop.at[k], inc=1, device_id=dev(slab + d, cross), device_id_type=MESH)

    def greeted(k):
        pl.semaphore_wait(hop.at[k], jnp.where(there(-(2**k)), 1, 0) + jnp.where(there(2**k), 1, 0))

    def send(src, dst, out, into, s, c):
        return pltpu.make_async_remote_copy(
            src_ref=src, dst_ref=dst, send_sem=hs.at[out], recv_sem=hr.at[into], device_id=dev(s, c),
            device_id_type=MESH,
        )

    def vx(s, k):
        src = visc.at[k if s == 0 else nx - 1 - k]
        dst = V.at[nx + 3 + k if s == 0 else 2 - k, own]
        return send(src, dst, s * 3 + k, (1 - s) * 3 + k, slab + (2 * s - 1), cross)

    def vy(w):
        return send(ypk.at[w], YV.at[1 - w], 6 + w, 7 - w, slab, cross + (2 * w - 1))

    def vc(w, s):
        src = ypk.at[w, pl.ds(0 if s == 0 else nx - 2, 2)]
        return send(src, CV.at[1 - w, 1 - s], 8 + 2 * w + s, 8 + 2 * (1 - w) + 1 - s, slab + (2 * s - 1), cross + (2 * w - 1))

    def fx(s, k):
        src = forc.at[:, k if s == 0 else nx - 1 - k]
        dst = F.at[:, nx + 2 + k if s == 0 else 1 - k, own]
        return send(src, dst, 12 + 2 * s + k, 12 + 2 * (1 - s) + k, slab + (2 * s - 1), cross)

    def fy(w):
        return send(fpk.at[w], YF.at[1 - w], 16 + w, 17 - w, slab, cross + (2 * w - 1))

    def fc(w, s):
        src = fpk.at[w, :, pl.ds(0 if s == 0 else nx - 1, 1)]
        return send(src, CF.at[1 - w, 1 - s], 18 + 2 * w + s, 18 + 2 * (1 - w) + 1 - s, slab + (2 * s - 1), cross + (2 * w - 1))

    def landed(ref, into):
        pltpu.make_async_copy(ref, ref, hr.at[into]).wait()

    def when_all(conds, run):
        cond = conds[0]
        for c in conds[1:]:
            cond = cond & c
        pl.when(cond)(run)

    first = [([side[s]], functools.partial(vx, s, 0)) for s in range(2)]
    walls = [([wall[w]], functools.partial(vy, w)) for w in range(2)]
    corners = [([wall[w], side[s]], functools.partial(vc, w, s)) for w in range(2) for s in range(2)]
    later = [([side[s]], functools.partial(vx, s, k)) for k in (1, 2) for s in range(2)]
    forces = [([wall[w]], functools.partial(fy, w)) for w in range(2)]
    forces += [([wall[w], side[s]], functools.partial(fc, w, s)) for w in range(2) for s in range(2)]
    bulk = [([side[s]], functools.partial(fx, s, k)) for k in range(2) for s in range(2)]

    def begin(sends):
        for conds, make in sends:
            when_all(conds, lambda: make().start())

    begin(first)
    load_v.wait()
    ypk[0] = V[3 : 3 + nx, TILE : TILE + 4, :]
    ypk[1] = V[3 : 3 + nx, TILE + ny - 4 : TILE + ny, :]
    begin(walls + corners + later)
    load_f.wait()
    fpk[0] = F[:, 2 : 2 + nx, TILE : TILE + 2, :]
    fpk[1] = F[:, 2 : 2 + nx, TILE + ny - 2 : TILE + ny, :]
    begin(forces + bulk[:2])
    if steps > 0:
        greet(0)

    inner = nt - 2

    def sweep(lo, n, body, k=10):
        while n % k:
            k -= 1

        def step(i, _):
            for j in range(k):
                body(lo + i * k + j)
            return 0

        lax.fori_loop(0, n // k, step, 0)

    def tile(t):
        return pl.ds(t * TILE if isinstance(t, int) else pl.multiple_of(t * TILE, TILE), TILE)

    def inside(plane, t):
        ok = ((t > 0) | up) & ((t < nt - 1) | down)
        if plane < 0:
            ok = ok & left
        if plane >= nx:
            ok = ok & right
        return jnp.where(ok, 1.0, 0.0)

    def zsides(v):
        return v + zshift(v, 1), v + zshift(v, -1)

    def zfaces(planes, t):
        for p in planes:
            ZF[0, p + 2, tile(t), :], ZF[1, p + 2, tile(t), :] = zsides(V[p + 3, tile(t), :])

    def diagonal(planes, t):
        for p in planes:
            c, yp, ym = rows(V, (p + 3,), t, nt - 1)
            zp, zm = zsides(c) if p < -1 or p > nx else (ZF[0, p + 2, tile(t), :], ZF[1, p + 2, tile(t), :])
            diag = V[p + 4, tile(t), :] + V[p + 2, tile(t), :] + yp + ym + zp + zm + 4.0 * c
            DI[p + 2, tile(t), :] = inside(p, t) * (1.0 / jnp.maximum(diag, 1e-30))

    def near(planes, comps, t):
        for p in planes:
            at = tile(t)
            d = DI[p + 2, at, :]
            wd = w2 * d
            if 0 in comps:
                v, vyp, vym = rows(V, (p + 3,), t, nt - 1)
                _, dyp, dym = rows(DI, (p + 2,), t, nt - 1)
                U[0, p + 1, at, :] = wd * ((v + vyp) * dyp + (v + vym) * dym) + w1 * d
            if 1 in comps:
                a = wd * ((V[p + 3, at, :] + V[p + 4, at, :]) * DI[p + 3, at, :])
                U[1, p + 1, at, :] = a
                U[2, p + 1, at, :] = zshift(a, 1)
                U[5, p + 1, at, :] = zshift(a, -1)
            if 3 in comps:
                U[3, p + 1, at, :] = wd * (ZF[0, p + 2, at, :] * zshift(d, 1))
                U[4, p + 1, at, :] = wd * (ZF[1, p + 2, at, :] * zshift(d, -1))

    def coefficients(planes, t):
        for p in planes:
            at, to = tile(t), tile(t - 1)
            v, vyp, vym = rows(V, (p + 3,), t, nt - 1)
            d = DI[p + 2, at, :]
            yp, ym = d * (v + vyp), d * (v + vym)
            xp, xm = d * (v + V[p + 4, at, :]), d * (v + V[p + 2, at, :])
            zp, zm = d * ZF[0, p + 2, at, :], d * ZF[1, p + 2, at, :]

            def put(o, a):
                M[ALL.index(o), p, to, :] = a

            def along(n, plane):
                a, au, ad = rows(U, (n, plane + 1), t, nt - 1)
                return a, yp * au + ym * ad

            def at_plane(n, plane):
                return U[n, plane + 1, at, :]

            u0, y0 = along(0, p)
            u1, y1 = along(1, p)
            b1, y2 = along(1, p - 1)
            u3, y3 = along(3, p)
            u4, y4 = along(4, p)
            put((0, 0), w0 * d + y0 + xp * u1 + xm * b1 + zp * u3 + zm * u4)
            put((1, 0), y1 + xp * at_plane(0, p + 1))
            put((-1, 0), y2 + xm * at_plane(0, p - 1))
            put((0, 1), y3 + zp * zshift(u0, 1))
            put((0, -1), y4 + zm * zshift(u0, -1))
            put((1, 1), xp * at_plane(3, p + 1) + zp * at_plane(2, p))
            put((1, -1), xp * at_plane(4, p + 1) + zm * at_plane(5, p))
            put((-1, 1), xm * at_plane(3, p - 1) + zp * at_plane(2, p - 1))
            put((-1, -1), xm * at_plane(4, p - 1) + zm * at_plane(5, p - 1))
            put((0, 2), zp * zshift(u3, 1))
            put((0, -2), zm * zshift(u4, -1))

    def far(pairs, t):
        for p, d in pairs:
            at = tile(t)
            v0, v1, v2 = [V[p + 3 + d * k, at, :] for k in range(3)]
            d0, d1, d2 = [DI[p + 2 + d * k, at, :] for k in range(3)]
            M[ALL.index((2 * d, 0)), p, tile(t - 1), :] = w2 * (d0 * (v0 + v1)) * (d1 * (v1 + v2)) * d2

    prow = lax.broadcasted_iota(jnp.int32, (nx, nz), 0)
    KF[...] = jnp.zeros_like(KF)
    CS[...] = jnp.zeros_like(CS)

    def sums(p, offsets):
        for o in offsets:
            n = ALL.index(o)
            acc = None
            for t in range(inner):
                m = M[n, p, tile(t), :]
                new = (m, m * F[0, p + 2, tile(t + 1), :], m * F[1, p + 2, tile(t + 1), :])
                acc = new if acc is None else [a + b for a, b in zip(acc, new)]
            here = prow == p
            for ref, a in zip((KF.at[n], CS.at[n, 0], CS.at[n, 1]), acc):
                for shift in (4, 2, 1):
                    a = a + pltpu.roll(a, shift, 0)
                ref[...] = jnp.where(here, a[0:nx], ref[...])

    mids, ends = list(range(1, nx - 1)), [0, nx - 1]

    def plane_sums(first, stride, n):
        def step(i, _):
            sums(first + i * stride, SHORT)
            return 0

        lax.fori_loop(0, n, step, 0)

    sweep(1, inner, lambda t: zfaces(range(nx), t))
    sweep(2, inner - 2, lambda t: diagonal(mids, t))

    parts = ((0, len(SHORT)), (len(SHORT), 2))

    def give_k(part):
        first, n = parts[part]
        for g in range(ng):
            for i in range(first, first + n):
                KP[g, i] = KF[i, :, g * LANES : (g + 1) * LANES]
        for dc in range(1, cn):
            pltpu.make_async_remote_copy(
                src_ref=KP.at[others(dc) // per, pl.ds(first, n)], dst_ref=KR.at[cross, pl.ds(first, n)],
                send_sem=ks.at[part], recv_sem=kr.at[part], device_id=dev(slab, others(dc)), device_id_type=MESH,
            ).start()

    def k_moved(sem, part):
        ref = KR.at[pl.ds(0, cn - 1), pl.ds(*parts[part])]
        pltpu.make_async_copy(ref, ref, sem.at[part]).wait()

    for s in range(2):
        when_all([side[s]], lambda: landed(V.at[nx + 3 if s == 1 else 2, own], s * 3))
    for w in range(2):

        def put():
            landed(YV.at[w], 6 + w)
            r0 = 4 if w == 0 else TILE + ny
            V[3 : 3 + nx, r0 : r0 + 4, :] = YV[w]

        when_all([wall[w]], put)
    for t in (0, nt - 1):
        zfaces(range(nx), t)
    for t in (0, 1, nt - 2, nt - 1):
        diagonal(mids, t)
    sweep(1, inner, lambda t: diagonal(ends, t))
    for w in range(2):
        for s in range(2):

            def put():
                landed(CV.at[w, s], 8 + 2 * w + s)
                r0 = 4 if w == 0 else TILE + ny
                p0 = 1 if s == 0 else nx + 3
                V[p0 : p0 + 2, r0 : r0 + 4, :] = CV[w, s]

            when_all([wall[w], side[s]], put)
    for t in (0, nt - 1):
        diagonal(ends, t)
    sweep(0, nt, lambda t: near(mids, (0, 1, 3), t))
    sweep(0, nt, lambda t: (near([0], (0, 1, 3), t), near([nx - 1], (0, 3), t)))
    sweep(1, inner, lambda t: coefficients(mids, t), 2)
    plane_sums(1, 1, nx - 2)
    for s in range(2):
        when_all([side[s]], lambda: landed(V.at[nx + 4 if s == 1 else 1, own], s * 3 + 1))
    sweep(0, nt, lambda t: (zfaces([-1, nx], t), diagonal([-1, nx], t)))
    sweep(0, nt, lambda t: (near([-1], (1,), t), near([nx - 1], (1,), t)))
    sweep(1, inner, lambda t: near([-1, nx], (0, 3), t))
    sweep(1, inner, lambda t: coefficients(ends, t), 2)
    plane_sums(0, nx - 1, 2)
    give_k(0)
    ready = [(p, d) for p in range(nx) for d in (1, -1) if 0 <= p + d < nx]
    sweep(1, inner, lambda t: far(ready, t), 2)
    for p, d in ready:
        sums(p, [(2 * d, 0)])
    for s in range(2):
        when_all([side[s]], lambda: landed(V.at[nx + 5 if s == 1 else 0, own], s * 3 + 2))
    sweep(1, inner, lambda t: diagonal([-2, nx + 1], t))
    sweep(1, inner, lambda t: far([(0, -1), (nx - 1, 1)], t))
    sums(0, [(-2, 0)])
    sums(nx - 1, [(2, 0)])

    FRAME[...] = jnp.zeros_like(FRAME)
    for c in range(2):
        for dx in range(-2, 3):
            total = None
            for n, o in enumerate(ALL):
                if o[0] == dx:
                    a = CS[n, c]
                    a = a if o[1] == 0 else zshift(a, -o[1])
                    total = a if total is None else total + a
            FRAME[c, nx + dx : 2 * nx + dx, :] += total
    cx, cz = FRAME[0], FRAME[1]
    e = cx - pltpu.roll(cx, 1, 0) + cz - zshift(cz, -1)
    WIN[:, 0:LANES] = jnp.zeros((4 * nx, LANES), f32)
    WIN[:, LANES + nz :] = jnp.zeros((4 * nx, LANES), f32)
    WIN[:, LANES : LANES + nz] = e

    def wide(get, g):
        main, before, after = get(g + 1), get(g), get(g + 2)
        lane = lax.broadcasted_iota(jnp.int32, main.shape, 1)
        return main, jnp.where(lane < LANES // 2, after, before)

    for g in range(ng):
        main, halo = wide(lambda i: WIN[:, i * LANES : (i + 1) * LANES], g)
        for b in range(3):
            EB[g, b, :, 0:LANES] = main[b * nx : (b + 1) * nx]
            EB[g, b, :, LANES : 2 * LANES] = halo[b * nx : (b + 1) * nx]

    if steps > 0:
        greeted(0)
        if steps > 1:
            greet(1)

    def span(ds):
        return pl.ds(max(0, ds), 3 - abs(ds))

    def e_copy(ds, dc):
        return pltpu.make_async_remote_copy(
            src_ref=EB.at[others(dc) // per, span(ds)], dst_ref=EBR.at[2 - ds, cross, span(ds)],
            send_sem=bs.at[ds + 2], recv_sem=br.at[2 - ds], device_id=dev(slab + ds, others(dc)), device_id_type=MESH,
        )

    for ds in (0, 1, -1, 2, -2):

        def start():
            for dc in range(1 if ds == 0 else 0, cn):
                e_copy(ds, dc).start()

        when_all([there(ds)], start)
    give_k(1)
    for b in range(3):
        EBR[2, cross, b] = EB[mine, b]
    KR[cross] = KP[mine]

    begin(bulk[2:])

    def forced(k):
        for s in range(2):
            when_all([side[s]], lambda: landed(F.at[:, nx + 2 + k if s == 1 else 1 - k, own], 12 + 2 * s + k))

    forced(0)
    for w in range(2):

        def put():
            landed(YF.at[w], 16 + w)
            r0 = TILE - 2 if w == 0 else TILE + ny
            F[:, 2 : 2 + nx, r0 : r0 + 2, :] = YF[w]

        when_all([wall[w]], put)
        for s in range(2):

            def put():
                landed(CF.at[w, s], 18 + 2 * w + s)
                r0 = TILE - 2 if w == 0 else TILE + ny
                p0 = 1 if s == 0 else nx + 2
                F[:, p0 : p0 + 1, r0 : r0 + 2, :] = CF[w, s]

            when_all([wall[w], side[s]], put)

    def scaled(planes, t):
        for p in planes:
            d = DI[p, tile(t), :]
            for c in range(2):
                Y0[c, p, tile(t), :] = d * F[c, p, tile(t), :]

    def faces(p, t):
        at = tile(t)
        v, vyp, vym = rows(V, (p + 3,), t, nt - 1)
        d = DI[p + 2, at, :]
        return (
            d * (v + vyp), d * (v + vym), d * (v + V[p + 4, at, :]), d * (v + V[p + 2, at, :]),
            d * ZF[0, p + 2, at, :], d * ZF[1, p + 2, at, :],
        )

    def carried(field, c, p, t, face):
        yp, ym, xp, xm, zp, zm = face
        a, au, ad = rows(field, (c, p), t, nt - 1)
        near_by = yp * au + ym * ad + xp * field[c, p + 1, tile(t), :] + xm * field[c, p - 1, tile(t), :]
        return a, near_by + zp * zshift(a, 1) + zm * zshift(a, -1)

    def once(planes, t):
        for p in planes:
            face = faces(p, t)
            for c in range(2):
                a, t1 = carried(Y0, c, p + 2, t, face)
                Z[c, p + 1, tile(t), :] = w1 * a + w2 * t1

    def twice(planes, t):
        for p in planes:
            face = faces(p, t)
            for c in range(2):
                a, t2 = carried(Z, c, p + 1, t, face)
                BASE[c, p, tile(t - 1), :] = w0 * Y0[c, p + 2, tile(t), :] + t2

    sweep(0, nt, lambda t: scaled(range(1, nx + 3), t))
    sweep(0, nt, lambda t: once(range(nx), t), 1)
    sweep(1, inner, lambda t: twice(mids, t), 1)

    for ds in range(-2, 3):
        src = -ds

        def wait():
            n = cn - 1 if ds == 0 else cn
            ref = EBR.at[2 + src, pl.ds(0, n), span(ds)]
            pltpu.make_async_copy(ref, ref, br.at[2 + src]).wait()

        when_all([there(src)], wait)
    for part in range(2):
        k_moved(kr, part)
    WINB = WIN.at[:, 0 : 2 * LANES]
    WINB[3 * nx :, :] = jnp.zeros((nx, 2 * LANES), f32)
    for t in range(-1, 2):
        WINB[(t + 1) * nx : (t + 2) * nx, :] = jnp.zeros((nx, 2 * LANES), f32)

        def gather():
            for b in range(-1, 2):
                src = t - b

                def take():
                    total = EBR[2 + src, 0, b + 1]
                    for c in range(1, cn):
                        total = total + EBR[2 + src, c, b + 1]
                    WINB[(t + 1) * nx : (t + 2) * nx, :] += total

                when_all([there(src)], take)

        when_all([there(t)], gather)
    for n in range(len(ALL)):
        total = KR[0, n]
        for c in range(1, cn):
            total = total + KR[c, n]
        KS[n] = total

    def columns(q):
        for c, grad in enumerate((q - ring(q, 1, 0), q - ring(q, 1, 1))):
            for dz in range(-2, 3):
                QS[dz + 2, c] = ring(grad, dz, 1)[:, 0:LANES]
        out = []
        for c in range(2):
            total = None
            for n, (dx, dz) in enumerate(ALL):
                a = KS[n] * QS[dz + 2, c, nx + dx : 2 * nx + dx, :]
                total = a if total is None else total + a
            out.append(total)
        return out

    q = WINB[...]
    c1 = columns(q)
    me = slab * ng + mine
    A1[me, 0] = q[nx : 2 * nx, 0:LANES]
    A1[me, 1] = c1[0]
    A1[me, 2] = c1[1]
    for k in range(1, steps):
        greeted(k)
        if k + 1 < steps:
            greet(k + 1)

    def share(buf, ssem, rsem):
        order = [0, 1, sn - 1] + list(range(2, sn - 1))
        for ds in list(dict.fromkeys(d % sn for d in order)):
            for dg in range(ng):
                if ds == 0 and dg == 0:
                    continue
                to = lax.rem(mine + dg, ng) * per + lax.rem(cross, per)
                pltpu.make_async_remote_copy(
                    src_ref=buf.at[me], dst_ref=buf.at[me], send_sem=ssem, recv_sem=rsem.at[slab],
                    device_id=dev(lax.rem(slab + ds, sn), to), device_id_type=MESH,
                ).start()

    def shared(buf, rsem, s, n):
        ref = buf.at[pl.ds(0, n)]
        pltpu.make_async_copy(ref, ref, rsem.at[s]).wait()

    share(A1, as1, ar1)
    forced(1)
    sweep(0, nt, lambda t: scaled([0, nx + 3], t))
    sweep(0, nt, lambda t: once([-1, nx], t), 1)
    sweep(1, inner, lambda t: twice(ends, t), 1)

    if ng > 1:
        shared(A1, ar1, slab, ng - 1)
    for ds in (-1, 1):
        when_all([there(ds)], lambda: shared(A1, ar1, slab + ds, ng))
    FRAME[...] = jnp.zeros_like(FRAME)
    for t in range(-1, 2):

        def fill():
            for g in range(ng):
                for a in range(3):
                    FRAME[a, (t + 1) * nx : (t + 2) * nx, g * LANES : (g + 1) * LANES] = A1[(slab + t) * ng + g, a]

        when_all([there(t)], fill)
    gwin = FRAME[0]
    cx, cz = FRAME[1], FRAME[2]
    sg = cx - pltpu.roll(cx, 1, 0) + cz - zshift(cz, -1)
    trow = lax.broadcasted_iota(jnp.int32, sg.shape, 0)
    known = (trow < 3 * nx) & ((trow < 2 * nx) | right) & ((trow >= nx) | left)
    sg = jnp.where(known, sg, 0.0)
    WIN[:, 0:LANES] = jnp.zeros((4 * nx, LANES), f32)
    WIN[:, LANES + nz :] = jnp.zeros((4 * nx, LANES), f32)
    WIN[:, LANES : LANES + nz] = sg
    main, halo = wide(lambda i: WIN[:, pl.ds(pl.multiple_of(i * LANES, LANES), LANES)], mine)
    c2 = columns(jnp.concatenate([main, halo], 1))
    A2[me, 0] = c2[0]
    A2[me, 1] = c2[1]
    share(A2, as2, ar2)

    for i, q in enumerate((gwin, sg)):
        for c, grad in enumerate((q - ring(q, 1, 0), q - zshift(q, 1))):
            for dz in range(-2, 3):
                a = grad if dz == 0 else zshift(grad, dz)
                for r in range(nx - 2, 2 * nx + 2):
                    GSR[i, dz + 2, c, r] = a[r : r + 1]

    def apply(i, _):
        p, t = i // inner, i % inner
        at = tile(t)
        total = [[None, None], [None, None]]
        for n, (dx, dz) in enumerate(ALL):
            m = M[n, p, at, :]
            for j in range(2):
                for c in range(2):
                    a = m * GSR[j, dz + 2, c, p + nx + dx]
                    total[j][c] = a if total[j][c] is None else total[j][c] + a
        for j in range(2):
            for c in range(2):
                FD[j, c, p, at, :] = total[j][c]
        return 0

    lax.fori_loop(0, nx * inner, apply, 0)

    width = nz // cn
    slot = lax.broadcasted_iota(jnp.int32, (width, nz), 0) + cross * width
    onehot = (jnp.broadcast_to(owner[...], (width, nz)) == slot).astype(f32).astype(jnp.bfloat16)
    rest = jnp.concatenate([gwin[nx : 2 * nx], sg[nx : 2 * nx]], 0)
    ordered = jnp.zeros((2 * nx, width), f32)
    for _ in range(3):
        piece = rest.astype(jnp.bfloat16)
        rest = rest - piece.astype(f32)
        ordered = ordered + lax.dot_general(
            piece, onehot, (((1,), (1,)), ((), ())), preferred_element_type=f32
        )

    for ds in range(2, sn - 1):
        s = lax.rem(slab + ds, sn)
        shared(A1, ar1, s, ng)
    for ds in (1, -1):
        when_all([jnp.logical_not(there(ds))], lambda: shared(A1, ar1, lax.rem(slab + ds + sn, sn), ng))

    def whole(buf, a, into):
        for s in range(sn):
            for g in range(ng):
                FULL[into, s * nx : (s + 1) * nx, g * LANES : (g + 1) * LANES] = buf[s * ng + g, a]

    def below(a):
        row = lax.broadcasted_iota(jnp.int32, a.shape, 0)
        return jnp.where(row == 0, 0.0, pltpu.roll(a, 1, 0))

    for a in range(3):
        whole(A1, a, a)
    g = FULL[0]
    s1 = FULL[1] - below(FULL[1]) + FULL[2] - zshift(FULL[2], -1)
    rr = jnp.sum(g * g)
    alpha0 = rr / jnp.sum(g * s1)
    resid = g - alpha0 * s1
    fresh = jnp.sum(resid * resid)
    beta = fresh / rr
    dirn = resid + beta * g
    known_part = jnp.sum(dirn * (s1 + beta * s1))
    lastrow = lax.broadcasted_iota(jnp.int32, dirn.shape, 0) == sn * nx - 1
    ahead = jnp.where(lastrow, 0.0, ring(dirn, 1, 0))
    for c, grad in enumerate((dirn - ahead, dirn - zshift(dirn, 1))):
        for s in range(sn):
            for g in range(ng):
                GD[s * ng + g, c] = grad[s * nx : (s + 1) * nx, g * LANES : (g + 1) * LANES]

    def combine(t):
        for p in range(nx):
            for c in range(2):
                a, b = FD[0, c, p, tile(t), :], FD[1, c, p, tile(t), :]
                BASE[c, p, tile(t), :] = BASE[c, p, tile(t), :] - alpha0 * a
                FD[0, c, p, tile(t), :] = a - alpha0 * b + beta * a

    sweep(0, inner, combine)
    pg, ps = ordered[:nx], ordered[nx:]

    if ng > 1:
        shared(A2, ar2, slab, ng - 1)
    for ds in range(1, sn):
        shared(A2, ar2, lax.rem(slab + ds, sn), ng)
    total = None
    for i in range(sn * ng):
        for c in range(2):
            a = GD[i, c] * A2[i, c]
            total = a if total is None else total + a
    alpha1 = fresh / (known_part - alpha0 * jnp.sum(total))
    press[...] = alpha0 * pg + alpha1 * (pg - alpha0 * ps + beta * pg)

    def finish(t):
        for p in range(nx):
            for c in range(2):
                vel[c, p, tile(t), :] = BASE[c, p, tile(t), :] - alpha1 * FD[0, c, p, tile(t), :]

    sweep(0, inner, finish)

    for conds, make in first + walls + corners + later + forces + bulk:
        when_all(conds, lambda: make().wait_send())
    for ds in range(-2, 3):

        def left_here():
            ref = EBR.at[2 - ds, pl.ds(0, cn - 1 if ds == 0 else cn), span(ds)]
            pltpu.make_async_copy(ref, ref, bs.at[ds + 2]).wait()

        when_all([there(ds)], left_here)
    for part in range(2):
        k_moved(ks, part)
    for buf, sem in ((A1, as1), (A2, as2)):
        ref = buf.at[pl.ds(0, sn * ng - 1)]
        pltpu.make_async_copy(ref, ref, sem).wait()


def stokes(forcing, viscosity, owner, sn, cn):
    nx, ny, nz = viscosity.shape
    f32 = jnp.float32
    ng, _ = chunks(cn, nz)
    no = len(ALL)
    ye = ny + 2 * TILE
    vmem = pl.BlockSpec(memory_space=pltpu.VMEM)
    anywhere = pl.BlockSpec(memory_space=pl.ANY)
    dma = pltpu.SemaphoreType.DMA

    def buf(*shape):
        return pltpu.VMEM(shape, f32)

    return pl.pallas_call(
        functools.partial(stokes_body, sn, cn),
        out_shape=(
            pltpu.VMEM(forcing.shape, f32),
            pltpu.VMEM((nx, nz // cn), f32),
        ),
        in_specs=[anywhere, anywhere, vmem],
        out_specs=(vmem, vmem),
        scratch_shapes=[
            buf(nx + 6, ye, nz),
            buf(2, nx + 4, ye, nz),
            buf(2, nx, 4, nz),
            buf(2, 2, nx, 2, nz),
            buf(2, nx, 4, nz),
            buf(2, 2, 2, 4, nz),
            buf(2, 2, nx, 2, nz),
            buf(2, 2, 2, 1, 2, nz),
            buf(2, nx + 4, ye, nz),
            buf(nx + 4, ye, nz),
            buf(6, nx + 2, ye, nz),
            buf(no, nx, ny, nz),
            buf(2, nx + 4, ye, nz),
            buf(2, nx + 2, ye, nz),
            buf(2, nx, ny, nz),
            buf(2, 2, nx, ny, nz),
            buf(no, nx, nz),
            buf(no, 2, nx, nz),
            buf(3, 4 * nx, nz),
            buf(ng, no, nx, LANES),
            buf(cn, no, nx, LANES),
            buf(ng, 3, nx, 2 * LANES),
            buf(5, cn, 3, nx, 2 * LANES),
            buf(sn * ng, 3, nx, LANES),
            buf(sn * ng, 2, nx, LANES),
            buf(4 * nx, nz + 2 * LANES),
            buf(5, 2, 4 * nx, LANES),
            buf(no, nx, LANES),
            buf(2, 5, 2, 4 * nx, 1, nz),
            buf(3, sn * nx, nz),
            buf(sn * ng, 2, nx, LANES),
            dma((2,)),
            dma((22,)),
            dma((22,)),
            dma((5,)),
            dma((5,)),
            dma((2,)),
            dma((2,)),
            dma,
            dma((sn,)),
            dma,
            dma((sn,)),
            pltpu.SemaphoreType.REGULAR((max(1, (sn - 2).bit_length()),)),
        ],
        compiler_params=pltpu.CompilerParams(
            collective_id=0, has_side_effects=True, vmem_limit_bytes=56 * 2**20
        ),
        name="stokes",
    )(viscosity, forcing, owner)


def shards(forcing, viscosity, owner_slot):
    sn, cn = lax.axis_size("slab"), lax.axis_size("cross")
    return stokes(forcing, viscosity, owner_slot.reshape(1, -1), sn, cn)


def solution(mesh):
    in_specs = (P(None, "slab", "cross", None), P("slab", "cross", None), P())
    out_specs = (P(None, "slab", "cross", None), P("slab", "cross"))
    return jax.shard_map(shards, mesh=mesh, in_specs=in_specs, out_specs=out_specs, check_vma=False)
```

```python
import functools

import jax
import jax.numpy as jnp
from jax import lax
from jax.experimental import pallas as pl
from jax.experimental.pallas import tpu as pltpu
from jax.sharding import PartitionSpec as P

MESH = pl.DeviceIdType.MESH

DEGREE = 3
LANES = 128
TILE = 8

cheb_theta = 1.025
cheb_delta = 0.975


def cheb_weights():
    sigma = cheb_theta / cheb_delta
    solved = [1.0 / cheb_theta] + [0.0] * (DEGREE - 1)
    change = list(solved)
    rho_prev = 1.0 / sigma
    for step in range(DEGREE - 1):
        resid = [(1.0 if k == 0 else solved[k - 1]) - solved[k] for k in range(DEGREE)]
        rho = 1.0 / (2.0 * sigma - rho_prev)
        change = [rho * rho_prev * c + 2.0 * rho / cheb_delta * r for c, r in zip(change, resid)]
        solved = [s + c for s, c in zip(solved, change)]
        rho_prev = rho
    return solved


SHORT = [(dx, dz) for dx in range(-1, 2) for dz in range(-2, 3) if abs(dx) + abs(dz) <= 2]
ALL = SHORT + [(-2, 0), (2, 0)]


def chunks(cn, nz):
    n = min(cn, nz // LANES)
    return n, cn // n


def zshift(a, d):
    n = a.shape[-1]
    k = lax.broadcasted_iota(jnp.int32, a.shape, a.ndim - 1)
    keep = (k < n - d) if d > 0 else (k >= -d)
    return jnp.where(keep, pltpu.roll(a, (-d) % n, a.ndim - 1), 0.0)


def ring(a, d, axis):
    return a if d == 0 else pltpu.roll(a, (-d) % a.shape[axis], axis)


def rows(ref, lead, t, last):
    def tile(i):
        return ref[lead + (pl.ds(pl.multiple_of(i * TILE, TILE), TILE), slice(None))]

    cur = tile(t)
    row = lax.broadcasted_iota(jnp.int32, cur.shape, 0)
    up = pltpu.roll(jnp.where(row == 0, tile(jnp.minimum(t + 1, last)), cur), TILE - 1, 0)
    down = pltpu.roll(jnp.where(row == TILE - 1, tile(jnp.maximum(t - 1, 0)), cur), 1, 0)
    return cur, up, down


def stokes_body(
    sn, cn, visc, forc, owner, vel, press,
    V, F, ypk, fpk, YV, CV, YF, CF, ZF, DI, U, M, Y0, Z, BASE, FD,
    KF, CS, FRAME, KP, KR, EB, EBR, A1, A2, WIN, QS, KS, GSR, FULL, GD,
    lsem, hs, hr, bs, br, ks, kr, as1, ar1, as2, ar2, hop,
):
    slab, cross = lax.axis_index("slab"), lax.axis_index("cross")
    nx, ny, nz = visc.shape
    nt = ny // TILE + 2
    ng, per = chunks(cn, nz)
    mine = cross // per
    f32 = jnp.float32
    w0, w1, w2 = [2.0 * w for w in cheb_weights()]

    def dev(s, c):
        return {"slab": s, "cross": c}

    def there(ds):
        return (slab + ds >= 0) & (slab + ds < sn)

    def others(dc):
        return lax.rem(cross + dc, cn)

    left, right = slab > 0, slab < sn - 1
    up, down = cross > 0, cross < cn - 1
    side, wall = (left, right), (up, down)
    own = pl.ds(TILE, ny)

    load_v = pltpu.make_async_copy(visc, V.at[pl.ds(3, nx), own], lsem.at[0])
    load_f = pltpu.make_async_copy(forc, F.at[:, pl.ds(2, nx), own], lsem.at[1])
    load_v.start()
    load_f.start()
    barrier = pltpu.get_barrier_semaphore()
    for ds in (0, 1, -1):
        for dc in range(cn):
            if ds == 0 and dc == 0:
                continue
            if ds == 0:
                pl.semaphore_signal(barrier, inc=1, device_id=dev(slab, others(dc)), device_id_type=MESH)
            else:

                @pl.when(there(ds))
                def _():
                    pl.semaphore_signal(barrier, inc=1, device_id=dev(slab + ds, others(dc)), device_id_type=MESH)

    zero_v = jnp.zeros((nx + 6, TILE, nz), f32)
    V[:, 0:TILE, :] = zero_v
    V[:, TILE + ny : 2 * TILE + ny, :] = zero_v
    zero_f = jnp.zeros((2, nx + 4, TILE, nz), f32)
    F[:, :, 0:TILE, :] = zero_f
    F[:, :, TILE + ny : 2 * TILE + ny, :] = zero_f
    for s in range(2):

        @pl.when(jnp.logical_not(side[s]))
        def _():
            v0, f0 = (0, 0) if s == 0 else (nx + 3, nx + 2)
            V[v0 : v0 + 3, TILE : TILE + ny, :] = jnp.zeros((3, ny, nz), f32)
            F[:, f0 : f0 + 2, TILE : TILE + ny, :] = jnp.zeros((2, 2, ny, nz), f32)

    count = (cn - 1) + cn * (jnp.where(left, 1, 0) + jnp.where(right, 1, 0))
    pl.semaphore_wait(barrier, count)

    steps = max(0, (sn - 2).bit_length())

    def greet(k):
        for d in (-(2**k), 2**k):

            @pl.when(there(d))
            def _():
                pl.semaphore_signal(hop.at[k], inc=1, device_id=dev(slab + d, cross), device_id_type=MESH)

    def greeted(k):
        pl.semaphore_wait(hop.at[k], jnp.where(there(-(2**k)), 1, 0) + jnp.where(there(2**k), 1, 0))

    def send(src, dst, out, into, s, c):
        return pltpu.make_async_remote_copy(
            src_ref=src, dst_ref=dst, send_sem=hs.at[out], recv_sem=hr.at[into], device_id=dev(s, c),
            device_id_type=MESH,
        )

    def vx(s, k):
        src = visc.at[k if s == 0 else nx - 1 - k]
        dst = V.at[nx + 3 + k if s == 0 else 2 - k, own]
        return send(src, dst, s * 3 + k, (1 - s) * 3 + k, slab + (2 * s - 1), cross)

    def vy(w):
        return send(ypk.at[w], YV.at[1 - w], 6 + w, 7 - w, slab, cross + (2 * w - 1))

    def vc(w, s):
        src = ypk.at[w, pl.ds(0 if s == 0 else nx - 2, 2)]
        return send(src, CV.at[1 - w, 1 - s], 8 + 2 * w + s, 8 + 2 * (1 - w) + 1 - s, slab + (2 * s - 1), cross + (2 * w - 1))

    def fx(s, k):
        src = forc.at[:, k if s == 0 else nx - 1 - k]
        dst = F.at[:, nx + 2 + k if s == 0 else 1 - k, own]
        return send(src, dst, 12 + 2 * s + k, 12 + 2 * (1 - s) + k, slab + (2 * s - 1), cross)

    def fy(w):
        return send(fpk.at[w], YF.at[1 - w], 16 + w, 17 - w, slab, cross + (2 * w - 1))

    def fc(w, s):
        src = fpk.at[w, :, pl.ds(0 if s == 0 else nx - 1, 1)]
        return send(src, CF.at[1 - w, 1 - s], 18 + 2 * w + s, 18 + 2 * (1 - w) + 1 - s, slab + (2 * s - 1), cross + (2 * w - 1))

    def landed(ref, into):
        pltpu.make_async_copy(ref, ref, hr.at[into]).wait()

    def when_all(conds, run):
        cond = conds[0]
        for c in conds[1:]:
            cond = cond & c
        pl.when(cond)(run)

    first = [([side[s]], functools.partial(vx, s, 0)) for s in range(2)]
    walls = [([wall[w]], functools.partial(vy, w)) for w in range(2)]
    corners = [([wall[w], side[s]], functools.partial(vc, w, s)) for w in range(2) for s in range(2)]
    later = [([side[s]], functools.partial(vx, s, k)) for k in (1, 2) for s in range(2)]
    forces = [([wall[w]], functools.partial(fy, w)) for w in range(2)]
    forces += [([wall[w], side[s]], functools.partial(fc, w, s)) for w in range(2) for s in range(2)]
    bulk = [([side[s]], functools.partial(fx, s, k)) for k in range(2) for s in range(2)]

    def begin(sends):
        for conds, make in sends:
            when_all(conds, lambda: make().start())

    begin(first)
    load_v.wait()
    ypk[0] = V[3 : 3 + nx, TILE : TILE + 4, :]
    ypk[1] = V[3 : 3 + nx, TILE + ny - 4 : TILE + ny, :]
    begin(walls + later[:2] + corners + later[2:])
    load_f.wait()
    fpk[0] = F[:, 2 : 2 + nx, TILE : TILE + 2, :]
    fpk[1] = F[:, 2 : 2 + nx, TILE + ny - 2 : TILE + ny, :]
    begin(forces + bulk[:2])
    if steps > 0:
        greet(0)

    inner = nt - 2

    def sweep(lo, n, body, k=10):
        while n % k:
            k -= 1

        def step(i, _):
            for j in range(k):
                body(lo + i * k + j)
            return 0

        lax.fori_loop(0, n // k, step, 0)

    def tile(t):
        return pl.ds(t * TILE if isinstance(t, int) else pl.multiple_of(t * TILE, TILE), TILE)

    def inside(plane, t):
        ok = ((t > 0) | up) & ((t < nt - 1) | down)
        if plane < 0:
            ok = ok & left
        if plane >= nx:
            ok = ok & right
        return jnp.where(ok, 1.0, 0.0)

    def zsides(v):
        return v + zshift(v, 1), v + zshift(v, -1)

    def zfaces(planes, t):
        for p in planes:
            ZF[0, p + 2, tile(t), :], ZF[1, p + 2, tile(t), :] = zsides(V[p + 3, tile(t), :])

    def diagonal(planes, t):
        for p in planes:
            c, yp, ym = rows(V, (p + 3,), t, nt - 1)
            zp, zm = zsides(c) if p < -1 or p > nx else (ZF[0, p + 2, tile(t), :], ZF[1, p + 2, tile(t), :])
            diag = V[p + 4, tile(t), :] + V[p + 2, tile(t), :] + yp + ym + zp + zm + 4.0 * c
            DI[p + 2, tile(t), :] = inside(p, t) * (1.0 / jnp.maximum(diag, 1e-30))

    def near(planes, comps, t):
        for p in planes:
            at = tile(t)
            d = DI[p + 2, at, :]
            wd = w2 * d
            if 0 in comps:
                v, vyp, vym = rows(V, (p + 3,), t, nt - 1)
                _, dyp, dym = rows(DI, (p + 2,), t, nt - 1)
                U[0, p + 1, at, :] = wd * ((v + vyp) * dyp + (v + vym) * dym) + w1 * d
            if 1 in comps:
                a = wd * ((V[p + 3, at, :] + V[p + 4, at, :]) * DI[p + 3, at, :])
                U[1, p + 1, at, :] = a
                U[2, p + 1, at, :] = zshift(a, 1)
                U[5, p + 1, at, :] = zshift(a, -1)
            if 3 in comps:
                U[3, p + 1, at, :] = wd * (ZF[0, p + 2, at, :] * zshift(d, 1))
                U[4, p + 1, at, :] = wd * (ZF[1, p + 2, at, :] * zshift(d, -1))

    def coefficients(planes, t):
        for p in planes:
            at, to = tile(t), tile(t - 1)
            v, vyp, vym = rows(V, (p + 3,), t, nt - 1)
            d = DI[p + 2, at, :]
            yp, ym = d * (v + vyp), d * (v + vym)
            xp, xm = d * (v + V[p + 4, at, :]), d * (v + V[p + 2, at, :])
            zp, zm = d * ZF[0, p + 2, at, :], d * ZF[1, p + 2, at, :]

            def put(o, a):
                M[ALL.index(o), p, to, :] = a

            def along(n, plane):
                a, au, ad = rows(U, (n, plane + 1), t, nt - 1)
                return a, yp * au + ym * ad

            def at_plane(n, plane):
                return U[n, plane + 1, at, :]

            u0, y0 = along(0, p)
            u1, y1 = along(1, p)
            b1, y2 = along(1, p - 1)
            u3, y3 = along(3, p)
            u4, y4 = along(4, p)
            put((0, 0), w0 * d + y0 + xp * u1 + xm * b1 + zp * u3 + zm * u4)
            put((1, 0), y1 + xp * at_plane(0, p + 1))
            put((-1, 0), y2 + xm * at_plane(0, p - 1))
            put((0, 1), y3 + zp * zshift(u0, 1))
            put((0, -1), y4 + zm * zshift(u0, -1))
            put((1, 1), xp * at_plane(3, p + 1) + zp * at_plane(2, p))
            put((1, -1), xp * at_plane(4, p + 1) + zm * at_plane(5, p))
            put((-1, 1), xm * at_plane(3, p - 1) + zp * at_plane(2, p - 1))
            put((-1, -1), xm * at_plane(4, p - 1) + zm * at_plane(5, p - 1))
            put((0, 2), zp * zshift(u3, 1))
            put((0, -2), zm * zshift(u4, -1))

    def far(pairs, t):
        for p, d in pairs:
            at = tile(t)
            v0, v1, v2 = [V[p + 3 + d * k, at, :] for k in range(3)]
            d0, d1, d2 = [DI[p + 2 + d * k, at, :] for k in range(3)]
            M[ALL.index((2 * d, 0)), p, tile(t - 1), :] = w2 * (d0 * (v0 + v1)) * (d1 * (v1 + v2)) * d2

    prow = lax.broadcasted_iota(jnp.int32, (nx, nz), 0)
    KF[...] = jnp.zeros_like(KF)
    CS[...] = jnp.zeros_like(CS)

    def sums(p, offsets):
        for o in offsets:
            n = ALL.index(o)
            acc = None
            for t in range(inner):
                m = M[n, p, tile(t), :]
                new = (m, m * F[0, p + 2, tile(t + 1), :], m * F[1, p + 2, tile(t + 1), :])
                acc = new if acc is None else [a + b for a, b in zip(acc, new)]
            here = prow == p
            for ref, a in zip((KF.at[n], CS.at[n, 0], CS.at[n, 1]), acc):
                for shift in (4, 2, 1):
                    a = a + pltpu.roll(a, shift, 0)
                ref[...] = jnp.where(here, a[0:nx], ref[...])

    mids, ends = list(range(1, nx - 1)), [0, nx - 1]

    def plane_sums(first, stride, n):
        def step(i, _):
            sums(first + i * stride, SHORT)
            return 0

        lax.fori_loop(0, n, step, 0)

    sweep(1, inner, lambda t: zfaces(range(nx), t))
    sweep(2, inner - 2, lambda t: diagonal(mids, t))

    parts = ((0, len(SHORT)), (len(SHORT), 2))

    def give_k(part):
        first, n = parts[part]
        for g in range(ng):
            for i in range(first, first + n):
                KP[g, i] = KF[i, :, g * LANES : (g + 1) * LANES]
        for dc in range(1, cn):
            pltpu.make_async_remote_copy(
                src_ref=KP.at[others(dc) // per, pl.ds(first, n)], dst_ref=KR.at[cross, pl.ds(first, n)],
                send_sem=ks.at[part], recv_sem=kr.at[part], device_id=dev(slab, others(dc)), device_id_type=MESH,
            ).start()

    def k_moved(sem, part):
        ref = KR.at[pl.ds(0, cn - 1), pl.ds(*parts[part])]
        pltpu.make_async_copy(ref, ref, sem.at[part]).wait()

    for s in range(2):
        when_all([side[s]], lambda: landed(V.at[nx + 3 if s == 1 else 2, own], s * 3))
    for w in range(2):

        def put():
            landed(YV.at[w], 6 + w)
            r0 = 4 if w == 0 else TILE + ny
            V[3 : 3 + nx, r0 : r0 + 4, :] = YV[w]

        when_all([wall[w]], put)
    for t in (0, nt - 1):
        zfaces(range(nx), t)
    for t in (0, 1, nt - 2, nt - 1):
        diagonal(mids, t)
    sweep(1, inner, lambda t: diagonal(ends, t))
    for w in range(2):
        for s in range(2):

            def put():
                landed(CV.at[w, s], 8 + 2 * w + s)
                r0 = 4 if w == 0 else TILE + ny
                p0 = 1 if s == 0 else nx + 3
                V[p0 : p0 + 2, r0 : r0 + 4, :] = CV[w, s]

            when_all([wall[w], side[s]], put)
    for t in (0, nt - 1):
        diagonal(ends, t)
    sweep(0, nt, lambda t: (near(mids + [0], (0, 1, 3), t), near([nx - 1], (0, 3), t)))
    sweep(1, inner, lambda t: coefficients(mids, t), 4)
    plane_sums(1, 1, nx - 2)
    for s in range(2):
        when_all([side[s]], lambda: landed(V.at[nx + 4 if s == 1 else 1, own], s * 3 + 1))
    sweep(0, nt, lambda t: (zfaces([-1, nx], t), diagonal([-1, nx], t)))
    sweep(0, nt, lambda t: (near([-1], (0, 1, 3), t), near([nx - 1], (1,), t), near([nx], (0, 3), t)))
    sweep(1, inner, lambda t: coefficients(ends, t), 4)
    plane_sums(0, nx - 1, 2)
    give_k(0)
    ready = [(p, d) for p in range(nx) for d in (1, -1) if 0 <= p + d < nx]
    sweep(1, inner, lambda t: far(ready, t), 8)
    for p, d in ready:
        sums(p, [(2 * d, 0)])
    for s in range(2):
        when_all([side[s]], lambda: landed(V.at[nx + 5 if s == 1 else 0, own], s * 3 + 2))
    sweep(1, inner, lambda t: diagonal([-2, nx + 1], t))
    sweep(1, inner, lambda t: far([(0, -1), (nx - 1, 1)], t))
    sums(0, [(-2, 0)])
    sums(nx - 1, [(2, 0)])

    FRAME[...] = jnp.zeros_like(FRAME)
    for c in range(2):
        for dx in range(-2, 3):
            total = None
            for n, o in enumerate(ALL):
                if o[0] == dx:
                    a = CS[n, c]
                    a = a if o[1] == 0 else zshift(a, -o[1])
                    total = a if total is None else total + a
            FRAME[c, nx + dx : 2 * nx + dx, :] += total
    cx, cz = FRAME[0], FRAME[1]
    e = cx - pltpu.roll(cx, 1, 0) + cz - zshift(cz, -1)
    WIN[:, 0:LANES] = jnp.zeros((4 * nx, LANES), f32)
    WIN[:, LANES + nz :] = jnp.zeros((4 * nx, LANES), f32)
    WIN[:, LANES : LANES + nz] = e

    def wide(get, g):
        main, before, after = get(g + 1), get(g), get(g + 2)
        lane = lax.broadcasted_iota(jnp.int32, main.shape, 1)
        return main, jnp.where(lane < LANES // 2, after, before)

    for g in range(ng):
        main, halo = wide(lambda i: WIN[:, i * LANES : (i + 1) * LANES], g)
        for b in range(3):
            EB[g, b, :, 0:LANES] = main[b * nx : (b + 1) * nx]
            EB[g, b, :, LANES : 2 * LANES] = halo[b * nx : (b + 1) * nx]

    if steps > 0:
        greeted(0)
        if steps > 1:
            greet(1)

    def span(ds):
        return pl.ds(max(0, ds), 3 - abs(ds))

    def e_copy(ds, dc):
        return pltpu.make_async_remote_copy(
            src_ref=EB.at[others(dc) // per, span(ds)], dst_ref=EBR.at[2 - ds, cross, span(ds)],
            send_sem=bs.at[ds + 2], recv_sem=br.at[2 - ds], device_id=dev(slab + ds, others(dc)), device_id_type=MESH,
        )

    for ds in (0, 1, -1, 2, -2):

        def start():
            for dc in range(1 if ds == 0 else 0, cn):
                e_copy(ds, dc).start()

        when_all([there(ds)], start)
    give_k(1)
    for b in range(3):
        EBR[2, cross, b] = EB[mine, b]
    KR[cross] = KP[mine]

    begin(bulk[2:])

    def forced(k):
        for s in range(2):
            when_all([side[s]], lambda: landed(F.at[:, nx + 2 + k if s == 1 else 1 - k, own], 12 + 2 * s + k))

    forced(0)
    for w in range(2):

        def put():
            landed(YF.at[w], 16 + w)
            r0 = TILE - 2 if w == 0 else TILE + ny
            F[:, 2 : 2 + nx, r0 : r0 + 2, :] = YF[w]

        when_all([wall[w]], put)
        for s in range(2):

            def put():
                landed(CF.at[w, s], 18 + 2 * w + s)
                r0 = TILE - 2 if w == 0 else TILE + ny
                p0 = 1 if s == 0 else nx + 2
                F[:, p0 : p0 + 1, r0 : r0 + 2, :] = CF[w, s]

            when_all([wall[w], side[s]], put)

    def scaled(planes, t):
        for p in planes:
            d = DI[p, tile(t), :]
            for c in range(2):
                Y0[c, p, tile(t), :] = d * F[c, p, tile(t), :]

    def faces(p, t):
        at = tile(t)
        v, vyp, vym = rows(V, (p + 3,), t, nt - 1)
        d = DI[p + 2, at, :]
        return (
            d * (v + vyp), d * (v + vym), d * (v + V[p + 4, at, :]), d * (v + V[p + 2, at, :]),
            d * ZF[0, p + 2, at, :], d * ZF[1, p + 2, at, :],
        )

    def carried(field, c, p, t, face):
        yp, ym, xp, xm, zp, zm = face
        a, au, ad = rows(field, (c, p), t, nt - 1)
        near_by = yp * au + ym * ad + xp * field[c, p + 1, tile(t), :] + xm * field[c, p - 1, tile(t), :]
        return a, near_by + zp * zshift(a, 1) + zm * zshift(a, -1)

    def once(planes, t):
        for p in planes:
            face = faces(p, t)
            for c in range(2):
                a, t1 = carried(Y0, c, p + 2, t, face)
                Z[c, p + 1, tile(t), :] = w1 * a + w2 * t1

    def twice(planes, t):
        for p in planes:
            face = faces(p, t)
            for c in range(2):
                a, t2 = carried(Z, c, p + 1, t, face)
                BASE[c, p, tile(t - 1), :] = w0 * Y0[c, p + 2, tile(t), :] + t2

    sweep(0, nt, lambda t: scaled(range(1, nx + 3), t))
    sweep(0, nt, lambda t: once(range(nx), t), 1)
    sweep(1, inner, lambda t: twice(mids, t), 1)

    for ds in range(-2, 3):
        src = -ds

        def wait():
            n = cn - 1 if ds == 0 else cn
            ref = EBR.at[2 + src, pl.ds(0, n), span(ds)]
            pltpu.make_async_copy(ref, ref, br.at[2 + src]).wait()

        when_all([there(src)], wait)
    for part in range(2):
        k_moved(kr, part)
    WINB = WIN.at[:, 0 : 2 * LANES]
    WINB[3 * nx :, :] = jnp.zeros((nx, 2 * LANES), f32)
    for t in range(-1, 2):
        WINB[(t + 1) * nx : (t + 2) * nx, :] = jnp.zeros((nx, 2 * LANES), f32)

        def gather():
            for b in range(-1, 2):
                src = t - b

                def take():
                    total = EBR[2 + src, 0, b + 1]
                    for c in range(1, cn):
                        total = total + EBR[2 + src, c, b + 1]
                    WINB[(t + 1) * nx : (t + 2) * nx, :] += total

                when_all([there(src)], take)

        when_all([there(t)], gather)
    for n in range(len(ALL)):
        total = KR[0, n]
        for c in range(1, cn):
            total = total + KR[c, n]
        KS[n] = total

    def columns(q):
        for c, grad in enumerate((q - ring(q, 1, 0), q - ring(q, 1, 1))):
            for dz in range(-2, 3):
                QS[dz + 2, c] = ring(grad, dz, 1)[:, 0:LANES]
        out = []
        for c in range(2):
            total = None
            for n, (dx, dz) in enumerate(ALL):
                a = KS[n] * QS[dz + 2, c, nx + dx : 2 * nx + dx, :]
                total = a if total is None else total + a
            out.append(total)
        return out

    q = WINB[...]
    c1 = columns(q)
    me = slab * ng + mine
    A1[me, 0] = q[nx : 2 * nx, 0:LANES]
    A1[me, 1] = c1[0]
    A1[me, 2] = c1[1]
    for k in range(1, steps):
        greeted(k)
        if k + 1 < steps:
            greet(k + 1)

    def share(buf, ssem, rsem):
        order = [0, 1, sn - 1] + list(range(2, sn - 1))
        for ds in list(dict.fromkeys(d % sn for d in order)):
            for dg in range(ng):
                if ds == 0 and dg == 0:
                    continue
                to = lax.rem(mine + dg, ng) * per + lax.rem(cross, per)
                pltpu.make_async_remote_copy(
                    src_ref=buf.at[me], dst_ref=buf.at[me], send_sem=ssem, recv_sem=rsem.at[slab],
                    device_id=dev(lax.rem(slab + ds, sn), to), device_id_type=MESH,
                ).start()

    def shared(buf, rsem, s, n):
        ref = buf.at[pl.ds(0, n)]
        pltpu.make_async_copy(ref, ref, rsem.at[s]).wait()

    share(A1, as1, ar1)
    forced(1)
    sweep(0, nt, lambda t: scaled([0, nx + 3], t))
    sweep(0, nt, lambda t: once([-1, nx], t), 1)
    sweep(1, inner, lambda t: twice(ends, t), 1)

    if ng > 1:
        shared(A1, ar1, slab, ng - 1)
    for ds in (-1, 1):
        when_all([there(ds)], lambda: shared(A1, ar1, slab + ds, ng))
    FRAME[...] = jnp.zeros_like(FRAME)
    for t in range(-1, 2):

        def fill():
            for g in range(ng):
                for a in range(3):
                    FRAME[a, (t + 1) * nx : (t + 2) * nx, g * LANES : (g + 1) * LANES] = A1[(slab + t) * ng + g, a]

        when_all([there(t)], fill)
    gwin = FRAME[0]
    cx, cz = FRAME[1], FRAME[2]
    sg = cx - pltpu.roll(cx, 1, 0) + cz - zshift(cz, -1)
    trow = lax.broadcasted_iota(jnp.int32, sg.shape, 0)
    known = (trow < 3 * nx) & ((trow < 2 * nx) | right) & ((trow >= nx) | left)
    sg = jnp.where(known, sg, 0.0)
    WIN[:, 0:LANES] = jnp.zeros((4 * nx, LANES), f32)
    WIN[:, LANES + nz :] = jnp.zeros((4 * nx, LANES), f32)
    WIN[:, LANES : LANES + nz] = sg
    main, halo = wide(lambda i: WIN[:, pl.ds(pl.multiple_of(i * LANES, LANES), LANES)], mine)
    c2 = columns(jnp.concatenate([main, halo], 1))
    A2[me, 0] = c2[0]
    A2[me, 1] = c2[1]
    share(A2, as2, ar2)

    for i, q in enumerate((gwin, sg)):
        for c, grad in enumerate((q - ring(q, 1, 0), q - zshift(q, 1))):
            for dz in range(-2, 3):
                a = grad if dz == 0 else zshift(grad, dz)
                for r in range(nx - 2, 2 * nx + 2):
                    GSR[i, dz + 2, c, r] = a[r : r + 1]

    def apply(i, _):
        p, t = i // inner, i % inner
        at = tile(t)
        total = [[None, None], [None, None]]
        for n, (dx, dz) in enumerate(ALL):
            m = M[n, p, at, :]
            for j in range(2):
                for c in range(2):
                    a = m * GSR[j, dz + 2, c, p + nx + dx]
                    total[j][c] = a if total[j][c] is None else total[j][c] + a
        for j in range(2):
            for c in range(2):
                FD[j, c, p, at, :] = total[j][c]
        return 0

    lax.fori_loop(0, nx * inner, apply, 0)

    width = nz // cn
    slot = lax.broadcasted_iota(jnp.int32, (width, nz), 0) + cross * width
    onehot = (jnp.broadcast_to(owner[...], (width, nz)) == slot).astype(f32).astype(jnp.bfloat16)
    rest = jnp.concatenate([gwin[nx : 2 * nx], sg[nx : 2 * nx]], 0)
    ordered = jnp.zeros((2 * nx, width), f32)
    for _ in range(3):
        piece = rest.astype(jnp.bfloat16)
        rest = rest - piece.astype(f32)
        ordered = ordered + lax.dot_general(
            piece, onehot, (((1,), (1,)), ((), ())), preferred_element_type=f32
        )

    for ds in range(2, sn - 1):
        s = lax.rem(slab + ds, sn)
        shared(A1, ar1, s, ng)
    for ds in (1, -1):
        when_all([jnp.logical_not(there(ds))], lambda: shared(A1, ar1, lax.rem(slab + ds + sn, sn), ng))

    def whole(buf, a, into):
        for s in range(sn):
            for g in range(ng):
                FULL[into, s * nx : (s + 1) * nx, g * LANES : (g + 1) * LANES] = buf[s * ng + g, a]

    def below(a):
        row = lax.broadcasted_iota(jnp.int32, a.shape, 0)
        return jnp.where(row == 0, 0.0, pltpu.roll(a, 1, 0))

    for a in range(3):
        whole(A1, a, a)
    g = FULL[0]
    s1 = FULL[1] - below(FULL[1]) + FULL[2] - zshift(FULL[2], -1)
    rr = jnp.sum(g * g)
    alpha0 = rr / jnp.sum(g * s1)
    resid = g - alpha0 * s1
    fresh = jnp.sum(resid * resid)
    beta = fresh / rr
    dirn = resid + beta * g
    known_part = jnp.sum(dirn * (s1 + beta * s1))
    lastrow = lax.broadcasted_iota(jnp.int32, dirn.shape, 0) == sn * nx - 1
    ahead = jnp.where(lastrow, 0.0, ring(dirn, 1, 0))
    for c, grad in enumerate((dirn - ahead, dirn - zshift(dirn, 1))):
        for s in range(sn):
            for g in range(ng):
                GD[s * ng + g, c] = grad[s * nx : (s + 1) * nx, g * LANES : (g + 1) * LANES]

    def combine(t):
        for p in range(nx):
            for c in range(2):
                a, b = FD[0, c, p, tile(t), :], FD[1, c, p, tile(t), :]
                BASE[c, p, tile(t), :] = BASE[c, p, tile(t), :] - alpha0 * a
                FD[0, c, p, tile(t), :] = a - alpha0 * b + beta * a

    sweep(0, inner, combine)
    pg, ps = ordered[:nx], ordered[nx:]

    if ng > 1:
        shared(A2, ar2, slab, ng - 1)
    for ds in range(1, sn):
        shared(A2, ar2, lax.rem(slab + ds, sn), ng)
    total = None
    for i in range(sn * ng):
        for c in range(2):
            a = GD[i, c] * A2[i, c]
            total = a if total is None else total + a
    alpha1 = fresh / (known_part - alpha0 * jnp.sum(total))
    press[...] = alpha0 * pg + alpha1 * (pg - alpha0 * ps + beta * pg)

    def finish(t):
        for p in range(nx):
            for c in range(2):
                vel[c, p, tile(t), :] = BASE[c, p, tile(t), :] - alpha1 * FD[0, c, p, tile(t), :]

    sweep(0, inner, finish)

    for conds, make in first + walls + corners + later + forces + bulk:
        when_all(conds, lambda: make().wait_send())
    for ds in range(-2, 3):

        def left_here():
            ref = EBR.at[2 - ds, pl.ds(0, cn - 1 if ds == 0 else cn), span(ds)]
            pltpu.make_async_copy(ref, ref, bs.at[ds + 2]).wait()

        when_all([there(ds)], left_here)
    for part in range(2):
        k_moved(ks, part)
    for buf, sem in ((A1, as1), (A2, as2)):
        ref = buf.at[pl.ds(0, sn * ng - 1)]
        pltpu.make_async_copy(ref, ref, sem).wait()


def stokes(forcing, viscosity, owner, sn, cn):
    nx, ny, nz = viscosity.shape
    f32 = jnp.float32
    ng, _ = chunks(cn, nz)
    no = len(ALL)
    ye = ny + 2 * TILE
    vmem = pl.BlockSpec(memory_space=pltpu.VMEM)
    anywhere = pl.BlockSpec(memory_space=pl.ANY)
    dma = pltpu.SemaphoreType.DMA

    def buf(*shape):
        return pltpu.VMEM(shape, f32)

    return pl.pallas_call(
        functools.partial(stokes_body, sn, cn),
        out_shape=(
            pltpu.VMEM(forcing.shape, f32),
            pltpu.VMEM((nx, nz // cn), f32),
        ),
        in_specs=[anywhere, anywhere, vmem],
        out_specs=(vmem, vmem),
        scratch_shapes=[
            buf(nx + 6, ye, nz),
            buf(2, nx + 4, ye, nz),
            buf(2, nx, 4, nz),
            buf(2, 2, nx, 2, nz),
            buf(2, nx, 4, nz),
            buf(2, 2, 2, 4, nz),
            buf(2, 2, nx, 2, nz),
            buf(2, 2, 2, 1, 2, nz),
            buf(2, nx + 4, ye, nz),
            buf(nx + 4, ye, nz),
            buf(6, nx + 2, ye, nz),
            buf(no, nx, ny, nz),
            buf(2, nx + 4, ye, nz),
            buf(2, nx + 2, ye, nz),
            buf(2, nx, ny, nz),
            buf(2, 2, nx, ny, nz),
            buf(no, nx, nz),
            buf(no, 2, nx, nz),
            buf(3, 4 * nx, nz),
            buf(ng, no, nx, LANES),
            buf(cn, no, nx, LANES),
            buf(ng, 3, nx, 2 * LANES),
            buf(5, cn, 3, nx, 2 * LANES),
            buf(sn * ng, 3, nx, LANES),
            buf(sn * ng, 2, nx, LANES),
            buf(4 * nx, nz + 2 * LANES),
            buf(5, 2, 4 * nx, LANES),
            buf(no, nx, LANES),
            buf(2, 5, 2, 4 * nx, 1, nz),
            buf(3, sn * nx, nz),
            buf(sn * ng, 2, nx, LANES),
            dma((2,)),
            dma((22,)),
            dma((22,)),
            dma((5,)),
            dma((5,)),
            dma((2,)),
            dma((2,)),
            dma,
            dma((sn,)),
            dma,
            dma((sn,)),
            pltpu.SemaphoreType.REGULAR((max(1, (sn - 2).bit_length()),)),
        ],
        compiler_params=pltpu.CompilerParams(
            collective_id=0, has_side_effects=True, vmem_limit_bytes=56 * 2**20
        ),
        name="stokes",
    )(viscosity, forcing, owner)


def shards(forcing, viscosity, owner_slot):
    sn, cn = lax.axis_size("slab"), lax.axis_size("cross")
    return stokes(forcing, viscosity, owner_slot.reshape(1, -1), sn, cn)


def solution(mesh):
    in_specs = (P(None, "slab", "cross", None), P("slab", "cross", None), P())
    out_specs = (P(None, "slab", "cross", None), P("slab", "cross"))
    return jax.shard_map(shards, mesh=mesh, in_specs=in_specs, out_specs=out_specs, check_vma=False)
```
